256 devices in a mesh: wide: 32 (over y, x, core), narrow: 8 (over z).
Axes of the slice: x: 4, y: 4, z: 8, core: 2. Of those that a mesh axis runs over, the one named last changes fastest.
Arguments:
- thinker_rows: bfloat16 [32, 8, 3, 2, 128, 2048], P('wide', 'narrow'), may hold values from -6 to 6
- codec_ids: int32 [32, 8, 3, 2, 128], P('wide', 'narrow'), may hold values from 0 to 2047
- block_lengths: int32 [32, 8, 3, 2], P('wide', 'narrow'), may hold values from 1 to 128
- chosen_label: int32 [32, 8, 3], P('wide', 'narrow'), may hold values from 0 to 1
- ref_logratio: float32 [32, 8, 3], P('wide', 'narrow'), may hold values from -6 to 6
- pair_count: int32 [32, 8], P('wide', 'narrow'), may hold values from 1 to 3, as said below
- proj_weight: bfloat16 [2048, 1024], P('narrow'), may hold values from -0.125 to 0.125
- norm_gain: bfloat16 [1024], P('narrow'), may hold values from 0.25 to 1.75
- head_weight: bfloat16 [1024, 2048], P('narrow')
Outputs:
- loss: float32 [], replicated
- grad_head: float32 [1024, 2048], P('narrow')
- grad_gain: float32 [1024], P('narrow')
The draws below stay inside these ranges and needn't reach their ends.
Inputs may be any that keep to these rules, and one draw needn't show every extreme that they name: `pair_count`: owners are ordered with the wide index slowest; the counts sum to 512; the sum of the counts of owners below owner i lies between i * 2 and i * 2 + 1; some owner holds 3 live pairs.
All inputs are finite; a program needn't handle non-finite values.
Results may differ from the reference program's by a relative error of at most 0.017.
The reference program's roundings to bfloat16 on the way (of `projected`, `normed` and `dlogits`) count: a program that leaves them out, or rounds other values in their place, can miss the bound.
Values may be sent and summed in bfloat16 or wider, within the bound.
No kernel may reach another device: no remote copies, remote signals or barrier semaphores. Data moves between devices by JAX's collectives and lax.ppermute only.
A program may use at most 64 MiB of HBM per device.

```python
import jax
import jax.numpy as jnp
from jax import lax

TW = 2048
D = 1024
V = 2048
FRAMES = 128
H = 2
SLOTS = 3
PAIRS = 512
N_WIDE = 32
N_NARROW = 8


def draw_pair_count(key, part):
    owners = N_WIDE * N_NARROW
    first_key = jax.random.fold_in(key, 11)
    second_key = jax.random.fold_in(key, 12)
    drift = jax.random.randint(first_key, (owners + 1,), 0, H)
    marked = jax.random.randint(second_key, (), 1, owners)
    drift = drift.at[marked].set(H - 1)
    drift = drift.at[marked - 1].set(0)
    drift = drift.at[0].set(0)
    drift = drift.at[owners].set(0)
    return (H + drift[1:] - drift[:-1]).astype(jnp.int32).reshape(N_WIDE, N_NARROW)


def draw_head_weight(key, part):
    values = jax.random.normal(jax.random.fold_in(key, 21), (D, V), jnp.float32) / jnp.sqrt(jnp.float32(D))
    return values.astype(jnp.bfloat16)


def place_ends(entries, rng, smallest, largest):
    longest = entries.shape.index(max(entries.shape))
    spots = []
    for shift in (0, 1):
        where = [jax.random.randint(jax.random.fold_in(rng, axis), (), 0, length) for axis, length in enumerate(entries.shape)]
        where[longest] = (where[longest] + shift) % entries.shape[longest]
        spots.append(tuple(where))
    return entries.at[spots[0]].set(smallest).at[spots[1]].set(largest)


def shard_levels(rng, extent, pieces, least, largest):
    loudness = 1.0
    for position, blocks in pieces:
        draws = jax.random.uniform(jax.random.fold_in(jax.random.fold_in(rng, 6), position), (blocks,), jnp.float32, least / len(pieces), largest / len(pieces))
        loudness = loudness * jnp.repeat(jnp.exp(draws), extent[position] // blocks).reshape((-1,) + (1,) * (len(extent) - 1 - position))
    return loudness


def noise(rng, dims, scale, reach, shards=(), kind=jnp.bfloat16):
    drawn = scale * jax.random.normal(rng, dims, jnp.float32)
    if shards:
        drawn = drawn * shard_levels(rng, dims, shards, -0.22, 0.18)
    return jnp.clip(drawn, -reach, reach).astype(kind)


def setup_inputs(seed: int = 0) -> dict:
    key_of = jax.random.split(jax.random.key(seed), 10)
    return {
        "thinker_rows": noise(key_of[0], (N_WIDE, N_NARROW, SLOTS, 2, FRAMES, TW), 1.0, 6.0, ((0, 32), (1, 8))),
        "codec_ids": place_ends(jax.random.randint(key_of[1], (N_WIDE, N_NARROW, SLOTS, 2, FRAMES), 0, V), jax.random.fold_in(key_of[1], 1), 0, V - 1).astype(jnp.int32),
        "block_lengths": place_ends(jax.random.randint(key_of[2], (N_WIDE, N_NARROW, SLOTS, 2), 1, FRAMES + 1), jax.random.fold_in(key_of[2], 1), 1, FRAMES).astype(jnp.int32),
        "chosen_label": place_ends(jax.random.randint(key_of[3], (N_WIDE, N_NARROW, SLOTS), 0, 2), jax.random.fold_in(key_of[3], 1), 0, 1).astype(jnp.int32),
        "ref_logratio": noise(key_of[4], (N_WIDE, N_NARROW, SLOTS), 1.0, 6.0, ((0, 32), (1, 8)), jnp.float32),
        "pair_count": draw_pair_count(jax.random.fold_in(key_of[9], 71), 0),
        "proj_weight": noise(key_of[6], (TW, D), TW ** -0.5, 0.125, ((0, 8),)),
        "norm_gain": jnp.clip(1.0 + 0.15 * jax.random.normal(key_of[7], (D,), jnp.float32), 0.25, 1.75).astype(jnp.bfloat16),
        "head_weight": draw_head_weight(jax.random.fold_in(key_of[9], 71), 0),
    }


norm_eps = 1e-06
margin_scale = 2.0

def forward_terms(projected, codes, lengths, live_pairs, gain_full, head_full):
    pairs = codes.shape[0]
    frames = codes.shape[2]
    flat = projected.astype(jnp.float32)
    inverse = lax.rsqrt(lax.optimization_barrier(jnp.mean(flat * flat, axis=1, keepdims=True)) + norm_eps)
    normed = (flat * inverse * gain_full.astype(jnp.float32)).astype(jnp.bfloat16)
    logits = jnp.dot(normed, head_full, preferred_element_type=jnp.float32)
    highest = lax.optimization_barrier(jnp.max(logits, axis=1, keepdims=True))
    log_total = highest + jnp.log(lax.optimization_barrier(jnp.sum(jnp.exp(logits - highest), axis=1, keepdims=True)))
    probs = jnp.exp(logits - log_total)
    target = (lax.broadcasted_iota(jnp.int32, logits.shape, 1) == codes.reshape(-1, 1)).astype(jnp.float32)
    token_logp = lax.optimization_barrier(jnp.sum(target * logits, axis=1)) - log_total[:, 0]
    frame_index = jnp.arange(frames, dtype=jnp.int32)
    valid = ((frame_index[None, None, :] < lengths[:, :, None]) & live_pairs[:, None, None]).astype(jnp.float32)
    partial_value = lax.optimization_barrier(jnp.sum(token_logp.reshape(pairs, 2, frames) * valid, axis=2))
    return (normed, flat, inverse, probs, target, valid, partial_value)

def backward_terms(scores, lengths, labels, ratios, live_pairs, normed, flat, inverse, probs, target, valid, head_full):
    length_f = lengths.astype(jnp.float32)
    score = scores / length_f
    first = labels == 0
    chosen = jnp.where(first, score[:, 0], score[:, 1])
    rejected = jnp.where(first, score[:, 1], score[:, 0])
    margin = margin_scale * (chosen - rejected - ratios)
    live_f = live_pairs.astype(jnp.float32)
    loss_part = jnp.sum(jax.nn.softplus(-margin) * live_f)
    slope = -jax.nn.sigmoid(-margin) * live_f
    weight_first = jnp.where(first, margin_scale * slope, -margin_scale * slope)
    block_weight = jnp.stack([weight_first, -weight_first], axis=1) / length_f
    coeff = (block_weight[:, :, None] * valid).reshape(-1, 1)
    dlogits = (coeff * (target - probs)).astype(jnp.bfloat16)
    head_term = jnp.dot(normed.T, dlogits, preferred_element_type=jnp.float32)
    dnormed = jnp.dot(dlogits, head_full.T, preferred_element_type=jnp.float32)
    gain_term = lax.optimization_barrier(jnp.sum(dnormed * flat * inverse, axis=0))
    return (loss_part, head_term, gain_term)

def reference(thinker_rows, codec_ids, block_lengths, chosen_label, ref_logratio, pair_count, proj_weight, norm_gain, head_weight):
    owners = N_WIDE * N_NARROW
    counts = pair_count.reshape(owners)
    live = jnp.arange(SLOTS, dtype=jnp.int32)[None, :] < counts[:, None]

    def one_owner(carry, items):
        rows, codes, lengths, labels, ratios, live_pairs = items
        projected = jnp.dot(rows.reshape(-1, TW), proj_weight, preferred_element_type=jnp.float32).astype(jnp.bfloat16)
        normed, flat, inverse, probs, target, valid, partial_value = forward_terms(projected, codes, lengths, live_pairs, norm_gain, head_weight)
        loss_part, head_term, gain_term = backward_terms(partial_value, lengths, labels, ratios, live_pairs, normed, flat, inverse, probs, target, valid, head_weight)
        return ((carry[0] + loss_part, carry[1] + head_term, carry[2] + gain_term), None)
    start = (jnp.zeros((), jnp.float32), jnp.zeros((D, V), jnp.float32), jnp.zeros((D,), jnp.float32))
    items = (thinker_rows.reshape(owners, SLOTS, 2, FRAMES, TW), codec_ids.reshape(owners, SLOTS, 2, FRAMES), block_lengths.reshape(owners, SLOTS, 2), chosen_label.reshape(owners, SLOTS), ref_logratio.reshape(owners, SLOTS), live)
    totals, unused = lax.scan(one_owner, start, items)
    return (totals[0] / PAIRS, totals[1], totals[2])
```

```python
import jax
import jax.numpy as jnp
from jax import lax
from jax.sharding import PartitionSpec as P

norm_eps = 1e-06
margin_scale = 2.0
nx = 4
ny = 4
nz = 8


def wide_index(x, y, c):
    return ((y % ny) * nx + x % nx) * 2 + c % 2


def core_swap():
    return [(wide_index(x, y, c), wide_index(x, y, 1 - c)) for y in range(ny) for x in range(nx) for c in range(2)]


def plane_shift(step, first):
    pairs = []
    for y in range(ny):
        for x in range(nx):
            for c in range(2):
                if (c == 0) == first:
                    pairs.append((wide_index(x, y, c), wide_index(x + step, y, c)))
                else:
                    pairs.append((wide_index(x, y, c), wide_index(x, y + step, c)))
    return pairs


def ring(step):
    return [(z, (z + step) % nz) for z in range(nz)]


def z_xor(bit):
    return [(z, z ^ bit) for z in range(nz)]


def all_sum(value):
    value = value + lax.ppermute(value, "wide", core_swap())
    for bit in (1, 2, 4):
        value = value + lax.ppermute(value, "narrow", z_xor(bit))
    for first in (True, False):
        for kind in (1, 2):
            value = value + lax.ppermute(value, "wide", plane_xor(kind, first))
    return value


def plane_xor(bit, along_x):
    return [
        (wide_index(x, y, c), wide_index(x ^ bit, y, c) if along_x else wide_index(x, y ^ bit, c))
        for y in range(ny)
        for x in range(nx)
        for c in range(2)
    ]


def gather_ring(piece, z, forward):
    up, down = (nz // 2, nz // 2 - 1) if forward else (nz // 2 - 1, nz // 2)
    stack = jnp.zeros((nz,) + piece.shape, piece.dtype)
    stack = lax.dynamic_update_index_in_dim(stack, piece, z, 0)
    right = left = piece
    for step in range(1, nz // 2 + 1):
        if step <= up:
            right = lax.ppermute(right, "narrow", ring(1))
            stack = lax.dynamic_update_index_in_dim(stack, right, (z - step) % nz, 0)
        if step <= down:
            left = lax.ppermute(left, "narrow", ring(-1))
            stack = lax.dynamic_update_index_in_dim(stack, left, (z + step) % nz, 0)
    return stack


def on_device(
    thinker_rows,
    codec_ids,
    block_lengths,
    chosen_label,
    ref_logratio,
    pair_count,
    proj_weight,
    norm_gain,
    head_weight,
):
    slots = thinker_rows.shape[2]
    frames = thinker_rows.shape[4]
    tw = thinker_rows.shape[5]
    k_shard, width = proj_weight.shape
    d_shard, vocab = head_weight.shape
    half_v = vocab // 2
    half_k = k_shard // 2
    count = slots * 2 * frames
    w = lax.axis_index("wide")
    z = lax.axis_index("narrow")
    c = w % 2
    x = (w // 2) % nx
    y = w // (2 * nx)
    a = jnp.where(c == 0, x, y)
    b = jnp.where(c == 0, y, x)

    p_piece = lax.dynamic_slice(proj_weight, (c * half_k, 0), (half_k, width))
    h_piece = lax.dynamic_slice(head_weight, (0, c * half_v), (d_shard, half_v))
    p_own = gather_ring(p_piece, z, True).reshape(nz * half_k, width)
    h_own = gather_ring(h_piece, z, False).reshape(nz * d_shard, half_v)
    p_oth = lax.ppermute(p_own, "wide", core_swap())
    h_oth = lax.ppermute(h_own, "wide", core_swap())
    gain = jnp.zeros((nz, d_shard), jnp.float32)
    gain = lax.dynamic_update_index_in_dim(gain, norm_gain.astype(jnp.float32), z, 0)
    for bit in (1, 2, 4):
        gain = gain + lax.ppermute(gain, "narrow", z_xor(bit))
    gain = gain.reshape(1, width)

    rows = thinker_rows.reshape(count, nz, 2, half_k)
    rows_own = lax.dynamic_index_in_dim(rows, c, 2, keepdims=False).reshape(count, tw // 2)
    rows_oth = lax.dynamic_index_in_dim(rows, 1 - c, 2, keepdims=False).reshape(count, tw // 2)
    rows_all = jnp.concatenate([rows_own, rows_oth], axis=1)
    p_all = jnp.concatenate([p_own, p_oth], axis=0)
    projected = jnp.dot(rows_all, p_all, preferred_element_type=jnp.float32).astype(jnp.bfloat16)

    codes = codec_ids[0, 0].reshape(-1, 1)
    lengths = block_lengths[0, 0]
    labels = chosen_label[0, 0]
    ratios = ref_logratio[0, 0]
    live_pairs = jnp.arange(slots, dtype=jnp.int32) < pair_count[0, 0]

    flat = projected.astype(jnp.float32)
    inverse = lax.rsqrt(jnp.mean(flat * flat, axis=1, keepdims=True) + norm_eps)
    normed = (flat * inverse * gain).astype(jnp.bfloat16)
    normed_p = lax.ppermute(normed, "wide", core_swap())
    log_own = jnp.dot(normed, h_own, preferred_element_type=jnp.float32)
    log_oth = jnp.dot(normed, h_oth, preferred_element_type=jnp.float32)
    highest = jnp.maximum(
        jnp.max(log_own, axis=1, keepdims=True), jnp.max(log_oth, axis=1, keepdims=True)
    )
    log_total = highest + jnp.log(
        jnp.sum(jnp.exp(log_own - highest), axis=1, keepdims=True)
        + jnp.sum(jnp.exp(log_oth - highest), axis=1, keepdims=True)
    )
    columns = lax.broadcasted_iota(jnp.int32, log_own.shape, 1)
    hit_own = (columns + c * half_v == codes).astype(jnp.float32)
    hit_oth = (columns + (1 - c) * half_v == codes).astype(jnp.float32)
    token_logp = (
        jnp.sum(hit_own * log_own, axis=1) + jnp.sum(hit_oth * log_oth, axis=1) - log_total[:, 0]
    )
    frame_index = jnp.arange(frames, dtype=jnp.int32)
    valid = ((frame_index[None, None, :] < lengths[:, :, None]) & live_pairs[:, None, None]).astype(
        jnp.float32
    )
    scores = jnp.sum(token_logp.reshape(slots, 2, frames) * valid, axis=2)

    length_f = lengths.astype(jnp.float32)
    score = scores / length_f
    first = labels == 0
    chosen = jnp.where(first, score[:, 0], score[:, 1])
    rejected = jnp.where(first, score[:, 1], score[:, 0])
    margin = margin_scale * (chosen - rejected - ratios)
    live_f = live_pairs.astype(jnp.float32)
    loss_part = jnp.sum(jax.nn.softplus(-margin) * live_f)
    slope = -jax.nn.sigmoid(-margin) * live_f
    weight_first = jnp.where(first, margin_scale * slope, -margin_scale * slope)
    block_weight = jnp.stack([weight_first, -weight_first], axis=1) / length_f
    coeff = (block_weight[:, :, None] * valid).reshape(-1, 1)
    dl_oth = (coeff * (hit_oth - jnp.exp(log_oth - log_total))).astype(jnp.bfloat16)
    dl_par = lax.ppermute(dl_oth, "wide", core_swap())
    dl_own = (coeff * (hit_own - jnp.exp(log_own - log_total))).astype(jnp.bfloat16)

    normed_all = jnp.concatenate([normed, normed_p], axis=0)
    dl_all = jnp.concatenate([dl_own, dl_par], axis=0)
    part = half_v // nx

    def head_term(j):
        piece = lax.dynamic_slice(dl_all, (0, ((a + j) % nx) * part), (2 * count, part))
        return lax.dot_general(
            normed_all, piece, (((0,), (0,)), ((), ())), preferred_element_type=jnp.float32
        )

    terms = {j: head_term(j) for j in (2, 1, 3, 0)}
    total = terms[0]
    for j in (2, 1, 3):
        total = total + lax.ppermute(terms[j], "wide", plane_shift(j, True))
    lines = d_shard // ny
    total = total.reshape(nz, ny, lines, part)

    def lines_of(j):
        return lax.dynamic_index_in_dim(total, (b + j) % ny, 1, keepdims=False)

    second = lines_of(0)
    for j in (2, 1, 3):
        second = second + lax.ppermute(lines_of(j), "wide", plane_shift(j, False))
    third = jnp.sum(lax.all_to_all(second, "narrow", 0, 0, tiled=True), axis=0)

    piece = third.astype(jnp.bfloat16)
    block = jnp.zeros((ny, lines, part), jnp.bfloat16)
    for j in range(ny):
        got = piece if j == 0 else lax.ppermute(piece, "wide", plane_shift(j, False))
        block = lax.dynamic_update_index_in_dim(block, got, (b - j) % ny, 0)
    block = block.reshape(d_shard, part)
    strip = jnp.zeros((d_shard, half_v), jnp.bfloat16)
    for j in range(nx):
        got = block if j == 0 else lax.ppermute(block, "wide", plane_shift(j, True))
        strip = lax.dynamic_update_slice(strip, got, (0, ((a - j) % nx) * part))
    other = lax.ppermute(strip, "wide", core_swap())
    grad_head = jnp.concatenate(
        [jnp.where(c == 0, strip, other), jnp.where(c == 0, other, strip)], axis=1
    ).astype(jnp.float32)

    contract = (((1,), (1,)), ((), ()))
    dnormed = lax.dot_general(
        dl_own, h_own, contract, preferred_element_type=jnp.float32
    ) + lax.dot_general(dl_oth, h_oth, contract, preferred_element_type=jnp.float32)
    gain_term = jnp.sum(dnormed * flat * inverse, axis=0)
    small = jnp.concatenate(
        [gain_term.reshape(nz, d_shard), jnp.full((nz, d_shard), loss_part, jnp.float32)], axis=0
    )
    small = all_sum(small)
    grad_gain = lax.dynamic_index_in_dim(small, z, 0, keepdims=False)
    pair_total = lax.axis_size("wide") * nz * ((slots + 1) // 2)
    return (small[nz, 0] / pair_total, grad_head, grad_gain)


def solution(mesh):
    in_specs = (
        P("wide", "narrow", None, None, None, None),
        P("wide", "narrow", None, None, None),
        P("wide", "narrow", None, None),
        P("wide", "narrow", None),
        P("wide", "narrow", None),
        P("wide", "narrow"),
        P("narrow", None),
        P("narrow"),
        P("narrow", None),
    )
    out_specs = (P(), P("narrow", None), P("narrow"))
    return jax.shard_map(
        on_device, mesh=mesh, in_specs=in_specs, out_specs=out_specs, check_vma=False
    )
```

```python
import functools

import jax
import jax.numpy as jnp
from jax import lax
from jax.experimental import pallas as pl
from jax.experimental.pallas import tpu as pltpu
from jax.sharding import PartitionSpec as P

norm_eps = 1e-06
margin_scale = 2.0
nx = 4
ny = 4
nz = 8
near = (3, -3, 2, 4)
far = (-1, 1, -2, 0)
small_rows = 8


def wide_index(x, y, c):
    return ((y % ny) * nx + x % nx) * 2 + c % 2


def core_swap():
    return [
        (wide_index(x, y, c), wide_index(x, y, 1 - c))
        for y in range(ny)
        for x in range(nx)
        for c in range(2)
    ]


def plane_shift(step, first):
    pairs = []
    for y in range(ny):
        for x in range(nx):
            for c in range(2):
                if (c == 0) == first:
                    pairs.append((wide_index(x, y, c), wide_index(x + step, y, c)))
                else:
                    pairs.append((wide_index(x, y, c), wide_index(x, y + step, c)))
    return pairs


def fetch_pairs(distance):
    pairs = []
    for y in range(ny):
        for x in range(nx):
            for c in range(2):
                w = wide_index(x, y, c)
                d = distance[x if c == 0 else y]
                pairs.extend((w * nz + (z + d) % nz, w * nz + z) for z in range(nz))
    return pairs


def z_xor(bit):
    return [(z, z ^ bit) for z in range(nz)]


def fetch(piece):
    both = ("wide", "narrow")
    stack = jnp.stack(
        [lax.ppermute(piece, both, fetch_pairs(near)), lax.ppermute(piece, both, fetch_pairs(far))]
    )
    own = [stack] + [lax.ppermute(stack, "wide", plane_shift(j, True)) for j in range(1, nx)]
    other = [lax.ppermute(s, "wide", core_swap()) for s in own]
    return own + other


def load_pieces(places, stacks, targets, sems):
    copies = []
    for i, stack in enumerate(stacks):
        target = targets[i // nx]
        rows = stack.shape[1]
        for s in range(2):
            k = 2 * i + s
            at = pl.multiple_of(places[k] * rows, rows)
            copies.append(
                pltpu.make_async_copy(stack.at[s], target.at[pl.ds(at, rows), :], sems.at[k])
            )
    for copy in copies:
        copy.start()
    return copies


def project_kernel(block, places, core, rows, gain, *refs):
    stacks, (projected, normed, turned, inverse), (w_own, w_oth, sems) = (
        refs[: 2 * nx],
        refs[2 * nx : 2 * nx + 4],
        refs[2 * nx + 4 :],
    )
    copies = load_pieces(places, stacks, (w_own, w_oth), sems)
    for copy in copies:
        copy.wait()
    half = w_own.shape[1]
    width = 2 * half
    at_own = pl.multiple_of(core[0] * half, half)
    at_oth = pl.multiple_of((1 - core[0]) * half, half)
    lines = width // nz // ny

    def step(i, carry):
        at = pl.multiple_of(i * block, block)
        here = rows[pl.ds(at, block), :]
        for weight, to in ((w_own, at_own), (w_oth, at_oth)):
            projected[pl.ds(at, block), pl.ds(to, half)] = jnp.dot(
                here, weight[...], preferred_element_type=jnp.float32
            ).astype(jnp.bfloat16)
        flat = projected[pl.ds(at, block), :].astype(jnp.float32)
        inv = lax.rsqrt(jnp.mean(flat * flat, axis=1, keepdims=True) + norm_eps)
        inverse[pl.ds(at, block), :] = inv
        value = flat * inv * gain[...]
        normed[pl.ds(at, block), :] = value.astype(jnp.bfloat16)
        back = value.T.astype(jnp.bfloat16)
        for z in range(nz):
            for b in range(ny):
                turned[pl.ds((b * nz + z) * lines, lines), pl.ds(at, block)] = back[
                    (z * ny + b) * lines : (z * ny + b + 1) * lines, :
                ]
        return carry

    lax.fori_loop(0, rows.shape[0] // block, step, 0)


def logits_kernel(frames, places, core, lengths, labels, ratios, live, normed, codes, *refs):
    stacks, (dl_own, dl_oth, loss), (h_own, h_oth, e_own, e_oth, sems) = (
        refs[: 2 * nx],
        refs[2 * nx : 2 * nx + 3],
        refs[2 * nx + 3 :],
    )
    copies = load_pieces(places, stacks, (h_own, h_oth), sems)
    loss[...] = jnp.zeros_like(loss)
    for copy in copies:
        copy.wait()
    half = h_own.shape[1]
    block = 2 * frames

    def pair(p, carry):
        at = pl.multiple_of(p * block, block)
        here = normed[pl.ds(at, block), :]
        code = codes[pl.ds(at, block), :]
        l_own = jnp.dot(here, h_own[...], preferred_element_type=jnp.float32)
        l_oth = jnp.dot(here, h_oth[...], preferred_element_type=jnp.float32)
        highest = jnp.maximum(
            jnp.max(l_own, axis=1, keepdims=True), jnp.max(l_oth, axis=1, keepdims=True)
        )
        columns = lax.broadcasted_iota(jnp.int32, l_own.shape, 1)
        hit_own = columns == code - core[0] * half
        hit_oth = columns == code - (1 - core[0]) * half
        picked = jnp.sum(jnp.where(hit_own, l_own, 0.0), axis=1, keepdims=True) + jnp.sum(
            jnp.where(hit_oth, l_oth, 0.0), axis=1, keepdims=True
        )
        x_own = jnp.exp(l_own - highest)
        x_oth = jnp.exp(l_oth - highest)
        e_own[...] = x_own
        e_oth[...] = x_oth
        total = jnp.sum(x_own, axis=1, keepdims=True) + jnp.sum(x_oth, axis=1, keepdims=True)
        logp = picked - (highest + jnp.log(total))
        frame = lax.broadcasted_iota(jnp.int32, (block, 1), 0)
        second = frame >= frames
        one = (frame < lengths[2 * p]) & jnp.logical_not(second)
        two = second & (frame - frames < lengths[2 * p + 1])
        length_one = jnp.full((1, 1), lengths[2 * p], jnp.int32).astype(jnp.float32)
        length_two = jnp.full((1, 1), lengths[2 * p + 1], jnp.int32).astype(jnp.float32)
        alive = jnp.full((1, 1), (p < live[0]).astype(jnp.int32), jnp.int32).astype(jnp.float32)
        score_one = jnp.sum(jnp.where(one, logp, 0.0), axis=0, keepdims=True) / length_one
        score_two = jnp.sum(jnp.where(two, logp, 0.0), axis=0, keepdims=True) / length_two
        sign = jnp.full((1, 1), 1 - 2 * labels[p], jnp.int32).astype(jnp.float32)
        margin = margin_scale * (sign * (score_one - score_two) - ratios[p])
        turn = jnp.exp(-jnp.abs(margin))
        loss[...] += alive * (jnp.maximum(-margin, 0.0) + jnp.log1p(turn))
        slope = -alive * jnp.where(margin >= 0.0, turn, 1.0) / (1.0 + turn)
        weight_one = margin_scale * sign * slope / length_one
        weight_two = -(margin_scale * sign * slope) / length_two
        coeff = jnp.where(one, weight_one, jnp.where(two, weight_two, 0.0))
        scale = 1.0 / total
        dl_own[pl.ds(at, block), :] = (
            coeff * (hit_own.astype(jnp.float32) - e_own[...] * scale)
        ).astype(jnp.bfloat16)
        dl_oth[pl.ds(at, block), :] = (
            coeff * (hit_oth.astype(jnp.float32) - e_oth[...] * scale)
        ).astype(jnp.bfloat16)
        return carry

    lax.fori_loop(0, normed.shape[0] // block, pair, 0)


def gain_kernel(block, places, dl_own, dl_oth, projected, inverse, loss, *refs):
    stacks, (small,), (h_own, h_oth, total, sems) = (
        refs[: 2 * nx],
        refs[2 * nx : 2 * nx + 1],
        refs[2 * nx + 1 :],
    )
    copies = load_pieces(places, stacks, (h_own, h_oth), sems)
    total[...] = jnp.zeros_like(total)
    for copy in copies:
        copy.wait()
    contract = (((1,), (1,)), ((), ()))

    def step(i, carry):
        at = pl.multiple_of(i * block, block)
        dnormed = lax.dot_general(
            dl_own[pl.ds(at, block), :], h_own[...], contract, preferred_element_type=jnp.float32
        ) + lax.dot_general(
            dl_oth[pl.ds(at, block), :], h_oth[...], contract, preferred_element_type=jnp.float32
        )
        flat = projected[pl.ds(at, block), :].astype(jnp.float32)
        total[...] += jnp.sum(
            dnormed * flat * inverse[pl.ds(at, block), :], axis=0, keepdims=True
        )
        return carry

    lax.fori_loop(0, dl_own.shape[0] // block, step, 0)
    part = small.shape[1]
    count = total.shape[1] // part
    for k in range(count):
        small[pl.ds(k, 1), :] = total[:, k * part : (k + 1) * part]
    small[pl.ds(count, 1), :] = jnp.broadcast_to(loss[...], (1, part))
    small[pl.ds(count + 1, small_rows - count - 1), :] = jnp.zeros(
        (small_rows - count - 1, part), jnp.float32
    )


def head_kernel(shift, core, turned, turned_par, dl_own, dl_par, small, out):
    rows = turned.shape[0]
    part = out.shape[1]
    at = pl.multiple_of(lax.rem(core[1] + shift, nx) * part, part)
    one = dl_own[:, pl.ds(at, part)]
    two = dl_par[:, pl.ds(at, part)]
    tile = 256

    def step(i, carry):
        r = pl.multiple_of(i * tile, tile)
        out[pl.ds(r, tile), :] = jnp.dot(
            turned[pl.ds(r, tile), :], one, preferred_element_type=jnp.float32
        ) + jnp.dot(turned_par[pl.ds(r, tile), :], two, preferred_element_type=jnp.float32)
        return carry

    lax.fori_loop(0, rows // tile, step, 0)
    out[pl.ds(rows, small_rows), :] = small[...]


def sum_kernel(core, term, one, two, three, *outs):
    zs, lines, part = outs[0].shape
    lines -= small_rows
    rows = zs * lines
    small = (
        (term[pl.ds(ny * rows, small_rows), :] + two[pl.ds(ny * rows, small_rows), :])
        + (one[pl.ds(ny * rows, small_rows), :] + three[pl.ds(ny * rows, small_rows), :])
    )
    for j, out in enumerate(outs):
        start = lax.rem(core[2] + j, ny) * rows
        for z in range(zs):
            at = pl.multiple_of(start + z * lines, lines)
            here = pl.ds(at, lines)
            out[z, pl.ds(0, lines), :] = (term[here, :] + two[here, :]) + (
                one[here, :] + three[here, :]
            )
            out[z, pl.ds(lines, small_rows), :] = small


SMEM = pl.BlockSpec(memory_space=pltpu.SMEM)
VMEM = pl.BlockSpec(memory_space=pltpu.VMEM)
ANY = pl.BlockSpec(memory_space=pl.ANY)


def shape(dims, dtype):
    return jax.ShapeDtypeStruct(dims, dtype)


def cost(flops, moved):
    return pl.CostEstimate(flops=flops, bytes_accessed=moved, transcendentals=0)


def on_device(
    thinker_rows,
    codec_ids,
    block_lengths,
    chosen_label,
    ref_logratio,
    pair_count,
    proj_weight,
    norm_gain,
    head_weight,
):
    slots = thinker_rows.shape[2]
    frames = thinker_rows.shape[4]
    tw = thinker_rows.shape[5]
    k_shard, width = proj_weight.shape
    d_shard, vocab = head_weight.shape
    half_v = vocab // 2
    half_d = width // 2
    count = slots * 2 * frames
    block = 2 * frames
    part = half_v // nx
    lines = d_shard // ny
    bf16, f32 = jnp.bfloat16, jnp.float32
    w = lax.axis_index("wide")
    z = lax.axis_index("narrow")
    c = w % 2
    x = (w // 2) % nx
    y = w // (2 * nx)
    a = jnp.where(c == 0, x, y)
    b = jnp.where(c == 0, y, x)
    core = jnp.stack([c, a, b]).astype(jnp.int32)
    origin = jnp.concatenate([(a - jnp.arange(nx)) % nx, (b - jnp.arange(nx)) % nx])
    table = jnp.array([near, far], jnp.int32).T
    places = ((z + jnp.take(table, origin, axis=0)) % nz).reshape(-1).astype(jnp.int32)

    p_stacks = fetch(lax.dynamic_slice(proj_weight, (0, c * half_d), (k_shard, half_d)))
    h_stacks = fetch(lax.dynamic_slice(head_weight, (0, c * half_v), (d_shard, half_v)))
    gain = jnp.zeros((nz, d_shard), f32)
    gain = lax.dynamic_update_index_in_dim(gain, norm_gain.astype(f32), z, 0)
    for bit in (1, 2, 4):
        gain = gain + lax.ppermute(gain, "narrow", z_xor(bit))

    rows = thinker_rows.reshape(count, tw)
    projected, normed, turned, inverse = pl.pallas_call(
        functools.partial(project_kernel, block),
        out_shape=(
            shape((count, width), bf16),
            shape((count, width), bf16),
            shape((width, count), bf16),
            shape((count, 1), f32),
        ),
        in_specs=[SMEM, SMEM, VMEM, VMEM] + [ANY] * (2 * nx),
        out_specs=(VMEM, VMEM, VMEM, VMEM),
        scratch_shapes=[
            pltpu.VMEM((tw, half_d), bf16),
            pltpu.VMEM((tw, half_d), bf16),
            pltpu.SemaphoreType.DMA((4 * nx,)),
        ],
        cost_estimate=cost(2 * count * tw * width, 12 << 20),
        name="project",
    )(places, core, rows, gain.reshape(1, width), *p_stacks)
    turned_par = lax.ppermute(turned, "wide", core_swap())

    dl_own, dl_oth, loss = pl.pallas_call(
        functools.partial(logits_kernel, frames),
        out_shape=(
            shape((count, half_v), bf16),
            shape((count, half_v), bf16),
            shape((1, 1), f32),
        ),
        in_specs=[SMEM] * 6 + [VMEM, VMEM] + [ANY] * (2 * nx),
        out_specs=(VMEM, VMEM, VMEM),
        scratch_shapes=[
            pltpu.VMEM((width, half_v), bf16),
            pltpu.VMEM((width, half_v), bf16),
            pltpu.VMEM((block, half_v), f32),
            pltpu.VMEM((block, half_v), f32),
            pltpu.SemaphoreType.DMA((4 * nx,)),
        ],
        cost_estimate=cost(2 * count * width * vocab, 12 << 20),
        name="logits",
    )(
        places,
        core,
        block_lengths.reshape(-1),
        chosen_label.reshape(-1),
        ref_logratio.reshape(-1),
        pair_count.reshape(-1),
        normed,
        codec_ids.reshape(count, 1),
        *h_stacks,
    )
    dl_par = lax.ppermute(dl_oth, "wide", core_swap())

    small = pl.pallas_call(
        functools.partial(gain_kernel, block),
        out_shape=shape((small_rows, part), f32),
        in_specs=[SMEM] + [VMEM] * 5 + [ANY] * (2 * nx),
        out_specs=VMEM,
        scratch_shapes=[
            pltpu.VMEM((width, half_v), bf16),
            pltpu.VMEM((width, half_v), bf16),
            pltpu.VMEM((1, width), f32),
            pltpu.SemaphoreType.DMA((4 * nx,)),
        ],
        cost_estimate=cost(2 * count * width * vocab, 8 << 20),
        name="gain",
    )(places, dl_own, dl_oth, projected, inverse, loss, *h_stacks)

    def head_term(j):
        return pl.pallas_call(
            functools.partial(head_kernel, j),
            out_shape=shape((width + small_rows, part), f32),
            in_specs=[SMEM] + [VMEM] * 5,
            out_specs=VMEM,
            cost_estimate=cost(4 * count * width * part, 5 << 20),
            name="head",
        )(core, turned, turned_par, dl_own, dl_par, small)

    sent = {j: lax.ppermute(head_term(j), "wide", plane_shift(j, True)) for j in (2, 1, 3)}
    chunks = pl.pallas_call(
        sum_kernel,
        out_shape=tuple(shape((nz, lines + small_rows, part), f32) for j in range(ny)),
        in_specs=[SMEM] + [VMEM] * 4,
        out_specs=(VMEM,) * ny,
        cost_estimate=cost(0, 5 << 20),
        name="fold",
    )(core, head_term(0), sent[1], sent[2], sent[3])
    got = {j: lax.ppermute(chunks[j], "wide", plane_shift(j, False)) for j in (2, 1, 3)}
    second = (chunks[0] + got[2]) + (got[1] + got[3])
    third = jnp.sum(lax.all_to_all(second, "narrow", 0, 0, tiled=True), axis=0)

    piece = third[:lines].astype(bf16)
    strip_b = jnp.zeros((ny, lines, part), bf16)
    for j in range(ny):
        here = piece if j == 0 else lax.ppermute(piece, "wide", plane_shift(j, False))
        strip_b = lax.dynamic_update_index_in_dim(strip_b, here, (b - j) % ny, 0)
    strip_b = strip_b.reshape(d_shard, part)
    strip = jnp.zeros((d_shard, half_v), bf16)
    for j in range(nx):
        here = strip_b if j == 0 else lax.ppermute(strip_b, "wide", plane_shift(j, True))
        strip = lax.dynamic_update_slice(strip, here, (0, ((a - j) % nx) * part))
    other = lax.ppermute(strip, "wide", core_swap())
    grad_head = jnp.concatenate(
        [jnp.where(c == 0, strip, other), jnp.where(c == 0, other, strip)], axis=1
    ).astype(f32)

    rest = third[lines:]
    rest = rest + lax.ppermute(rest, "wide", core_swap())
    sums = rest[: width // part].reshape(nz, d_shard)
    grad_gain = lax.dynamic_index_in_dim(sums, z, 0, keepdims=False)
    pair_total = lax.axis_size("wide") * nz * ((slots + 1) // 2)
    return (rest[width // part, 0] / pair_total, grad_head, grad_gain)


def solution(mesh):
    in_specs = (
        P("wide", "narrow", None, None, None, None),
        P("wide", "narrow", None, None, None),
        P("wide", "narrow", None, None),
        P("wide", "narrow", None),
        P("wide", "narrow", None),
        P("wide", "narrow"),
        P("narrow", None),
        P("narrow"),
        P("narrow", None),
    )
    out_specs = (P(), P("narrow", None), P("narrow"))
    return jax.shard_map(
        on_device, mesh=mesh, in_specs=in_specs, out_specs=out_specs, check_vma=False
    )
```

```python
import functools

import jax
import jax.numpy as jnp
from jax import lax
from jax.experimental import pallas as pl
from jax.experimental.pallas import tpu as pltpu
from jax.sharding import PartitionSpec as P

norm_eps = 1e-06
margin_scale = 2.0
nx = 4
ny = 4
nz = 8
near = (1, 2, 3, 4)
far = (-1, -2, -3, 0)
small_rows = 8


def wide_index(x, y, c):
    return ((y % ny) * nx + x % nx) * 2 + c % 2


def core_swap():
    return [
        (wide_index(x, y, c), wide_index(x, y, 1 - c))
        for y in range(ny)
        for x in range(nx)
        for c in range(2)
    ]


def plane_shift(step, first):
    pairs = []
    for y in range(ny):
        for x in range(nx):
            for c in range(2):
                if (c == 0) == first:
                    pairs.append((wide_index(x, y, c), wide_index(x + step, y, c)))
                else:
                    pairs.append((wide_index(x, y, c), wide_index(x, y + step, c)))
    return pairs


def fetch_pairs(distance):
    pairs = []
    for y in range(ny):
        for x in range(nx):
            for c in range(2):
                w = wide_index(x, y, c)
                d = distance[(x + y + 2 * c) % nx]
                pairs.extend((w * nz + (z + d) % nz, w * nz + z) for z in range(nz))
    return pairs


def fetch(piece):
    both = ("wide", "narrow")
    return (
        lax.ppermute(piece, both, fetch_pairs(near)),
        lax.ppermute(piece, both, fetch_pairs(far)),
    )


def spread(pieces):
    stack = jnp.stack(pieces)
    return [stack] + [lax.ppermute(stack, "wide", plane_shift(j, True)) for j in range(1, nx)]


def swap_all(stacks):
    return [lax.ppermute(s, "wide", core_swap()) for s in stacks]


def load_pieces(places, stacks, targets, sems):
    copies = []
    for i, stack in enumerate(stacks):
        target = targets[i // nx]
        rows = target.shape[0] // nz
        for s in range(2):
            k = 2 * i + s
            at = pl.multiple_of(places[k] * rows, rows)
            copies.append(
                pltpu.make_async_copy(
                    stack.at[s, pl.ds(0, rows), :], target.at[pl.ds(at, rows), :], sems.at[k]
                )
            )
    for copy in copies:
        copy.start()
    return copies


def project_kernel(block, places, core, rows, *refs):
    stacks, (projected,), (r_all, w_own, w_oth, sems, r_sems) = (
        refs[: 2 * nx],
        refs[2 * nx : 2 * nx + 1],
        refs[2 * nx + 1 :],
    )
    copies = load_pieces(places, stacks, (w_own, w_oth), sems)
    steps = r_all.shape[0] // block
    reads = [
        pltpu.make_async_copy(
            rows.at[pl.ds(i * block, block), :], r_all.at[pl.ds(i * block, block), :], r_sems.at[i]
        )
        for i in range(steps)
    ]
    for read in reads:
        read.start()
    half = w_own.shape[1]
    at_own = pl.multiple_of(core[0] * half, half)
    at_oth = pl.multiple_of((1 - core[0]) * half, half)
    for copy in copies:
        copy.wait()
    for read in reads:
        read.wait()

    def step(i, carry):
        at = pl.multiple_of(i * block, block)
        here = r_all[pl.ds(at, block), :]
        for weight, to in ((w_own, at_own), (w_oth, at_oth)):
            projected[pl.ds(at, block), pl.ds(to, half)] = jnp.dot(
                here, weight[...], preferred_element_type=jnp.float32
            ).astype(jnp.bfloat16)
        return carry

    lax.fori_loop(0, steps, step, 0)


def logits_kernel(frames, places, core, lengths, labels, ratios, live, projected, codes, *refs):
    stacks, (dl_own, dl_oth, turned, loss), (h_own, h_oth, gains, e_own, e_oth, sems, g_sems) = (
        refs[: 2 * nx],
        refs[2 * nx : 2 * nx + 4],
        refs[2 * nx + 4 :],
    )
    copies = load_pieces(places, stacks, (h_own, h_oth), sems)
    shard = h_own.shape[0] // nz
    for i in range(nx):
        for s in range(2):
            k = 2 * i + s
            copies.append(
                pltpu.make_async_copy(
                    stacks[i].at[s, pl.ds(shard, small_rows), pl.ds(0, shard)],
                    gains.at[places[k]],
                    g_sems.at[k],
                )
            )
            copies[-1].start()
    loss[...] = jnp.zeros_like(loss)
    for copy in copies:
        copy.wait()
    half = h_own.shape[1]
    block = 2 * frames
    lines = shard // ny
    gain = jnp.concatenate([gains[z, 0:1, :].astype(jnp.float32) for z in range(nz)], axis=1)

    def pair(p, carry):
        at = pl.multiple_of(p * block, block)
        flat = projected[pl.ds(at, block), :].astype(jnp.float32)
        inverse = lax.rsqrt(jnp.mean(flat * flat, axis=1, keepdims=True) + norm_eps)
        value = flat * inverse * gain
        here = value.astype(jnp.bfloat16)
        code = codes[pl.ds(at, block), :]
        l_own = jnp.dot(here, h_own[...], preferred_element_type=jnp.float32)
        l_oth = jnp.dot(here, h_oth[...], preferred_element_type=jnp.float32)
        back = value.T.astype(jnp.bfloat16)
        for z in range(nz):
            for b in range(ny):
                turned[pl.ds((b * nz + z) * lines, lines), pl.ds(at, block)] = back[
                    (z * ny + b) * lines : (z * ny + b + 1) * lines, :
                ]
        highest = jnp.maximum(
            jnp.max(l_own, axis=1, keepdims=True), jnp.max(l_oth, axis=1, keepdims=True)
        )
        columns = lax.broadcasted_iota(jnp.int32, l_own.shape, 1)
        hit_own = columns == code - core[0] * half
        hit_oth = columns == code - (1 - core[0]) * half
        picked = jnp.sum(jnp.where(hit_own, l_own, 0.0), axis=1, keepdims=True) + jnp.sum(
            jnp.where(hit_oth, l_oth, 0.0), axis=1, keepdims=True
        )
        x_own = jnp.exp(l_own - highest)
        x_oth = jnp.exp(l_oth - highest)
        e_own[...] = x_own
        e_oth[...] = x_oth
        total = jnp.sum(x_own, axis=1, keepdims=True) + jnp.sum(x_oth, axis=1, keepdims=True)
        logp = picked - (highest + jnp.log(total))
        frame = lax.broadcasted_iota(jnp.int32, (block, 1), 0)
        second = frame >= frames
        one = (frame < lengths[2 * p]) & jnp.logical_not(second)
        two = second & (frame - frames < lengths[2 * p + 1])
        length_one = jnp.full((1, 1), lengths[2 * p], jnp.int32).astype(jnp.float32)
        length_two = jnp.full((1, 1), lengths[2 * p + 1], jnp.int32).astype(jnp.float32)
        alive = jnp.full((1, 1), (p < live[0]).astype(jnp.int32), jnp.int32).astype(jnp.float32)
        score_one = jnp.sum(jnp.where(one, logp, 0.0), axis=0, keepdims=True) / length_one
        score_two = jnp.sum(jnp.where(two, logp, 0.0), axis=0, keepdims=True) / length_two
        sign = jnp.full((1, 1), 1 - 2 * labels[p], jnp.int32).astype(jnp.float32)
        margin = margin_scale * (sign * (score_one - score_two) - ratios[p])
        turn = jnp.exp(-jnp.abs(margin))
        loss[...] += alive * (jnp.maximum(-margin, 0.0) + jnp.log1p(turn))
        slope = -alive * jnp.where(margin >= 0.0, turn, 1.0) / (1.0 + turn)
        weight_one = margin_scale * sign * slope / length_one
        weight_two = -(margin_scale * sign * slope) / length_two
        coeff = jnp.where(one, weight_one, jnp.where(two, weight_two, 0.0))
        scale = 1.0 / total
        dl_own[pl.ds(at, block), :] = (
            coeff * (hit_own.astype(jnp.float32) - e_own[...] * scale)
        ).astype(jnp.bfloat16)
        dl_oth[pl.ds(at, block), :] = (
            coeff * (hit_oth.astype(jnp.float32) - e_oth[...] * scale)
        ).astype(jnp.bfloat16)
        return carry

    lax.fori_loop(0, projected.shape[0] // block, pair, 0)


def gain_kernel(block, places, dl_own, dl_oth, projected, loss, *refs):
    stacks, (small,), (h_own, h_oth, total, sems) = (
        refs[: 2 * nx],
        refs[2 * nx : 2 * nx + 1],
        refs[2 * nx + 1 :],
    )
    copies = load_pieces(places, stacks, (h_own, h_oth), sems)
    total[...] = jnp.zeros_like(total)
    for copy in copies:
        copy.wait()
    contract = (((1,), (1,)), ((), ()))

    def step(i, carry):
        at = pl.multiple_of(i * block, block)
        dnormed = lax.dot_general(
            dl_own[pl.ds(at, block), :], h_own[...], contract, preferred_element_type=jnp.float32
        ) + lax.dot_general(
            dl_oth[pl.ds(at, block), :], h_oth[...], contract, preferred_element_type=jnp.float32
        )
        flat = projected[pl.ds(at, block), :].astype(jnp.float32)
        inverse = lax.rsqrt(jnp.mean(flat * flat, axis=1, keepdims=True) + norm_eps)
        total[...] += jnp.sum(dnormed * flat * inverse, axis=0, keepdims=True)
        return carry

    lax.fori_loop(0, dl_own.shape[0] // block, step, 0)
    part = small.shape[1]
    count = total.shape[1] // part
    for k in range(count):
        small[pl.ds(k, 1), :] = total[:, k * part : (k + 1) * part]
    small[pl.ds(count, 1), :] = jnp.broadcast_to(loss[...], (1, part))
    small[pl.ds(count + 1, small_rows - count - 1), :] = jnp.zeros(
        (small_rows - count - 1, part), jnp.float32
    )


def own_kernel(core, turned, dl_own, out):
    part = out.shape[1]
    at = pl.multiple_of(lax.rem(core[1] + pl.program_id(0), nx) * part, part)
    out[...] = jnp.dot(
        turned[...], dl_own[:, pl.ds(at, part)], preferred_element_type=jnp.float32
    )


def head_kernel(shift, core, term, turned, dl_par, out, piece, sem):
    part = out.shape[1]
    at = pl.multiple_of(lax.rem(core[1] + shift, nx) * part, part)
    copy = pltpu.make_async_copy(dl_par.at[:, pl.ds(at, part)], piece, sem)
    copy.start()
    copy.wait()
    out[...] = term[...] + jnp.dot(turned[...], piece[...], preferred_element_type=jnp.float32)


def sum_kernel(core, *refs):
    (term, one, two, three), (s_term, s_one, s_two, s_three), outs = refs[:4], refs[4:8], refs[8:]
    zs, lines, part = outs[0].shape
    lines -= small_rows
    rows = zs * lines
    small = (s_term[...] + s_two[...]) + (s_one[...] + s_three[...])
    for j, out in enumerate(outs):
        start = lax.rem(core[2] + j, ny) * rows
        for z in range(zs):
            here = pl.ds(pl.multiple_of(start + z * lines, lines), lines)
            out[z, pl.ds(0, lines), :] = (term[here, :] + two[here, :]) + (
                one[here, :] + three[here, :]
            )
            out[z, pl.ds(lines, small_rows), :] = small


SMEM = pl.BlockSpec(memory_space=pltpu.SMEM)
VMEM = pl.BlockSpec(memory_space=pltpu.VMEM)
ANY = pl.BlockSpec(memory_space=pl.ANY)


def shape(dims, dtype):
    return jax.ShapeDtypeStruct(dims, dtype)


def cost(flops, moved):
    return pl.CostEstimate(flops=flops, bytes_accessed=moved, transcendentals=0)


def on_device(
    thinker_rows,
    codec_ids,
    block_lengths,
    chosen_label,
    ref_logratio,
    pair_count,
    proj_weight,
    norm_gain,
    head_weight,
):
    slots = thinker_rows.shape[2]
    frames = thinker_rows.shape[4]
    tw = thinker_rows.shape[5]
    k_shard, width = proj_weight.shape
    d_shard, vocab = head_weight.shape
    half_v = vocab // 2
    half_d = width // 2
    count = slots * 2 * frames
    block = 2 * frames
    part = half_v // nx
    lines = d_shard // ny
    bf16, f32 = jnp.bfloat16, jnp.float32
    w = lax.axis_index("wide")
    z = lax.axis_index("narrow")
    c = w % 2
    x = (w // 2) % nx
    y = w // (2 * nx)
    a = jnp.where(c == 0, x, y)
    b = jnp.where(c == 0, y, x)
    core = jnp.stack([c, a, b]).astype(jnp.int32)
    back = x + y - jnp.arange(nx)
    origin = jnp.concatenate([(back + 2 * c) % nx, (back + 2 - 2 * c) % nx])
    table = jnp.array([near, far], jnp.int32).T
    places = ((z + jnp.take(table, origin, axis=0)) % nz).reshape(-1).astype(jnp.int32)

    p_two = fetch(lax.dynamic_slice(proj_weight, (0, c * half_d), (k_shard, half_d)))
    h_piece = jnp.concatenate(
        [
            lax.dynamic_slice(head_weight, (0, c * half_v), (d_shard, half_v)),
            jnp.pad(norm_gain.reshape(1, d_shard), ((0, small_rows - 1), (0, half_v - d_shard))),
        ],
        axis=0,
    )
    p_near, h_piece = lax.optimization_barrier((p_two[0], h_piece))
    p_stacks = spread((p_near, p_two[1]))
    p_stacks = p_stacks + swap_all(p_stacks)
    h_stacks = spread(fetch(h_piece))

    rows = thinker_rows.reshape(count, tw)
    projected = pl.pallas_call(
        functools.partial(project_kernel, block),
        out_shape=shape((count, width), bf16),
        in_specs=[SMEM, SMEM, ANY] + [ANY] * (2 * nx),
        out_specs=VMEM,
        scratch_shapes=[
            pltpu.VMEM((count, tw), bf16),
            pltpu.VMEM((tw, half_d), bf16),
            pltpu.VMEM((tw, half_d), bf16),
            pltpu.SemaphoreType.DMA((4 * nx,)),
            pltpu.SemaphoreType.DMA((slots,)),
        ],
        cost_estimate=cost(2 * count * tw * width, 12 << 20),
        name="project",
    )(places, core, rows, *p_stacks)
    projected, *h_late = lax.optimization_barrier((projected, *h_stacks[1:]))
    h_stacks = h_stacks[:1] + h_late
    h_stacks = h_stacks + swap_all(h_stacks)

    dl_own, dl_oth, turned, loss = pl.pallas_call(
        functools.partial(logits_kernel, frames),
        out_shape=(
            shape((count, half_v), bf16),
            shape((count, half_v), bf16),
            shape((width, count), bf16),
            shape((1, 1), f32),
        ),
        in_specs=[SMEM] * 6 + [VMEM, VMEM] + [ANY] * (2 * nx),
        out_specs=(VMEM,) * 4,
        scratch_shapes=[
            pltpu.VMEM((width, half_v), bf16),
            pltpu.VMEM((width, half_v), bf16),
            pltpu.VMEM((nz, small_rows, d_shard), bf16),
            pltpu.VMEM((block, half_v), f32),
            pltpu.VMEM((block, half_v), f32),
            pltpu.SemaphoreType.DMA((4 * nx,)),
            pltpu.SemaphoreType.DMA((2 * nx,)),
        ],
        cost_estimate=cost(2 * count * width * vocab, 12 << 20),
        name="logits",
    )(
        places,
        core,
        block_lengths.reshape(-1),
        chosen_label.reshape(-1),
        ref_logratio.reshape(-1),
        pair_count.reshape(-1),
        projected,
        codec_ids.reshape(count, 1),
        *h_stacks,
    )
    dl_par = lax.ppermute(dl_oth, "wide", core_swap())
    turned_par = lax.ppermute(turned, "wide", core_swap())
    tile = 256
    mine = pl.pallas_call(
        own_kernel,
        out_shape=shape((nx, width, part), f32),
        grid=(nx, width // tile),
        in_specs=[
            SMEM,
            pl.BlockSpec((tile, count), lambda j, i: (i, 0)),
            pl.BlockSpec((count, half_v), lambda j, i: (0, 0)),
        ],
        out_specs=pl.BlockSpec((None, tile, part), lambda j, i: (j, i, 0)),
        cost_estimate=cost(2 * count * width * half_v, 8 << 20),
        name="own",
    )(core, turned, dl_own)

    def head_term(j):
        return pl.pallas_call(
            functools.partial(head_kernel, j),
            out_shape=shape((width, part), f32),
            grid=(1,),
            in_specs=[SMEM, pl.BlockSpec((None, width, part), lambda i: (j, 0, 0)), VMEM, ANY],
            out_specs=pl.BlockSpec((width, part), lambda i: (0, 0)),
            scratch_shapes=[pltpu.VMEM((count, part), bf16), pltpu.SemaphoreType.DMA],
            cost_estimate=cost(2 * count * width * part, 4 << 20),
            name="head",
        )(core, mine, turned_par, dl_par)

    terms = {j: head_term(j) for j in (2, 1, 3, 0)}
    sent = {j: lax.ppermute(terms[j], "wide", plane_shift(j, True)) for j in (2, 1, 3)}
    small = pl.pallas_call(
        functools.partial(gain_kernel, block),
        out_shape=shape((small_rows, part), f32),
        in_specs=[SMEM] + [VMEM] * 4 + [ANY] * (2 * nx),
        out_specs=VMEM,
        scratch_shapes=[
            pltpu.VMEM((width, half_v), bf16),
            pltpu.VMEM((width, half_v), bf16),
            pltpu.VMEM((1, width), f32),
            pltpu.SemaphoreType.DMA((4 * nx,)),
        ],
        cost_estimate=cost(2 * count * width * vocab, 8 << 20),
        name="gain",
    )(places, dl_own, dl_oth, projected, loss, *h_stacks)
    s_sent = {j: lax.ppermute(small, "wide", plane_shift(j, True)) for j in (2, 1, 3)}
    chunks = pl.pallas_call(
        sum_kernel,
        out_shape=tuple(shape((nz, lines + small_rows, part), f32) for j in range(ny)),
        in_specs=[SMEM] + [VMEM] * 8,
        out_specs=(VMEM,) * ny,
        cost_estimate=cost(0, 5 << 20),
        name="fold",
    )(core, terms[0], sent[1], sent[2], sent[3], small, s_sent[1], s_sent[2], s_sent[3])
    got = {j: lax.ppermute(chunks[j], "wide", plane_shift(j, False)) for j in (2, 1, 3)}
    second = (chunks[0] + got[2]) + (got[1] + got[3])
    third = jnp.sum(lax.all_to_all(second, "narrow", 0, 0, tiled=True), axis=0)

    piece = third[:lines].astype(bf16)
    strip_b = jnp.zeros((ny, lines, part), bf16)
    for j in range(ny):
        here = piece if j == 0 else lax.ppermute(piece, "wide", plane_shift(j, False))
        strip_b = lax.dynamic_update_index_in_dim(strip_b, here, (b - j) % ny, 0)
    strip_b = strip_b.reshape(d_shard, part)
    strip = jnp.zeros((d_shard, half_v), bf16)
    for j in range(nx):
        here = strip_b if j == 0 else lax.ppermute(strip_b, "wide", plane_shift(j, True))
        strip = lax.dynamic_update_slice(strip, here, (0, ((a - j) % nx) * part))
    other = lax.ppermute(strip, "wide", core_swap())
    grad_head = jnp.concatenate(
        [jnp.where(c == 0, strip, other), jnp.where(c == 0, other, strip)], axis=1
    ).astype(f32)

    rest = third[lines:]
    rest = rest + lax.ppermute(rest, "wide", core_swap())
    sums = rest[: width // part].reshape(nz, d_shard)
    grad_gain = lax.dynamic_index_in_dim(sums, z, 0, keepdims=False)
    pair_total = lax.axis_size("wide") * nz * ((slots + 1) // 2)
    return (rest[width // part, 0] / pair_total, grad_head, grad_gain)


def solution(mesh):
    in_specs = (
        P("wide", "narrow", None, None, None, None),
        P("wide", "narrow", None, None, None),
        P("wide", "narrow", None, None),
        P("wide", "narrow", None),
        P("wide", "narrow", None),
        P("wide", "narrow"),
        P("narrow", None),
        P("narrow"),
        P("narrow", None),
    )
    out_specs = (P(), P("narrow", None), P("narrow"))
    return jax.shard_map(
        on_device, mesh=mesh, in_specs=in_specs, out_specs=out_specs, check_vma=False
    )
```

```python
import functools

import jax
import jax.numpy as jnp
from jax import lax
from jax.experimental import pallas as pl
from jax.experimental.pallas import tpu as pltpu
from jax.sharding import PartitionSpec as P


norm_eps = 1e-06
margin_scale = 2.0
nx = 4
ny = 4
nz = 8
near = (1, 2, 3, 4)
far = (-1, -2, -3, 0)
small_rows = 8


def wide_index(x, y, c):
    return ((y % ny) * nx + x % nx) * 2 + c % 2


def core_swap():
    return [
        (wide_index(x, y, c), wide_index(x, y, 1 - c))
        for y in range(ny)
        for x in range(nx)
        for c in range(2)
    ]


def plane_shift(step, first):
    pairs = []
    for y in range(ny):
        for x in range(nx):
            for c in range(2):
                if (c == 0) == first:
                    pairs.append((wide_index(x, y, c), wide_index(x + step, y, c)))
                else:
                    pairs.append((wide_index(x, y, c), wide_index(x, y + step, c)))
    return pairs


def fetch_pairs(distance):
    pairs = []
    for y in range(ny):
        for x in range(nx):
            for c in range(2):
                w = wide_index(x, y, c)
                d = distance[(x + y + 2 * c) % nx]
                pairs.extend((w * nz + (z + d) % nz, w * nz + z) for z in range(nz))
    return pairs


def fetch(piece):
    both = ("wide", "narrow")
    got = []
    for distance in (near, far):
        got.append(lax.ppermute(piece, both, fetch_pairs(distance)))
    return got


def spread(pieces):
    stack = jnp.stack(pieces)
    return [stack] + [lax.ppermute(stack, "wide", plane_shift(j, True)) for j in range(1, nx)]


def swap_all(stacks):
    return [lax.ppermute(s, "wide", core_swap()) for s in stacks]


def load_pieces(places, stacks, targets, sems):
    copies = []
    for i, stack in enumerate(stacks):
        target = targets[i // nx]
        rows = target.shape[0] // nz
        for s in range(2):
            k = 2 * i + s
            at = pl.multiple_of(places[k] * rows, rows)
            copies.append(
                pltpu.make_async_copy(
                    stack.at[s, pl.ds(0, rows), :], target.at[pl.ds(at, rows), :], sems.at[k]
                )
            )
    for copy in copies:
        copy.start()
    return copies


def project_kernel(block, places, core, rows, *refs):
    stacks, (projected,), (r_all, w_own, w_oth, sems, r_sems) = (
        refs[: 2 * nx],
        refs[2 * nx : 2 * nx + 1],
        refs[2 * nx + 1 :],
    )
    copies = load_pieces(places, stacks, (w_own, w_oth), sems)
    steps = r_all.shape[0] // block
    reads = [
        pltpu.make_async_copy(
            rows.at[pl.ds(i * block, block), :], r_all.at[pl.ds(i * block, block), :], r_sems.at[i]
        )
        for i in range(steps)
    ]
    for read in reads:
        read.start()
    half = w_own.shape[1]
    at_own = pl.multiple_of(core[0] * half, half)
    at_oth = pl.multiple_of((1 - core[0]) * half, half)
    for copy in copies:
        copy.wait()
    for read in reads:
        read.wait()

    def step(i, carry):
        at = pl.multiple_of(i * block, block)
        here = r_all[pl.ds(at, block), :]
        for weight, to in ((w_own, at_own), (w_oth, at_oth)):
            projected[pl.ds(at, block), pl.ds(to, half)] = jnp.dot(
                here, weight[...], preferred_element_type=jnp.float32
            ).astype(jnp.bfloat16)
        return carry

    lax.fori_loop(0, steps, step, 0)


def logits_kernel(frames, places, core, lengths, labels, ratios, live, projected, codes, *refs):
    stacks, (dl_own, dl_oth, turned, loss), (h_own, h_oth, gains, e_own, e_oth, sems, g_sems) = (
        refs[: 2 * nx],
        refs[2 * nx : 2 * nx + 4],
        refs[2 * nx + 4 :],
    )
    copies = load_pieces(places, stacks, (h_own, h_oth), sems)
    shard = h_own.shape[0] // nz
    for i in range(nx):
        for s in range(2):
            k = 2 * i + s
            copies.append(
                pltpu.make_async_copy(
                    stacks[i].at[s, pl.ds(shard, small_rows), pl.ds(0, shard)],
                    gains.at[places[k]],
                    g_sems.at[k],
                )
            )
            copies[-1].start()
    loss[...] = jnp.zeros_like(loss)
    for copy in copies:
        copy.wait()
    half = h_own.shape[1]
    block = 2 * frames
    lines = shard // ny
    gain = jnp.concatenate([gains[z, 0:1, :].astype(jnp.float32) for z in range(nz)], axis=1)

    def pair(p, carry):
        at = pl.multiple_of(p * block, block)
        flat = projected[pl.ds(at, block), :].astype(jnp.float32)
        inverse = lax.rsqrt(jnp.mean(flat * flat, axis=1, keepdims=True) + norm_eps)
        value = flat * inverse * gain
        here = value.astype(jnp.bfloat16)
        code = codes[pl.ds(at, block), :]
        l_own = jnp.dot(here, h_own[...], preferred_element_type=jnp.float32)
        l_oth = jnp.dot(here, h_oth[...], preferred_element_type=jnp.float32)
        back = value.T.astype(jnp.bfloat16)
        for z in range(nz):
            for b in range(ny):
                turned[pl.ds((b * nz + z) * lines, lines), pl.ds(at, block)] = back[
                    (z * ny + b) * lines : (z * ny + b + 1) * lines, :
                ]
        highest = jnp.maximum(
            jnp.max(l_own, axis=1, keepdims=True), jnp.max(l_oth, axis=1, keepdims=True)
        )
        columns = lax.broadcasted_iota(jnp.int32, l_own.shape, 1)
        hit_own = columns == code - core[0] * half
        hit_oth = columns == code - (1 - core[0]) * half
        picked = jnp.sum(jnp.where(hit_own, l_own, 0.0), axis=1, keepdims=True) + jnp.sum(
            jnp.where(hit_oth, l_oth, 0.0), axis=1, keepdims=True
        )
        x_own = jnp.exp(l_own - highest)
        x_oth = jnp.exp(l_oth - highest)
        e_own[...] = x_own
        e_oth[...] = x_oth
        total = jnp.sum(x_own, axis=1, keepdims=True) + jnp.sum(x_oth, axis=1, keepdims=True)
        logp = picked - (highest + jnp.log(total))
        frame = lax.broadcasted_iota(jnp.int32, (block, 1), 0)
        second = frame >= frames
        one = (frame < lengths[2 * p]) & jnp.logical_not(second)
        two = second & (frame - frames < lengths[2 * p + 1])
        length_one = jnp.full((1, 1), lengths[2 * p], jnp.int32).astype(jnp.float32)
        length_two = jnp.full((1, 1), lengths[2 * p + 1], jnp.int32).astype(jnp.float32)
        alive = jnp.full((1, 1), (p < live[0]).astype(jnp.int32), jnp.int32).astype(jnp.float32)
        score_one = jnp.sum(jnp.where(one, logp, 0.0), axis=0, keepdims=True) / length_one
        score_two = jnp.sum(jnp.where(two, logp, 0.0), axis=0, keepdims=True) / length_two
        sign = jnp.full((1, 1), 1 - 2 * labels[p], jnp.int32).astype(jnp.float32)
        margin = margin_scale * (sign * (score_one - score_two) - ratios[p])
        turn = jnp.exp(-jnp.abs(margin))
        loss[...] += alive * (jnp.maximum(-margin, 0.0) + jnp.log1p(turn))
        slope = -alive * jnp.where(margin >= 0.0, turn, 1.0) / (1.0 + turn)
        weight_one = margin_scale * sign * slope / length_one
        weight_two = -(margin_scale * sign * slope) / length_two
        coeff = jnp.where(one, weight_one, jnp.where(two, weight_two, 0.0))
        scale = 1.0 / total
        dl_own[pl.ds(at, block), :] = (
            coeff * (hit_own.astype(jnp.float32) - e_own[...] * scale)
        ).astype(jnp.bfloat16)
        dl_oth[pl.ds(at, block), :] = (
            coeff * (hit_oth.astype(jnp.float32) - e_oth[...] * scale)
        ).astype(jnp.bfloat16)
        return carry

    lax.fori_loop(0, projected.shape[0] // block, pair, 0)


def gain_kernel(block, places, dl_own, dl_oth, projected, loss, *refs):
    stacks, (small,), (h_own, h_oth, total, sems) = (
        refs[: 2 * nx],
        refs[2 * nx : 2 * nx + 1],
        refs[2 * nx + 1 :],
    )
    copies = load_pieces(places, stacks, (h_own, h_oth), sems)
    total[...] = jnp.zeros_like(total)
    for copy in copies:
        copy.wait()
    contract = (((1,), (1,)), ((), ()))

    def step(i, carry):
        at = pl.multiple_of(i * block, block)
        dnormed = lax.dot_general(
            dl_own[pl.ds(at, block), :], h_own[...], contract, preferred_element_type=jnp.float32
        ) + lax.dot_general(
            dl_oth[pl.ds(at, block), :], h_oth[...], contract, preferred_element_type=jnp.float32
        )
        flat = projected[pl.ds(at, block), :].astype(jnp.float32)
        inverse = lax.rsqrt(jnp.mean(flat * flat, axis=1, keepdims=True) + norm_eps)
        total[...] += jnp.sum(dnormed * flat * inverse, axis=0, keepdims=True)
        return carry

    lax.fori_loop(0, dl_own.shape[0] // block, step, 0)
    part = small.shape[1]
    count = total.shape[1] // part
    for k in range(count):
        small[pl.ds(k, 1), :] = total[:, k * part : (k + 1) * part]
    small[pl.ds(count, 1), :] = jnp.broadcast_to(loss[...], (1, part))
    small[pl.ds(count + 1, small_rows - count - 1), :] = jnp.zeros(
        (small_rows - count - 1, part), jnp.float32
    )


def own_kernel(core, turned, dl_own, out):
    part = out.shape[1]
    at = pl.multiple_of(lax.rem(core[1] + pl.program_id(0), nx) * part, part)
    out[...] = jnp.dot(
        turned[...], dl_own[:, pl.ds(at, part)], preferred_element_type=jnp.float32
    )


def head_kernel(shift, core, term, turned, dl_par, out, piece, sem):
    part = out.shape[1]
    at = pl.multiple_of(lax.rem(core[1] + shift, nx) * part, part)
    copy = pltpu.make_async_copy(dl_par.at[:, pl.ds(at, part)], piece, sem)
    copy.start()
    copy.wait()
    out[...] = term[...] + jnp.dot(turned[...], piece[...], preferred_element_type=jnp.float32)


def sum_kernel(core, *refs):
    (term, one, two, three), (s_term, s_one, s_two, s_three), outs = refs[:4], refs[4:8], refs[8:]
    zs, lines, _ = outs[0].shape
    lines -= small_rows
    rows = zs * lines
    small = (s_term[...] + s_two[...]) + (s_one[...] + s_three[...])
    for j, out in enumerate(outs):
        start = lax.rem(core[2] + j, ny) * rows
        for z in range(zs):
            here = pl.ds(pl.multiple_of(start + z * lines, lines), lines)
            out[z, pl.ds(0, lines), :] = (term[here, :] + two[here, :]) + (
                one[here, :] + three[here, :]
            )
            out[z, pl.ds(lines, small_rows), :] = small


SMEM = pl.BlockSpec(memory_space=pltpu.SMEM)
VMEM = pl.BlockSpec(memory_space=pltpu.VMEM)
ANY = pl.BlockSpec(memory_space=pl.ANY)


def shape(dims, dtype):
    return jax.ShapeDtypeStruct(dims, dtype)


def limit(mebibytes):
    return pltpu.CompilerParams(vmem_limit_bytes=mebibytes << 20)


def cost(flops, moved):
    return pl.CostEstimate(flops=flops, bytes_accessed=moved, transcendentals=0)


def on_device(
    thinker_rows,
    codec_ids,
    block_lengths,
    chosen_label,
    ref_logratio,
    pair_count,
    proj_weight,
    norm_gain,
    head_weight,
):
    slots = thinker_rows.shape[2]
    frames = thinker_rows.shape[4]
    tw = thinker_rows.shape[5]
    k_shard, width = proj_weight.shape
    d_shard, vocab = head_weight.shape
    half_v = vocab // 2
    half_d = width // 2
    count = slots * 2 * frames
    block = 2 * frames
    part = half_v // nx
    lines = d_shard // ny
    bf16, f32 = jnp.bfloat16, jnp.float32
    w = lax.axis_index("wide")
    z = lax.axis_index("narrow")
    c = w % 2
    x = (w // 2) % nx
    y = w // (2 * nx)
    a = jnp.where(c == 0, x, y)
    b = jnp.where(c == 0, y, x)
    core = jnp.stack([c, a, b]).astype(jnp.int32)
    back = x + y - jnp.arange(nx)
    origin = jnp.concatenate([(back + 2 * c) % nx, (back + 2 - 2 * c) % nx])
    table = jnp.array([near, far], jnp.int32).T
    places = ((z + jnp.take(table, origin, axis=0)) % nz).reshape(-1).astype(jnp.int32)

    p_piece = lax.dynamic_slice(proj_weight, (0, c * half_d), (k_shard, half_d))
    h_piece = jnp.concatenate(
        [
            lax.dynamic_slice(head_weight, (0, c * half_v), (d_shard, half_v)),
            jnp.pad(norm_gain.reshape(1, d_shard), ((0, small_rows - 1), (0, half_v - d_shard))),
        ],
        axis=0,
    )
    p_stacks = spread(fetch(p_piece))
    p_stacks = p_stacks + swap_all(p_stacks)
    h_stacks = spread(fetch(h_piece))

    rows = thinker_rows.reshape(count, tw)
    projected = pl.pallas_call(
        functools.partial(project_kernel, block),
        out_shape=shape((count, width), bf16),
        in_specs=[SMEM, SMEM, ANY] + [ANY] * (2 * nx),
        out_specs=VMEM,
        scratch_shapes=[
            pltpu.VMEM((count, tw), bf16),
            pltpu.VMEM((tw, half_d), bf16),
            pltpu.VMEM((tw, half_d), bf16),
            pltpu.SemaphoreType.DMA((4 * nx,)),
            pltpu.SemaphoreType.DMA((slots,)),
        ],
        cost_estimate=cost(2 * count * tw * width, 12 << 20),
        compiler_params=limit(24),
        name="project",
    )(places, core, rows, *p_stacks)
    projected, *h_late = lax.optimization_barrier((projected, *h_stacks[1:]))
    h_stacks = h_stacks[:1] + h_late
    h_stacks = h_stacks + swap_all(h_stacks)

    dl_own, dl_oth, turned, loss = pl.pallas_call(
        functools.partial(logits_kernel, frames),
        out_shape=(
            shape((count, half_v), bf16),
            shape((count, half_v), bf16),
            shape((width, count), bf16),
            shape((1, 1), f32),
        ),
        in_specs=[SMEM] * 6 + [VMEM, VMEM] + [ANY] * (2 * nx),
        out_specs=(VMEM,) * 4,
        scratch_shapes=[
            pltpu.VMEM((width, half_v), bf16),
            pltpu.VMEM((width, half_v), bf16),
            pltpu.VMEM((nz, small_rows, d_shard), bf16),
            pltpu.VMEM((block, half_v), f32),
            pltpu.VMEM((block, half_v), f32),
            pltpu.SemaphoreType.DMA((4 * nx,)),
            pltpu.SemaphoreType.DMA((2 * nx,)),
        ],
        cost_estimate=cost(2 * count * width * vocab, 12 << 20),
        compiler_params=limit(32),
        name="logits",
    )(
        places,
        core,
        block_lengths.reshape(-1),
        chosen_label.reshape(-1),
        ref_logratio.reshape(-1),
        pair_count.reshape(-1),
        projected,
        codec_ids.reshape(count, 1),
        *h_stacks,
    )
    dl_par = lax.ppermute(dl_oth, "wide", core_swap())
    turned_par = lax.ppermute(turned, "wide", core_swap())
    mine = pl.pallas_call(
        own_kernel,
        out_shape=shape((nx, width, part), f32),
        grid=(nx,),
        in_specs=[SMEM, VMEM, VMEM],
        out_specs=pl.BlockSpec((None, width, part), lambda j: (j, 0, 0)),
        compiler_params=limit(20),
        cost_estimate=cost(2 * count * width * half_v, 8 << 20),
        name="own",
    )(core, turned, dl_own)

    def head_term(j):
        return pl.pallas_call(
            functools.partial(head_kernel, j),
            out_shape=shape((width, part), f32),
            grid=(1,),
            in_specs=[SMEM, pl.BlockSpec((None, width, part), lambda i: (j, 0, 0)), VMEM, ANY],
            out_specs=pl.BlockSpec((width, part), lambda i: (0, 0)),
            scratch_shapes=[pltpu.VMEM((count, part), bf16), pltpu.SemaphoreType.DMA],
            cost_estimate=cost(2 * count * width * part, 4 << 20),
            compiler_params=limit(16),
        name="head",
        )(core, mine, turned_par, dl_par)

    terms = {j: head_term(j) for j in (2, 1, 3, 0)}
    sent = {j: lax.ppermute(terms[j], "wide", plane_shift(j, True)) for j in (2, 1, 3)}
    small = pl.pallas_call(
        functools.partial(gain_kernel, block),
        out_shape=shape((small_rows, part), f32),
        in_specs=[SMEM] + [VMEM] * 4 + [ANY] * (2 * nx),
        out_specs=VMEM,
        scratch_shapes=[
            pltpu.VMEM((width, half_v), bf16),
            pltpu.VMEM((width, half_v), bf16),
            pltpu.VMEM((1, width), f32),
            pltpu.SemaphoreType.DMA((4 * nx,)),
        ],
        cost_estimate=cost(2 * count * width * vocab, 8 << 20),
        compiler_params=limit(24),
        name="gain",
    )(places, dl_own, dl_oth, projected, loss, *h_stacks)
    s_sent = {j: lax.ppermute(small, "wide", plane_shift(j, True)) for j in (2, 1, 3)}
    chunks = pl.pallas_call(
        sum_kernel,
        out_shape=tuple(shape((nz, lines + small_rows, part), f32) for _ in range(ny)),
        in_specs=[SMEM] + [VMEM] * 8,
        out_specs=(VMEM,) * ny,
        cost_estimate=cost(0, 5 << 20),
        compiler_params=limit(24),
        name="fold",
    )(core, terms[0], sent[1], sent[2], sent[3], small, s_sent[1], s_sent[2], s_sent[3])
    got = {j: lax.ppermute(chunks[j], "wide", plane_shift(j, False)) for j in (2, 1, 3)}
    second = (chunks[0] + got[2]) + (got[1] + got[3])
    third = jnp.sum(lax.all_to_all(second, "narrow", 0, 0, tiled=True), axis=0)

    piece = third[:lines].astype(bf16)
    strip_b = jnp.zeros((ny, lines, part), bf16)
    for j in range(ny):
        here = piece if j == 0 else lax.ppermute(piece, "wide", plane_shift(j, False))
        strip_b = lax.dynamic_update_index_in_dim(strip_b, here, (b - j) % ny, 0)
    strip_b = strip_b.reshape(d_shard, part)
    strip = jnp.zeros((d_shard, half_v), bf16)
    for j in range(nx):
        here = strip_b if j == 0 else lax.ppermute(strip_b, "wide", plane_shift(j, True))
        strip = lax.dynamic_update_slice(strip, here, (0, ((a - j) % nx) * part))
    other = lax.ppermute(strip, "wide", core_swap())
    grad_head = jnp.concatenate(
        [jnp.where(c == 0, strip, other), jnp.where(c == 0, other, strip)], axis=1
    ).astype(f32)

    rest = third[lines:]
    rest = rest + lax.ppermute(rest, "wide", core_swap())
    sums = rest[: width // part].reshape(nz, d_shard)
    grad_gain = lax.dynamic_index_in_dim(sums, z, 0, keepdims=False)
    pair_total = lax.axis_size("wide") * nz * ((slots + 1) // 2)
    return (rest[width // part, 0] / pair_total, grad_head, grad_gain)


def solution(mesh):
    in_specs = (
        P("wide", "narrow", None, None, None, None),
        P("wide", "narrow", None, None, None),
        P("wide", "narrow", None, None),
        P("wide", "narrow", None),
        P("wide", "narrow", None),
        P("wide", "narrow"),
        P("narrow", None),
        P("narrow"),
        P("narrow", None),
    )
    out_specs = (P(), P("narrow", None), P("narrow"))
    return jax.shard_map(
        on_device, mesh=mesh, in_specs=in_specs, out_specs=out_specs, check_vma=False
    )
```

```python
import functools

import jax
import jax.numpy as jnp
from jax import lax
from jax.experimental import pallas as pl
from jax.experimental.pallas import tpu as pltpu
from jax.sharding import PartitionSpec as P


norm_eps = 1e-06
margin_scale = 2.0
nx = 4
ny = 4
nz = 8
near = (1, 2, 3, 4)
far = (-1, -2, -3, 0)
small_rows = 8
half_top = 16384.0


def wide_index(x, y, c):
    return ((y % ny) * nx + x % nx) * 2 + c % 2


def core_swap():
    return [
        (wide_index(x, y, c), wide_index(x, y, 1 - c))
        for y in range(ny)
        for x in range(nx)
        for c in range(2)
    ]


def plane_shift(step, first):
    pairs = []
    for y in range(ny):
        for x in range(nx):
            for c in range(2):
                if (c == 0) == first:
                    pairs.append((wide_index(x, y, c), wide_index(x + step, y, c)))
                else:
                    pairs.append((wide_index(x, y, c), wide_index(x, y + step, c)))
    return pairs


def fetch_pairs(distance):
    pairs = []
    for y in range(ny):
        for x in range(nx):
            for c in range(2):
                w = wide_index(x, y, c)
                d = distance[(x + y + 2 * c) % nx]
                pairs.extend((w * nz + (z + d) % nz, w * nz + z) for z in range(nz))
    return pairs


def fetch(piece):
    both = ("wide", "narrow")
    got = []
    for distance in (near, far):
        got.append(lax.ppermute(piece, both, fetch_pairs(distance)))
    return got


def spread(pieces):
    stack = jnp.stack(pieces)
    got = [stack]
    for j in range(1, nx):
        got.append(lax.ppermute(stack, "wide", plane_shift(j, True)))
    return got


def swap_all(stacks):
    got = []
    for stack in stacks:
        got.append(lax.ppermute(stack, "wide", core_swap()))
    return got


def load_pieces(places, stacks, targets, sems):
    copies = []
    for i, stack in enumerate(stacks):
        target = targets[i // nx]
        rows = target.shape[0] // nz
        for s in range(2):
            k = 2 * i + s
            at = pl.multiple_of(places[k] * rows, rows)
            copies.append(
                pltpu.make_async_copy(
                    stack.at[s, pl.ds(0, rows), :], target.at[pl.ds(at, rows), :], sems.at[k]
                )
            )
    for copy in copies:
        copy.start()
    return copies


def project_kernel(block, places, core, rows, *refs):
    stacks, (projected,), (w_own, w_oth, sems) = (
        refs[: 2 * nx],
        refs[2 * nx : 2 * nx + 1],
        refs[2 * nx + 1 :],
    )
    copies = load_pieces(places, stacks, (w_own, w_oth), sems)
    half = w_own.shape[1]
    at_own = pl.multiple_of(core[0] * half, half)
    at_oth = pl.multiple_of((1 - core[0]) * half, half)
    for copy in copies:
        copy.wait()

    def step(i, carry):
        at = pl.multiple_of(i * block, block)
        here = rows[pl.ds(at, block), :]
        for weight, to in ((w_own, at_own), (w_oth, at_oth)):
            projected[pl.ds(at, block), pl.ds(to, half)] = jnp.dot(
                here, weight[...], preferred_element_type=jnp.float32
            ).astype(jnp.bfloat16)
        return carry

    lax.fori_loop(0, rows.shape[0] // block, step, 0)


def logits_kernel(frames, places, core, lengths, labels, ratios, live, projected, codes, *refs):
    stacks, (dl_own, dl_oth, turned, kept, loss), (h_own, h_oth, gains, e_own, e_oth, sems, g_sems) = (
        refs[: 2 * nx],
        refs[2 * nx : 2 * nx + 5],
        refs[2 * nx + 5 :],
    )
    copies = load_pieces(places, stacks, (h_own, h_oth), sems)
    shard = h_own.shape[0] // nz
    for i in range(nx):
        for s in range(2):
            k = 2 * i + s
            copies.append(
                pltpu.make_async_copy(
                    stacks[i].at[s, pl.ds(shard, small_rows), pl.ds(0, shard)],
                    gains.at[places[k]],
                    g_sems.at[k],
                )
            )
            copies[-1].start()
    loss[...] = jnp.zeros_like(loss)
    for copy in copies:
        copy.wait()
    half = h_own.shape[1]
    block = 2 * frames
    lines = shard // ny
    gain = jnp.concatenate([gains[z, 0:1, :].astype(jnp.float32) for z in range(nz)], axis=1)

    def pair(p, carry):
        at = pl.multiple_of(p * block, block)
        kept[pl.ds(at, block), :] = projected[pl.ds(at, block), :]
        flat = projected[pl.ds(at, block), :].astype(jnp.float32)
        inverse = lax.rsqrt(jnp.mean(flat * flat, axis=1, keepdims=True) + norm_eps)
        value = flat * inverse * gain
        here = value.astype(jnp.bfloat16)
        code = codes[pl.ds(at, block), :]
        l_own = jnp.dot(here, h_own[...], preferred_element_type=jnp.float32)
        l_oth = jnp.dot(here, h_oth[...], preferred_element_type=jnp.float32)
        back = value.T.astype(jnp.bfloat16)
        for z in range(nz):
            for b in range(ny):
                turned[pl.ds((b * nz + z) * lines, lines), pl.ds(at, block)] = back[
                    (z * ny + b) * lines : (z * ny + b + 1) * lines, :
                ]
        highest = jnp.maximum(
            jnp.max(l_own, axis=1, keepdims=True), jnp.max(l_oth, axis=1, keepdims=True)
        )
        columns = lax.broadcasted_iota(jnp.int32, l_own.shape, 1)
        hit_own = columns == code - core[0] * half
        hit_oth = columns == code - (1 - core[0]) * half
        picked = jnp.sum(jnp.where(hit_own, l_own, 0.0), axis=1, keepdims=True) + jnp.sum(
            jnp.where(hit_oth, l_oth, 0.0), axis=1, keepdims=True
        )
        x_own = jnp.exp(l_own - highest)
        x_oth = jnp.exp(l_oth - highest)
        e_own[...] = x_own
        e_oth[...] = x_oth
        total = jnp.sum(x_own, axis=1, keepdims=True) + jnp.sum(x_oth, axis=1, keepdims=True)
        logp = picked - (highest + jnp.log(total))
        frame = lax.broadcasted_iota(jnp.int32, (block, 1), 0)
        second = frame >= frames
        one = (frame < lengths[2 * p]) & jnp.logical_not(second)
        two = second & (frame - frames < lengths[2 * p + 1])
        length_one = jnp.full((1, 1), lengths[2 * p], jnp.int32).astype(jnp.float32)
        length_two = jnp.full((1, 1), lengths[2 * p + 1], jnp.int32).astype(jnp.float32)
        alive = jnp.full((1, 1), (p < live[0]).astype(jnp.int32), jnp.int32).astype(jnp.float32)
        score_one = jnp.sum(jnp.where(one, logp, 0.0), axis=0, keepdims=True) / length_one
        score_two = jnp.sum(jnp.where(two, logp, 0.0), axis=0, keepdims=True) / length_two
        sign = jnp.full((1, 1), 1 - 2 * labels[p], jnp.int32).astype(jnp.float32)
        margin = margin_scale * (sign * (score_one - score_two) - ratios[p])
        turn = jnp.exp(-jnp.abs(margin))
        loss[...] += alive * (jnp.maximum(-margin, 0.0) + jnp.log1p(turn))
        slope = -alive * jnp.where(margin >= 0.0, turn, 1.0) / (1.0 + turn)
        weight_one = margin_scale * sign * slope / length_one
        weight_two = -(margin_scale * sign * slope) / length_two
        coeff = jnp.where(one, weight_one, jnp.where(two, weight_two, 0.0))
        scale = 1.0 / total
        dl_own[pl.ds(at, block), :] = (
            coeff * (hit_own.astype(jnp.float32) - e_own[...] * scale)
        ).astype(jnp.bfloat16)
        dl_oth[pl.ds(at, block), :] = (
            coeff * (hit_oth.astype(jnp.float32) - e_oth[...] * scale)
        ).astype(jnp.bfloat16)
        return carry

    lax.fori_loop(0, projected.shape[0] // block, pair, 0)


def gain_kernel(block, places, dl_own, dl_oth, projected, loss, u_one, u_two, u_three, *refs):
    stacks, (small,), (h_own, h_oth, total, sems) = (
        refs[: 2 * nx],
        refs[2 * nx : 2 * nx + 1],
        refs[2 * nx + 1 :],
    )
    copies = load_pieces(places, stacks, (h_own, h_oth), sems)
    total[...] = jnp.zeros_like(total)
    for copy in copies:
        copy.wait()
    contract = (((1,), (1,)), ((), ()))

    def step(i, carry):
        at = pl.multiple_of(i * block, block)
        dnormed = lax.dot_general(
            dl_own[pl.ds(at, block), :], h_own[...], contract, preferred_element_type=jnp.float32
        ) + lax.dot_general(
            dl_oth[pl.ds(at, block), :], h_oth[...], contract, preferred_element_type=jnp.float32
        )
        flat = projected[pl.ds(at, block), :].astype(jnp.float32)
        inverse = lax.rsqrt(jnp.mean(flat * flat, axis=1, keepdims=True) + norm_eps)
        total[...] += jnp.sum(dnormed * flat * inverse, axis=0, keepdims=True)
        return carry

    lax.fori_loop(0, dl_own.shape[0] // block, step, 0)
    part = small.shape[1]
    count = total.shape[1] // part
    for k in range(count):
        small[pl.ds(k, 1), :] = total[:, k * part : (k + 1) * part]
    small[pl.ds(count, 1), :] = jnp.broadcast_to(loss[...], (1, part))
    for j, unit in ((1, u_one), (2, u_two), (3, u_three)):
        small[pl.ds(small_rows - nx + j, 1), :] = unit[...]


def own_kernel(core, turned, dl_own, out):
    part = out.shape[1]
    at = pl.multiple_of(lax.rem(core[1] + pl.program_id(0), nx) * part, part)
    out[...] = jnp.dot(
        turned[...], dl_own[:, pl.ds(at, part)], preferred_element_type=jnp.float32
    )


def head_kernel(shift, core, term, turned, dl_par, out, *refs):
    part = out.shape[1]
    at = pl.multiple_of(lax.rem(core[1] + shift, nx) * part, part)
    value = term[...] + jnp.dot(
        turned[...], dl_par[:, pl.ds(at, part)], preferred_element_type=jnp.float32
    )
    out[...] = value
    if not refs:
        return
    largest = jnp.max(jnp.max(jnp.abs(value), axis=0, keepdims=True), axis=1, keepdims=True)
    largest = jnp.maximum(largest, 1e-30)
    refs[0][...] = jnp.broadcast_to(largest / half_top, refs[0].shape)
    out[...] = out[...] * (half_top / largest)


def sum_kernel(core, *refs):
    (term, one, two, three), (s_term, s_one, s_two, s_three), outs = refs[:4], refs[4:8], refs[8:]
    zs, lines, _ = outs[0].shape
    lines -= small_rows
    rows = zs * lines
    small = (s_term[...] + s_two[...]) + (s_one[...] + s_three[...])
    first = small_rows - nx
    u_one, u_two, u_three = (
        ref[first + j : first + j + 1, :] for j, ref in ((1, s_one), (2, s_two), (3, s_three))
    )
    for j, out in enumerate(outs):
        start = lax.rem(core[2] + j, ny) * rows
        for z in range(zs):
            here = pl.ds(pl.multiple_of(start + z * lines, lines), lines)
            out[z, pl.ds(0, lines), :] = (term[here, :] + two[here, :] * u_two) + (
                one[here, :] * u_one + three[here, :] * u_three
            )
            out[z, pl.ds(lines, small_rows), :] = small


SMEM = pl.BlockSpec(memory_space=pltpu.SMEM)
VMEM = pl.BlockSpec(memory_space=pltpu.VMEM)
ANY = pl.BlockSpec(memory_space=pl.ANY)


def shape(dims, dtype):
    return jax.ShapeDtypeStruct(dims, dtype)


def limit(mebibytes):
    return pltpu.CompilerParams(vmem_limit_bytes=mebibytes << 20)


def cost(flops, moved):
    return pl.CostEstimate(flops=flops, bytes_accessed=moved, transcendentals=0)


def on_device(
    thinker_rows,
    codec_ids,
    block_lengths,
    chosen_label,
    ref_logratio,
    pair_count,
    proj_weight,
    norm_gain,
    head_weight,
):
    slots = thinker_rows.shape[2]
    frames = thinker_rows.shape[4]
    tw = thinker_rows.shape[5]
    k_shard, width = proj_weight.shape
    d_shard, vocab = head_weight.shape
    half_v = vocab // 2
    half_d = width // 2
    count = slots * 2 * frames
    block = 2 * frames
    part = half_v // nx
    lines = d_shard // ny
    bf16, f32 = jnp.bfloat16, jnp.float32
    w = lax.axis_index("wide")
    z = lax.axis_index("narrow")
    c = w % 2
    x = (w // 2) % nx
    y = w // (2 * nx)
    a = jnp.where(c == 0, x, y)
    b = jnp.where(c == 0, y, x)
    core = jnp.stack([c, a, b]).astype(jnp.int32)
    back = x + y - jnp.arange(nx)
    origin = jnp.concatenate([(back + 2 * c) % nx, (back + 2 - 2 * c) % nx])
    table = jnp.array([near, far], jnp.int32).T
    places = ((z + jnp.take(table, origin, axis=0)) % nz).reshape(-1).astype(jnp.int32)

    p_piece = lax.dynamic_slice(proj_weight, (0, c * half_d), (k_shard, half_d))
    h_piece = jnp.concatenate(
        [
            lax.dynamic_slice(head_weight, (0, c * half_v), (d_shard, half_v)),
            jnp.pad(norm_gain.reshape(1, d_shard), ((0, small_rows - 1), (0, half_v - d_shard))),
        ],
        axis=0,
    )
    p_stacks = spread(fetch(p_piece))
    p_stacks = p_stacks + swap_all(p_stacks)
    h_stacks = spread(fetch(h_piece))

    rows = thinker_rows.reshape(count, tw)
    project = pl.pallas_call(
        functools.partial(project_kernel, block),
        out_shape=shape((count, width), bf16),
        in_specs=[SMEM, SMEM, VMEM] + [ANY] * (2 * nx),
        out_specs=VMEM,
        scratch_shapes=[
            pltpu.VMEM((tw, half_d), bf16),
            pltpu.VMEM((tw, half_d), bf16),
            pltpu.SemaphoreType.DMA((4 * nx,)),
        ],
        cost_estimate=cost(2 * count * tw * width, 12 << 20),
        compiler_params=limit(16),
        name="project",
    )
    projected = project(places, core, rows, *p_stacks)
    h_stacks = h_stacks + swap_all(h_stacks)

    dl_own, dl_oth, turned, kept, loss = pl.pallas_call(
        functools.partial(logits_kernel, frames),
        out_shape=(
            shape((count, half_v), bf16),
            shape((count, half_v), bf16),
            shape((width, count), bf16),
            shape((count, width), bf16),
            shape((1, 1), f32),
        ),
        in_specs=[SMEM] * 6 + [VMEM, VMEM] + [ANY] * (2 * nx),
        out_specs=(VMEM,) * 5,
        scratch_shapes=[
            pltpu.VMEM((width, half_v), bf16),
            pltpu.VMEM((width, half_v), bf16),
            pltpu.VMEM((nz, small_rows, d_shard), bf16),
            pltpu.VMEM((block, half_v), f32),
            pltpu.VMEM((block, half_v), f32),
            pltpu.SemaphoreType.DMA((4 * nx,)),
            pltpu.SemaphoreType.DMA((2 * nx,)),
        ],
        cost_estimate=cost(2 * count * width * vocab, 12 << 20),
        compiler_params=limit(32),
        name="logits",
    )(
        places,
        core,
        block_lengths.reshape(-1),
        chosen_label.reshape(-1),
        ref_logratio.reshape(-1),
        pair_count.reshape(-1),
        projected,
        codec_ids.reshape(count, 1),
        *h_stacks,
    )
    dl_par = lax.ppermute(dl_oth, "wide", core_swap())
    turned_par = lax.ppermute(turned, "wide", core_swap())
    mine = pl.pallas_call(
        own_kernel,
        out_shape=shape((nx, width, part), f32),
        grid=(nx,),
        in_specs=[SMEM, VMEM, VMEM],
        out_specs=pl.BlockSpec((None, width, part), lambda j: (j, 0, 0)),
        compiler_params=limit(20),
        cost_estimate=cost(2 * count * width * half_v, 8 << 20),
        name="own",
    )(core, turned, dl_own)

    def head_term(j):
        outs = ((width, part),) + ((1, part),) * (j > 0)
        return pl.pallas_call(
            functools.partial(head_kernel, j),
            out_shape=tuple(shape(dims, f32) for dims in outs),
            grid=(1,),
            in_specs=[SMEM, pl.BlockSpec((None, width, part), lambda i: (j, 0, 0)), VMEM, VMEM],
            out_specs=tuple(pl.BlockSpec(dims, lambda i: (0, 0)) for dims in outs),
            cost_estimate=cost(2 * count * width * part, 4 << 20),
            compiler_params=limit(16),
            name="head",
        )(core, mine, turned_par, dl_par)

    terms = {j: head_term(j) for j in (2, 1, 3, 0)}
    sent = {
        j: lax.ppermute(
            lax.optimization_barrier(terms[j][0].astype(jnp.float16)), "wide", plane_shift(j, True)
        ).astype(f32)
        for j in (2, 1, 3)
    }
    small = pl.pallas_call(
        functools.partial(gain_kernel, block),
        out_shape=shape((small_rows, part), f32),
        in_specs=[SMEM] + [VMEM] * 7 + [ANY] * (2 * nx),
        out_specs=VMEM,
        scratch_shapes=[
            pltpu.VMEM((width, half_v), bf16),
            pltpu.VMEM((width, half_v), bf16),
            pltpu.VMEM((1, width), f32),
            pltpu.SemaphoreType.DMA((4 * nx,)),
        ],
        cost_estimate=cost(2 * count * width * vocab, 8 << 20),
        compiler_params=limit(24),
        name="gain",
    )(places, dl_own, dl_oth, kept, loss, *(terms[j][1] for j in (1, 2, 3)), *h_stacks)
    s_sent = {j: lax.ppermute(small, "wide", plane_shift(j, True)) for j in (2, 1, 3)}
    chunks = pl.pallas_call(
        sum_kernel,
        out_shape=tuple(shape((nz, lines + small_rows, part), f32) for _ in range(ny)),
        in_specs=[SMEM] + [VMEM] * 8,
        out_specs=(VMEM,) * ny,
        cost_estimate=cost(0, 5 << 20),
        compiler_params=limit(24),
        name="fold",
    )(core, terms[0][0], sent[1], sent[2], sent[3], small, s_sent[1], s_sent[2], s_sent[3])
    got = {j: lax.ppermute(chunks[j], "wide", plane_shift(j, False)) for j in (2, 1, 3)}
    second = (chunks[0] + got[2]) + (got[1] + got[3])
    third = jnp.sum(lax.all_to_all(second, "narrow", 0, 0, tiled=True), axis=0)

    piece = third[:lines].astype(bf16)
    strip_b = jnp.zeros((ny, lines, part), bf16)
    for j in range(ny):
        here = piece if j == 0 else lax.ppermute(piece, "wide", plane_shift(j, False))
        strip_b = lax.dynamic_update_index_in_dim(strip_b, here, (b - j) % ny, 0)
    strip_b = strip_b.reshape(d_shard, part)
    strip = jnp.zeros((d_shard, half_v), bf16)
    for j in range(nx):
        here = strip_b if j == 0 else lax.ppermute(strip_b, "wide", plane_shift(j, True))
        strip = lax.dynamic_update_slice(strip, here, (0, ((a - j) % nx) * part))
    other = lax.ppermute(strip, "wide", core_swap())
    grad_head = jnp.concatenate(
        [jnp.where(c == 0, strip, other), jnp.where(c == 0, other, strip)], axis=1
    ).astype(f32)

    rest = third[lines:]
    rest = rest + lax.ppermute(rest, "wide", core_swap())
    sums = rest[: width // part].reshape(nz, d_shard)
    grad_gain = lax.dynamic_index_in_dim(sums, z, 0, keepdims=False)
    pair_total = lax.axis_size("wide") * nz * ((slots + 1) // 2)
    return (rest[width // part, 0] / pair_total, grad_head, grad_gain)


def solution(mesh):
    in_specs = (
        P("wide", "narrow", None, None, None, None),
        P("wide", "narrow", None, None, None),
        P("wide", "narrow", None, None),
        P("wide", "narrow", None),
        P("wide", "narrow", None),
        P("wide", "narrow"),
        P("narrow", None),
        P("narrow"),
        P("narrow", None),
    )
    out_specs = (P(), P("narrow", None), P("narrow"))
    return jax.shard_map(
        on_device, mesh=mesh, in_specs=in_specs, out_specs=out_specs, check_vma=False
    )
```

```python
import functools

import jax
import jax.numpy as jnp
from jax import lax
from jax.experimental import pallas as pl
from jax.experimental.pallas import tpu as pltpu
from jax.sharding import PartitionSpec as P


norm_eps = 1e-06
margin_scale = 2.0
nx = 4
ny = 4
nz = 8
near = (1, 2, 3, 4)
far = (-1, -2, -3, 0)
small_rows = 8
half_top = 16384.0
log2_e = 1.4426950408889634


def wide_index(x, y, c):
    return ((y % ny) * nx + x % nx) * 2 + c % 2


def core_swap():
    return [
        (wide_index(x, y, c), wide_index(x, y, 1 - c))
        for y in range(ny)
        for x in range(nx)
        for c in range(2)
    ]


def plane_shift(step, first):
    pairs = []
    for y in range(ny):
        for x in range(nx):
            for c in range(2):
                if (c == 0) == first:
                    pairs.append((wide_index(x, y, c), wide_index(x + step, y, c)))
                else:
                    pairs.append((wide_index(x, y, c), wide_index(x, y + step, c)))
    return pairs


def fetch_pairs(distance):
    pairs = []
    for y in range(ny):
        for x in range(nx):
            for c in range(2):
                w = wide_index(x, y, c)
                d = distance[(x + y + 2 * c) % nx]
                pairs.extend((w * nz + (z + d) % nz, w * nz + z) for z in range(nz))
    return pairs


def fetch(piece):
    both = ("wide", "narrow")
    got = []
    for distance in (near, far):
        got.append(lax.ppermute(piece, both, fetch_pairs(distance)))
    return got


def spread(pieces):
    stack = jnp.stack(pieces)
    got = [stack]
    for j in range(1, nx):
        got.append(lax.ppermute(stack, "wide", plane_shift(j, True)))
    return got


def swap_all(stacks):
    got = []
    for stack in stacks:
        got.append(lax.ppermute(stack, "wide", core_swap()))
    return got


def load_pieces(places, stacks, targets, sems):
    copies = []
    for i, stack in enumerate(stacks):
        target = targets[i // nx]
        rows = target.shape[0] // nz
        for s in range(2):
            k = 2 * i + s
            at = pl.multiple_of(places[k] * rows, rows)
            copies.append(
                pltpu.make_async_copy(
                    stack.at[s, pl.ds(0, rows), :], target.at[pl.ds(at, rows), :], sems.at[k]
                )
            )
    for copy in copies:
        copy.start()
    return copies


def project_kernel(block, places, core, rows, *refs):
    stacks, (projected,), (w_own, w_oth, sems) = (
        refs[: 2 * nx],
        refs[2 * nx : 2 * nx + 1],
        refs[2 * nx + 1 :],
    )
    copies = load_pieces(places, stacks, (w_own, w_oth), sems)
    half = w_own.shape[1]
    at_own = pl.multiple_of(core[0] * half, half)
    at_oth = pl.multiple_of((1 - core[0]) * half, half)
    for copy in copies:
        copy.wait()

    def step(i, carry):
        at = pl.multiple_of(i * block, block)
        here = rows[pl.ds(at, block), :]
        for weight, to in ((w_own, at_own), (w_oth, at_oth)):
            projected[pl.ds(at, block), pl.ds(to, half)] = jnp.dot(
                here, weight[...], preferred_element_type=jnp.float32
            ).astype(jnp.bfloat16)
        return carry

    lax.fori_loop(0, rows.shape[0] // block, step, 0)


def logits_kernel(frames, places, core, lengths, labels, ratios, live, projected, codes, *refs):
    stacks, (dl_own, dl_oth, turned, kept, loss), (h_own, h_oth, gains, e_own, e_oth, sems, g_sems) = (
        refs[: 2 * nx],
        refs[2 * nx : 2 * nx + 5],
        refs[2 * nx + 5 :],
    )
    copies = load_pieces(places, stacks, (h_own, h_oth), sems)
    shard = h_own.shape[0] // nz
    for i in range(nx):
        for s in range(2):
            k = 2 * i + s
            copies.append(
                pltpu.make_async_copy(
                    stacks[i].at[s, pl.ds(shard, small_rows), pl.ds(0, shard)],
                    gains.at[places[k]],
                    g_sems.at[k],
                )
            )
            copies[-1].start()
    loss[...] = jnp.zeros_like(loss)
    for copy in copies:
        copy.wait()
    half = h_own.shape[1]
    block = 2 * frames
    lines = shard // ny
    gain = jnp.concatenate([gains[z, 0:1, :].astype(jnp.float32) for z in range(nz)], axis=1)

    def pair(p, carry):
        at = pl.multiple_of(p * block, block)
        kept[pl.ds(at, block), :] = projected[pl.ds(at, block), :]
        flat = projected[pl.ds(at, block), :].astype(jnp.float32)
        inverse = lax.rsqrt(jnp.mean(flat * flat, axis=1, keepdims=True) + norm_eps)
        value = flat * inverse * gain
        here = value.astype(jnp.bfloat16)
        code = codes[pl.ds(at, block), :]
        l_own = jnp.dot(here, h_own[...], preferred_element_type=jnp.float32)
        l_oth = jnp.dot(here, h_oth[...], preferred_element_type=jnp.float32)
        back = value.T.astype(jnp.bfloat16)
        for z in range(nz):
            for b in range(ny):
                turned[pl.ds((b * nz + z) * lines, lines), pl.ds(at, block)] = back[
                    (z * ny + b) * lines : (z * ny + b + 1) * lines, :
                ]
        highest = jnp.maximum(
            jnp.max(l_own, axis=1, keepdims=True), jnp.max(l_oth, axis=1, keepdims=True)
        )
        columns = lax.broadcasted_iota(jnp.int32, l_own.shape, 1)
        hit_own = columns == code - core[0] * half
        hit_oth = columns == code - (1 - core[0]) * half
        picked = jnp.sum(jnp.where(hit_own, l_own, 0.0), axis=1, keepdims=True) + jnp.sum(
            jnp.where(hit_oth, l_oth, 0.0), axis=1, keepdims=True
        )
        x_own = jnp.exp(l_own - highest)
        x_oth = jnp.exp(l_oth - highest)
        e_own[...] = x_own
        e_oth[...] = x_oth
        total = jnp.sum(x_own, axis=1, keepdims=True) + jnp.sum(x_oth, axis=1, keepdims=True)
        logp = picked - (highest + jnp.log(total))
        frame = lax.broadcasted_iota(jnp.int32, (block, 1), 0)
        second = frame >= frames
        one = (frame < lengths[2 * p]) & jnp.logical_not(second)
        two = second & (frame - frames < lengths[2 * p + 1])
        length_one = jnp.full((1, 1), lengths[2 * p], jnp.int32).astype(jnp.float32)
        length_two = jnp.full((1, 1), lengths[2 * p + 1], jnp.int32).astype(jnp.float32)
        alive = jnp.full((1, 1), (p < live[0]).astype(jnp.int32), jnp.int32).astype(jnp.float32)
        score_one = jnp.sum(jnp.where(one, logp, 0.0), axis=0, keepdims=True) / length_one
        score_two = jnp.sum(jnp.where(two, logp, 0.0), axis=0, keepdims=True) / length_two
        sign = jnp.full((1, 1), 1 - 2 * labels[p], jnp.int32).astype(jnp.float32)
        margin = margin_scale * (sign * (score_one - score_two) - ratios[p])
        turn = jnp.exp(-jnp.abs(margin))
        loss[...] += alive * (jnp.maximum(-margin, 0.0) + jnp.log1p(turn))
        slope = -alive * jnp.where(margin >= 0.0, turn, 1.0) / (1.0 + turn)
        weight_one = margin_scale * sign * slope / length_one
        weight_two = -(margin_scale * sign * slope) / length_two
        coeff = jnp.where(one, weight_one, jnp.where(two, weight_two, 0.0))
        scale = 1.0 / total
        dl_own[pl.ds(at, block), :] = (
            coeff * (hit_own.astype(jnp.float32) - e_own[...] * scale)
        ).astype(jnp.bfloat16)
        dl_oth[pl.ds(at, block), :] = (
            coeff * (hit_oth.astype(jnp.float32) - e_oth[...] * scale)
        ).astype(jnp.bfloat16)
        return carry

    lax.fori_loop(0, projected.shape[0] // block, pair, 0)


def gain_kernel(block, places, dl_own, dl_oth, projected, loss, u_one, u_two, u_three, *refs):
    stacks, (small,), (h_own, h_oth, total, sems) = (
        refs[: 2 * nx],
        refs[2 * nx : 2 * nx + 1],
        refs[2 * nx + 1 :],
    )
    copies = load_pieces(places, stacks, (h_own, h_oth), sems)
    total[...] = jnp.zeros_like(total)
    for copy in copies:
        copy.wait()
    contract = (((1,), (1,)), ((), ()))

    def step(i, carry):
        at = pl.multiple_of(i * block, block)
        dnormed = lax.dot_general(
            dl_own[pl.ds(at, block), :], h_own[...], contract, preferred_element_type=jnp.float32
        ) + lax.dot_general(
            dl_oth[pl.ds(at, block), :], h_oth[...], contract, preferred_element_type=jnp.float32
        )
        flat = projected[pl.ds(at, block), :].astype(jnp.float32)
        inverse = lax.rsqrt(jnp.mean(flat * flat, axis=1, keepdims=True) + norm_eps)
        total[...] += jnp.sum(dnormed * flat * inverse, axis=0, keepdims=True)
        return carry

    lax.fori_loop(0, dl_own.shape[0] // block, step, 0)
    part = small.shape[1]
    count = total.shape[1] // part
    for k in range(count):
        small[pl.ds(k, 1), :] = total[:, k * part : (k + 1) * part]
    small[pl.ds(count, 1), :] = jnp.broadcast_to(loss[...], (1, part))
    for j, unit in ((1, u_one), (2, u_two), (3, u_three)):
        small[pl.ds(small_rows - nx + j, 1), :] = unit[...]


def own_kernel(core, turned, dl_own, out):
    part = out.shape[1]
    at = pl.multiple_of(lax.rem(core[1] + pl.program_id(0), nx) * part, part)
    out[...] = jnp.dot(
        turned[...], dl_own[:, pl.ds(at, part)], preferred_element_type=jnp.float32
    )


def head_kernel(shift, core, term, turned, dl_par, out, *refs):
    part = out.shape[1]
    at = pl.multiple_of(lax.rem(core[1] + shift, nx) * part, part)
    value = term[...] + jnp.dot(
        turned[...], dl_par[:, pl.ds(at, part)], preferred_element_type=jnp.float32
    )
    out[...] = value
    if not refs:
        return
    largest = jnp.max(jnp.max(jnp.abs(value), axis=0, keepdims=True), axis=1, keepdims=True)
    largest = jnp.maximum(largest, 1e-30)
    refs[0][...] = jnp.broadcast_to(largest / half_top, refs[0].shape)
    out[...] = out[...] * (half_top / largest)


def exponent(largest):
    return jnp.ceil(jnp.log(jnp.maximum(largest, 1e-30)) * log2_e) - 14.0


def power(k):
    return jnp.exp(k * (1.0 / log2_e))


def top(value):
    return jnp.max(jnp.max(jnp.abs(value), axis=0, keepdims=True), axis=1, keepdims=True)


def split(value, width):
    head = value.astype(jnp.bfloat16).astype(jnp.float32)
    rest = (value - head) * 256.0
    wide = (1, width)
    return jnp.concatenate([jnp.broadcast_to(head, wide), jnp.broadcast_to(rest, wide)], axis=1)


def write_coded(out, blocks, scale, k, gains, loss):
    zs, lines, part = out.shape
    lines -= small_rows
    half = part // 2
    k_gain = exponent(functools.reduce(jnp.maximum, [top(g) for g in gains]))
    k_loss = exponent(loss)
    loss_row = split(loss * power(-k_loss), half)
    k_row = jnp.broadcast_to(k, (1, part))
    kk_row = jnp.concatenate(
        [jnp.broadcast_to(k_gain, (1, half)), jnp.broadcast_to(k_loss, (1, half))], axis=1
    )
    unit = power(-k_gain)
    for z in range(zs):
        out[z, pl.ds(0, lines), :] = blocks(z) * scale
        out[z, pl.ds(lines, 1), :] = split(gains[z] * unit, half)
        out[z, pl.ds(lines + 1, 1), :] = loss_row
        out[z, pl.ds(lines + 2, 1), :] = k_row
        out[z, pl.ds(lines + 3, 1), :] = kk_row
        out[z, pl.ds(lines + 4, small_rows - 4), :] = jnp.zeros((small_rows - 4, part), jnp.float32)


def read_coded(ref, z):
    lines = ref.shape[1] - small_rows
    half = ref.shape[2] // 2
    gain = ref[z, pl.ds(lines, 1), :]
    loss = ref[z, pl.ds(lines + 1, 1), :]
    k = ref[z, pl.ds(lines + 2, 1), :][:, :1]
    kk = ref[z, pl.ds(lines + 3, 1), :]
    return (
        power(k),
        (gain[:, :half] + gain[:, half:] * (1.0 / 256.0)) * power(kk[:, :1]),
        (loss[:, :1] + loss[:, half : half + 1] * (1.0 / 256.0)) * power(kk[:, half : half + 1]),
    )


def sum_kernel(core, *refs):
    (term, one, two, three), (s_term, s_one, s_two, s_three) = refs[:4], refs[4:8]
    outs, total = refs[8:-1], refs[-1]
    zs, lines, part = outs[0].shape
    lines -= small_rows
    rows = zs * lines
    half = part // 2
    small = (s_term[...] + s_two[...]) + (s_one[...] + s_three[...])
    first = small_rows - nx
    u_one, u_two, u_three = (
        ref[first + j : first + j + 1, :] for j, ref in ((1, s_one), (2, s_two), (3, s_three))
    )
    value = (term[...] + two[...] * u_two) + (one[...] * u_one + three[...] * u_three)
    total[...] = value
    k = exponent(top(value))
    scale = power(-k)
    gains = [small[z // 2 : z // 2 + 1, z % 2 * half : (z % 2 + 1) * half] for z in range(zs)]
    loss = small[zs // 2 : zs // 2 + 1, :1]
    for j, out in enumerate(outs):
        start = lax.rem(core[2] + j, ny) * rows
        write_coded(
            out,
            lambda z: total[pl.ds(pl.multiple_of(start + z * lines, lines), lines), :],
            scale,
            k,
            gains,
            loss,
        )


def second_kernel(term, one, two, three, out, total):
    zs, lines, _ = out.shape
    lines -= small_rows
    gains, loss, largest = [], None, None
    for z in range(zs):
        (u0, g0, l0), (u1, g1, l1), (u2, g2, l2), (u3, g3, l3) = (
            read_coded(ref, z) for ref in (term, one, two, three)
        )
        here = pl.ds(0, lines)
        value = (term[z, here, :] * u0 + two[z, here, :] * u2) + (
            one[z, here, :] * u1 + three[z, here, :] * u3
        )
        total[z] = value
        largest = top(value) if z == 0 else jnp.maximum(largest, top(value))
        gains.append((g0 + g2) + (g1 + g3))
        if z == 0:
            loss = (l0 + l2) + (l1 + l3)
    k = exponent(largest)
    write_coded(out, lambda z: total[z], power(-k), k, gains, loss)


def third_kernel(got, piece, small):
    zs, lines, part = got.shape
    lines -= small_rows
    half = part // 2
    value = gain = loss = None
    for z in range(zs):
        u, g, l = read_coded(got, z)
        here = got[z, pl.ds(0, lines), :] * u
        value, gain, loss = (here, g, l) if z == 0 else (value + here, gain + g, loss + l)
    piece[...] = value.astype(jnp.bfloat16)
    small[pl.ds(0, 1), :] = gain
    small[pl.ds(1, 1), :] = jnp.broadcast_to(loss, (1, half))
    small[pl.ds(2, small_rows - 2), :] = jnp.zeros((small_rows - 2, half), jnp.float32)


def last_kernel(scale, core, strip, other, small, small_par, head, gain, loss):
    half = strip.shape[1]
    head[:, pl.ds(pl.multiple_of(core[0] * half, half), half)] = strip[...].astype(jnp.float32)
    head[:, pl.ds(pl.multiple_of((1 - core[0]) * half, half), half)] = other[...].astype(
        jnp.float32
    )
    both = small[...] + small_par[...]
    gain[...] = both[0:1, :]
    loss[...] = both[1:2, 0:1] * scale


SMEM = pl.BlockSpec(memory_space=pltpu.SMEM)
VMEM = pl.BlockSpec(memory_space=pltpu.VMEM)
ANY = pl.BlockSpec(memory_space=pl.ANY)


def shape(dims, dtype):
    return jax.ShapeDtypeStruct(dims, dtype)


def limit(mebibytes):
    return pltpu.CompilerParams(vmem_limit_bytes=mebibytes << 20)


def cost(flops, moved):
    return pl.CostEstimate(flops=flops, bytes_accessed=moved, transcendentals=0)


def on_device(
    thinker_rows,
    codec_ids,
    block_lengths,
    chosen_label,
    ref_logratio,
    pair_count,
    proj_weight,
    norm_gain,
    head_weight,
):
    slots = thinker_rows.shape[2]
    frames = thinker_rows.shape[4]
    tw = thinker_rows.shape[5]
    k_shard, width = proj_weight.shape
    d_shard, vocab = head_weight.shape
    half_v = vocab // 2
    half_d = width // 2
    count = slots * 2 * frames
    block = 2 * frames
    part = half_v // nx
    lines = d_shard // ny
    bf16, f32 = jnp.bfloat16, jnp.float32
    w = lax.axis_index("wide")
    z = lax.axis_index("narrow")
    c = w % 2
    x = (w // 2) % nx
    y = w // (2 * nx)
    a = jnp.where(c == 0, x, y)
    b = jnp.where(c == 0, y, x)
    core = jnp.stack([c, a, b]).astype(jnp.int32)
    back = x + y - jnp.arange(nx)
    origin = jnp.concatenate([(back + 2 * c) % nx, (back + 2 - 2 * c) % nx])
    table = jnp.array([near, far], jnp.int32).T
    places = ((z + jnp.take(table, origin, axis=0)) % nz).reshape(-1).astype(jnp.int32)

    p_piece = lax.dynamic_slice(proj_weight, (0, c * half_d), (k_shard, half_d))
    h_piece = jnp.concatenate(
        [
            lax.dynamic_slice(head_weight, (0, c * half_v), (d_shard, half_v)),
            jnp.pad(norm_gain.reshape(1, d_shard), ((0, small_rows - 1), (0, half_v - d_shard))),
        ],
        axis=0,
    )
    p_stacks = spread(fetch(p_piece))
    p_stacks = p_stacks + swap_all(p_stacks)
    h_stacks = spread(fetch(h_piece))

    rows = thinker_rows.reshape(count, tw)
    project = pl.pallas_call(
        functools.partial(project_kernel, block),
        out_shape=shape((count, width), bf16),
        in_specs=[SMEM, SMEM, VMEM] + [ANY] * (2 * nx),
        out_specs=VMEM,
        scratch_shapes=[
            pltpu.VMEM((tw, half_d), bf16),
            pltpu.VMEM((tw, half_d), bf16),
            pltpu.SemaphoreType.DMA((4 * nx,)),
        ],
        cost_estimate=cost(2 * count * tw * width, 12 << 20),
        compiler_params=limit(16),
        name="project",
    )
    projected = project(places, core, rows, *p_stacks)
    h_stacks = h_stacks + swap_all(h_stacks)

    dl_own, dl_oth, turned, kept, loss = pl.pallas_call(
        functools.partial(logits_kernel, frames),
        out_shape=(
            shape((count, half_v), bf16),
            shape((count, half_v), bf16),
            shape((width, count), bf16),
            shape((count, width), bf16),
            shape((1, 1), f32),
        ),
        in_specs=[SMEM] * 6 + [VMEM, VMEM] + [ANY] * (2 * nx),
        out_specs=(VMEM,) * 5,
        scratch_shapes=[
            pltpu.VMEM((width, half_v), bf16),
            pltpu.VMEM((width, half_v), bf16),
            pltpu.VMEM((nz, small_rows, d_shard), bf16),
            pltpu.VMEM((block, half_v), f32),
            pltpu.VMEM((block, half_v), f32),
            pltpu.SemaphoreType.DMA((4 * nx,)),
            pltpu.SemaphoreType.DMA((2 * nx,)),
        ],
        cost_estimate=cost(2 * count * width * vocab, 12 << 20),
        compiler_params=limit(32),
        name="logits",
    )(
        places,
        core,
        block_lengths.reshape(-1),
        chosen_label.reshape(-1),
        ref_logratio.reshape(-1),
        pair_count.reshape(-1),
        projected,
        codec_ids.reshape(count, 1),
        *h_stacks,
    )
    dl_par = lax.ppermute(dl_oth, "wide", core_swap())
    turned_par = lax.ppermute(turned, "wide", core_swap())
    mine = pl.pallas_call(
        own_kernel,
        out_shape=shape((nx, width, part), f32),
        grid=(nx,),
        in_specs=[SMEM, VMEM, VMEM],
        out_specs=pl.BlockSpec((None, width, part), lambda j: (j, 0, 0)),
        compiler_params=limit(20),
        cost_estimate=cost(2 * count * width * half_v, 8 << 20),
        name="own",
    )(core, turned, dl_own)

    def head_term(j):
        outs = ((width, part),) + ((1, part),) * (j > 0)
        return pl.pallas_call(
            functools.partial(head_kernel, j),
            out_shape=tuple(shape(dims, f32) for dims in outs),
            grid=(1,),
            in_specs=[SMEM, pl.BlockSpec((None, width, part), lambda i: (j, 0, 0)), VMEM, VMEM],
            out_specs=tuple(pl.BlockSpec(dims, lambda i: (0, 0)) for dims in outs),
            cost_estimate=cost(2 * count * width * part, 4 << 20),
            compiler_params=limit(16),
            name="head",
        )(core, mine, turned_par, dl_par)

    terms = {j: head_term(j) for j in (2, 1, 3, 0)}
    sent = {
        j: lax.ppermute(
            lax.optimization_barrier(terms[j][0].astype(jnp.float16)), "wide", plane_shift(j, True)
        ).astype(f32)
        for j in (2, 1, 3)
    }
    small = pl.pallas_call(
        functools.partial(gain_kernel, block),
        out_shape=shape((small_rows, part), f32),
        in_specs=[SMEM] + [VMEM] * 7 + [ANY] * (2 * nx),
        out_specs=VMEM,
        scratch_shapes=[
            pltpu.VMEM((width, half_v), bf16),
            pltpu.VMEM((width, half_v), bf16),
            pltpu.VMEM((1, width), f32),
            pltpu.SemaphoreType.DMA((4 * nx,)),
        ],
        cost_estimate=cost(2 * count * width * vocab, 8 << 20),
        compiler_params=limit(24),
        name="gain",
    )(places, dl_own, dl_oth, kept, loss, *(terms[j][1] for j in (1, 2, 3)), *h_stacks)
    s_sent = {j: lax.ppermute(small, "wide", plane_shift(j, True)) for j in (2, 1, 3)}
    coded = (nz, lines + small_rows, part)
    f16 = jnp.float16
    chunks = pl.pallas_call(
        sum_kernel,
        out_shape=tuple(shape(coded, f32) for _ in range(ny)),
        in_specs=[SMEM] + [VMEM] * 8,
        out_specs=(VMEM,) * ny,
        scratch_shapes=[pltpu.VMEM((width, part), f32)],
        cost_estimate=cost(0, 5 << 20),
        compiler_params=limit(24),
        name="fold",
    )(core, terms[0][0], sent[1], sent[2], sent[3], small, s_sent[1], s_sent[2], s_sent[3])
    rounded = [lax.optimization_barrier(chunk.astype(f16)) for chunk in chunks]
    got = [rounded[0]] + [
        lax.ppermute(rounded[j], "wide", plane_shift(j, False)) for j in range(1, ny)
    ]
    second = pl.pallas_call(
        second_kernel,
        out_shape=shape(coded, f32),
        in_specs=[VMEM] * ny,
        out_specs=VMEM,
        scratch_shapes=[pltpu.VMEM((nz, lines, part), f32)],
        cost_estimate=cost(0, 2 << 20),
        compiler_params=limit(8),
        name="second",
    )(*(g.astype(f32) for g in got))
    second = lax.optimization_barrier(second.astype(f16))
    third = lax.all_to_all(second, "narrow", 0, 0, tiled=True).astype(f32)
    piece, rest = pl.pallas_call(
        third_kernel,
        out_shape=(shape((lines, part), bf16), shape((small_rows, d_shard), f32)),
        in_specs=[VMEM],
        out_specs=(VMEM, VMEM),
        cost_estimate=cost(0, 1 << 20),
        compiler_params=limit(8),
        name="third",
    )(third)

    strip_b = jnp.zeros((ny, lines, part), bf16)
    for j in range(ny):
        here = piece if j == 0 else lax.ppermute(piece, "wide", plane_shift(j, False))
        strip_b = lax.dynamic_update_index_in_dim(strip_b, here, (b - j) % ny, 0)
    strip_b = strip_b.reshape(d_shard, part)
    strip = jnp.zeros((d_shard, half_v), bf16)
    for j in range(nx):
        here = strip_b if j == 0 else lax.ppermute(strip_b, "wide", plane_shift(j, True))
        strip = lax.dynamic_update_slice(strip, here, (0, ((a - j) % nx) * part))
    other = lax.ppermute(strip, "wide", core_swap())
    rest_par = lax.ppermute(rest, "wide", core_swap())
    pair_total = lax.axis_size("wide") * nz * ((slots + 1) // 2)
    grad_head, grad_gain, loss_sum = pl.pallas_call(
        functools.partial(last_kernel, 1.0 / pair_total),
        out_shape=(
            shape((d_shard, vocab), f32),
            shape((1, d_shard), f32),
            shape((1, 1), f32),
        ),
        in_specs=[SMEM] + [VMEM] * 4,
        out_specs=(VMEM,) * 3,
        cost_estimate=cost(0, 2 << 20),
        compiler_params=limit(8),
        name="last",
    )(core, strip, other, rest, rest_par)
    return (loss_sum.reshape(()), grad_head, grad_gain.reshape(d_shard))


def solution(mesh):
    in_specs = (
        P("wide", "narrow", None, None, None, None),
        P("wide", "narrow", None, None, None),
        P("wide", "narrow", None, None),
        P("wide", "narrow", None),
        P("wide", "narrow", None),
        P("wide", "narrow"),
        P("narrow", None),
        P("narrow"),
        P("narrow", None),
    )
    out_specs = (P(), P("narrow", None), P("narrow"))
    return jax.shard_map(
        on_device, mesh=mesh, in_specs=in_specs, out_specs=out_specs, check_vma=False
    )
```

```python
import functools

import jax
import jax.numpy as jnp
from jax import lax
from jax.experimental import pallas as pl
from jax.experimental.pallas import tpu as pltpu
from jax.sharding import PartitionSpec as P


norm_eps = 1e-06
margin_scale = 2.0
nx = 4
ny = 4
nz = 8
near = (1, 2, 3, 4)
far = (-1, -2, -3, 0)
small_rows = 8
half_top = 16384.0
log2_e = 1.4426950408889634


def wide_index(x, y, c):
    return ((y % ny) * nx + x % nx) * 2 + c % 2


def core_swap():
    return [
        (wide_index(x, y, c), wide_index(x, y, 1 - c))
        for y in range(ny)
        for x in range(nx)
        for c in range(2)
    ]


def plane_shift(step, first):
    pairs = []
    for y in range(ny):
        for x in range(nx):
            for c in range(2):
                if (c == 0) == first:
                    pairs.append((wide_index(x, y, c), wide_index(x + step, y, c)))
                else:
                    pairs.append((wide_index(x, y, c), wide_index(x, y + step, c)))
    return pairs


def fetch_pairs(distance):
    pairs = []
    for y in range(ny):
        for x in range(nx):
            for c in range(2):
                w = wide_index(x, y, c)
                d = distance[(x + y + 2 * c) % nx]
                pairs.extend((w * nz + (z + d) % nz, w * nz + z) for z in range(nz))
    return pairs


def fetch(piece):
    both = ("wide", "narrow")
    got = []
    for distance in (near, far):
        got.append(lax.ppermute(piece, both, fetch_pairs(distance)))
    return got


def spread(pieces):
    stack = jnp.stack(pieces)
    got = [stack]
    for j in range(1, nx):
        got.append(lax.ppermute(stack, "wide", plane_shift(j, True)))
    return got


def swap_all(stacks):
    got = []
    for stack in stacks:
        got.append(lax.ppermute(stack, "wide", core_swap()))
    return got


def load_pieces(places, stacks, targets, sems, skip=0):
    copies = []
    for i, stack in enumerate(stacks):
        target = targets[i // nx]
        rows = target.shape[0] // nz
        for s in range(2):
            k = 2 * i + s
            at = pl.multiple_of(places[k + 2 * skip] * rows, rows)
            copies.append(
                pltpu.make_async_copy(
                    stack.at[s, pl.ds(0, rows), :], target.at[pl.ds(at, rows), :], sems.at[k]
                )
            )
    for copy in copies:
        copy.start()
    return copies


def project_kernel(block, places, core, rows, *refs):
    stacks, (projected,), (w_own, w_oth, sems) = (
        refs[: 2 * nx],
        refs[2 * nx : 2 * nx + 1],
        refs[2 * nx + 1 :],
    )
    copies = load_pieces(places, stacks, (w_own, w_oth), sems)
    half = w_own.shape[1]
    at_own = pl.multiple_of(core[0] * half, half)
    at_oth = pl.multiple_of((1 - core[0]) * half, half)
    for copy in copies:
        copy.wait()

    def step(i, carry):
        at = pl.multiple_of(i * block, block)
        here = rows[pl.ds(at, block), :]
        for weight, to in ((w_own, at_own), (w_oth, at_oth)):
            projected[pl.ds(at, block), pl.ds(to, half)] = jnp.dot(
                here, weight[...], preferred_element_type=jnp.float32
            ).astype(jnp.bfloat16)
        return carry

    lax.fori_loop(0, rows.shape[0] // block, step, 0)


def near_kernel(frames, places, projected, *refs):
    stacks, (logits, normed, turned, kept), (h_own, gains, sems, g_sems) = (
        refs[:nx],
        refs[nx : nx + 4],
        refs[nx + 4 :],
    )
    copies = load_pieces(places, stacks, (h_own,), sems)
    shard = h_own.shape[0] // nz
    for i in range(nx):
        for s in range(2):
            k = 2 * i + s
            copies.append(
                pltpu.make_async_copy(
                    stacks[i].at[s, pl.ds(shard, small_rows), pl.ds(0, shard)],
                    gains.at[places[k]],
                    g_sems.at[k],
                )
            )
            copies[-1].start()
    for copy in copies:
        copy.wait()
    block = 2 * frames
    lines = shard // ny
    gain = jnp.concatenate([gains[z, 0:1, :].astype(jnp.float32) for z in range(nz)], axis=1)

    def pair(p, carry):
        at = pl.multiple_of(p * block, block)
        kept[pl.ds(at, block), :] = projected[pl.ds(at, block), :]
        flat = projected[pl.ds(at, block), :].astype(jnp.float32)
        inverse = lax.rsqrt(jnp.mean(flat * flat, axis=1, keepdims=True) + norm_eps)
        value = flat * inverse * gain
        here = value.astype(jnp.bfloat16)
        normed[pl.ds(at, block), :] = here
        logits[pl.ds(at, block), :] = jnp.dot(
            here, h_own[...], preferred_element_type=jnp.float32
        )
        back = value.T.astype(jnp.bfloat16)
        for z in range(nz):
            for b in range(ny):
                turned[pl.ds((b * nz + z) * lines, lines), pl.ds(at, block)] = back[
                    (z * ny + b) * lines : (z * ny + b + 1) * lines, :
                ]
        return carry

    lax.fori_loop(0, projected.shape[0] // block, pair, 0)


def far_kernel(frames, places, core, lengths, labels, ratios, live, logits, normed, codes, *refs):
    stacks, (dl_own, dl_oth, loss), (h_oth, e_own, e_oth, sems) = (
        refs[:nx],
        refs[nx : nx + 3],
        refs[nx + 3 :],
    )
    copies = load_pieces(places, stacks, (h_oth,), sems, nx)
    loss[...] = jnp.zeros_like(loss)
    for copy in copies:
        copy.wait()
    half = h_oth.shape[1]
    block = 2 * frames

    def pair(p, carry):
        at = pl.multiple_of(p * block, block)
        code = codes[pl.ds(at, block), :]
        l_own = logits[pl.ds(at, block), :]
        l_oth = jnp.dot(
            normed[pl.ds(at, block), :], h_oth[...], preferred_element_type=jnp.float32
        )
        highest = jnp.maximum(
            jnp.max(l_own, axis=1, keepdims=True), jnp.max(l_oth, axis=1, keepdims=True)
        )
        columns = lax.broadcasted_iota(jnp.int32, l_own.shape, 1)
        hit_own = columns == code - core[0] * half
        hit_oth = columns == code - (1 - core[0]) * half
        picked = jnp.sum(jnp.where(hit_own, l_own, 0.0), axis=1, keepdims=True) + jnp.sum(
            jnp.where(hit_oth, l_oth, 0.0), axis=1, keepdims=True
        )
        x_own = jnp.exp(l_own - highest)
        x_oth = jnp.exp(l_oth - highest)
        e_own[...] = x_own
        e_oth[...] = x_oth
        total = jnp.sum(x_own, axis=1, keepdims=True) + jnp.sum(x_oth, axis=1, keepdims=True)
        logp = picked - (highest + jnp.log(total))
        frame = lax.broadcasted_iota(jnp.int32, (block, 1), 0)
        second = frame >= frames
        one = (frame < lengths[2 * p]) & jnp.logical_not(second)
        two = second & (frame - frames < lengths[2 * p + 1])
        length_one = jnp.full((1, 1), lengths[2 * p], jnp.int32).astype(jnp.float32)
        length_two = jnp.full((1, 1), lengths[2 * p + 1], jnp.int32).astype(jnp.float32)
        alive = jnp.full((1, 1), (p < live[0]).astype(jnp.int32), jnp.int32).astype(jnp.float32)
        score_one = jnp.sum(jnp.where(one, logp, 0.0), axis=0, keepdims=True) / length_one
        score_two = jnp.sum(jnp.where(two, logp, 0.0), axis=0, keepdims=True) / length_two
        sign = jnp.full((1, 1), 1 - 2 * labels[p], jnp.int32).astype(jnp.float32)
        margin = margin_scale * (sign * (score_one - score_two) - ratios[p])
        turn = jnp.exp(-jnp.abs(margin))
        loss[...] += alive * (jnp.maximum(-margin, 0.0) + jnp.log1p(turn))
        slope = -alive * jnp.where(margin >= 0.0, turn, 1.0) / (1.0 + turn)
        weight_one = margin_scale * sign * slope / length_one
        weight_two = -(margin_scale * sign * slope) / length_two
        coeff = jnp.where(one, weight_one, jnp.where(two, weight_two, 0.0))
        scale = 1.0 / total
        dl_own[pl.ds(at, block), :] = (
            coeff * (hit_own.astype(jnp.float32) - e_own[...] * scale)
        ).astype(jnp.bfloat16)
        dl_oth[pl.ds(at, block), :] = (
            coeff * (hit_oth.astype(jnp.float32) - e_oth[...] * scale)
        ).astype(jnp.bfloat16)
        return carry

    lax.fori_loop(0, normed.shape[0] // block, pair, 0)


def gain_kernel(block, places, dl_own, dl_oth, projected, loss, u_one, u_two, u_three, *refs):
    stacks, (small,), (h_own, h_oth, total, sems) = (
        refs[: 2 * nx],
        refs[2 * nx : 2 * nx + 1],
        refs[2 * nx + 1 :],
    )
    copies = load_pieces(places, stacks, (h_own, h_oth), sems)
    total[...] = jnp.zeros_like(total)
    for copy in copies:
        copy.wait()
    contract = (((1,), (1,)), ((), ()))

    def step(i, carry):
        at = pl.multiple_of(i * block, block)
        dnormed = lax.dot_general(
            dl_own[pl.ds(at, block), :], h_own[...], contract, preferred_element_type=jnp.float32
        ) + lax.dot_general(
            dl_oth[pl.ds(at, block), :], h_oth[...], contract, preferred_element_type=jnp.float32
        )
        flat = projected[pl.ds(at, block), :].astype(jnp.float32)
        inverse = lax.rsqrt(jnp.mean(flat * flat, axis=1, keepdims=True) + norm_eps)
        total[...] += jnp.sum(dnormed * flat * inverse, axis=0, keepdims=True)
        return carry

    lax.fori_loop(0, dl_own.shape[0] // block, step, 0)
    part = small.shape[1]
    count = total.shape[1] // part
    for k in range(count):
        small[pl.ds(k, 1), :] = total[:, k * part : (k + 1) * part]
    small[pl.ds(count, 1), :] = jnp.broadcast_to(loss[...], (1, part))
    for j, unit in ((1, u_one), (2, u_two), (3, u_three)):
        small[pl.ds(small_rows - nx + j, 1), :] = unit[...]


def own_kernel(core, turned, dl_own, out):
    part = out.shape[1]
    at = pl.multiple_of(lax.rem(core[1] + pl.program_id(0), nx) * part, part)
    out[...] = jnp.dot(
        turned[...], dl_own[:, pl.ds(at, part)], preferred_element_type=jnp.float32
    )


def head_kernel(shift, core, term, turned, dl_par, out, *refs):
    part = out.shape[1]
    at = pl.multiple_of(lax.rem(core[1] + shift, nx) * part, part)
    value = term[...] + jnp.dot(
        turned[...], dl_par[:, pl.ds(at, part)], preferred_element_type=jnp.float32
    )
    out[...] = value
    if not refs:
        return
    largest = jnp.max(jnp.max(jnp.abs(value), axis=0, keepdims=True), axis=1, keepdims=True)
    largest = jnp.maximum(largest, 1e-30)
    refs[0][...] = jnp.broadcast_to(largest / half_top, refs[0].shape)
    out[...] = out[...] * (half_top / largest)


def exponent(largest):
    return jnp.ceil(jnp.log(jnp.maximum(largest, 1e-30)) * log2_e) - 14.0


def power(k):
    return jnp.exp(k * (1.0 / log2_e))


def top(value):
    return jnp.max(jnp.max(jnp.abs(value), axis=0, keepdims=True), axis=1, keepdims=True)


def split(value, width):
    head = value.astype(jnp.bfloat16).astype(jnp.float32)
    rest = (value - head) * 256.0
    wide = (1, width)
    return jnp.concatenate([jnp.broadcast_to(head, wide), jnp.broadcast_to(rest, wide)], axis=1)


def write_coded(out, blocks, scale, k, gains, loss):
    zs, lines, part = out.shape
    lines -= small_rows
    half = part // 2
    k_gain = exponent(functools.reduce(jnp.maximum, [top(g) for g in gains]))
    k_loss = exponent(loss)
    loss_row = split(loss * power(-k_loss), half)
    k_row = jnp.broadcast_to(k, (1, part))
    kk_row = jnp.concatenate(
        [jnp.broadcast_to(k_gain, (1, half)), jnp.broadcast_to(k_loss, (1, half))], axis=1
    )
    unit = power(-k_gain)
    for z in range(zs):
        out[z, pl.ds(0, lines), :] = blocks(z) * scale
        out[z, pl.ds(lines, 1), :] = split(gains[z] * unit, half)
        out[z, pl.ds(lines + 1, 1), :] = loss_row
        out[z, pl.ds(lines + 2, 1), :] = k_row
        out[z, pl.ds(lines + 3, 1), :] = kk_row
        out[z, pl.ds(lines + 4, small_rows - 4), :] = jnp.zeros((small_rows - 4, part), jnp.float32)


def read_coded(ref, z):
    lines = ref.shape[1] - small_rows
    half = ref.shape[2] // 2
    gain = ref[z, pl.ds(lines, 1), :]
    loss = ref[z, pl.ds(lines + 1, 1), :]
    k = ref[z, pl.ds(lines + 2, 1), :][:, :1]
    kk = ref[z, pl.ds(lines + 3, 1), :]
    return (
        power(k),
        (gain[:, :half] + gain[:, half:] * (1.0 / 256.0)) * power(kk[:, :1]),
        (loss[:, :1] + loss[:, half : half + 1] * (1.0 / 256.0)) * power(kk[:, half : half + 1]),
    )


def sum_kernel(core, *refs):
    (term, one, two, three), (s_term, s_one, s_two, s_three) = refs[:4], refs[4:8]
    outs, total = refs[8:-1], refs[-1]
    zs, lines, part = outs[0].shape
    lines -= small_rows
    rows = zs * lines
    half = part // 2
    small = (s_term[...] + s_two[...]) + (s_one[...] + s_three[...])
    first = small_rows - nx
    u_one, u_two, u_three = (
        ref[first + j : first + j + 1, :] for j, ref in ((1, s_one), (2, s_two), (3, s_three))
    )
    value = (term[...] + two[...] * u_two) + (one[...] * u_one + three[...] * u_three)
    total[...] = value
    k = exponent(top(value))
    scale = power(-k)
    gains = [small[z // 2 : z // 2 + 1, z % 2 * half : (z % 2 + 1) * half] for z in range(zs)]
    loss = small[zs // 2 : zs // 2 + 1, :1]
    for j, out in enumerate(outs):
        start = lax.rem(core[2] + j, ny) * rows
        write_coded(
            out,
            lambda z: total[pl.ds(pl.multiple_of(start + z * lines, lines), lines), :],
            scale,
            k,
            gains,
            loss,
        )


def second_kernel(term, one, two, three, out, total):
    zs, lines, _ = out.shape
    lines -= small_rows
    gains, loss, largest = [], None, None
    for z in range(zs):
        (u0, g0, l0), (u1, g1, l1), (u2, g2, l2), (u3, g3, l3) = (
            read_coded(ref, z) for ref in (term, one, two, three)
        )
        here = pl.ds(0, lines)
        value = (term[z, here, :] * u0 + two[z, here, :] * u2) + (
            one[z, here, :] * u1 + three[z, here, :] * u3
        )
        total[z] = value
        largest = top(value) if z == 0 else jnp.maximum(largest, top(value))
        gains.append((g0 + g2) + (g1 + g3))
        if z == 0:
            loss = (l0 + l2) + (l1 + l3)
    k = exponent(largest)
    write_coded(out, lambda z: total[z], power(-k), k, gains, loss)


def third_kernel(got, piece, small):
    zs, lines, part = got.shape
    lines -= small_rows
    half = part // 2
    value = gain = loss = None
    for z in range(zs):
        u, g, l = read_coded(got, z)
        here = got[z, pl.ds(0, lines), :] * u
        value, gain, loss = (here, g, l) if z == 0 else (value + here, gain + g, loss + l)
    piece[...] = value.astype(jnp.bfloat16)
    small[pl.ds(0, 1), :] = gain
    small[pl.ds(1, 1), :] = jnp.broadcast_to(loss, (1, half))
    small[pl.ds(2, small_rows - 2), :] = jnp.zeros((small_rows - 2, half), jnp.float32)


def last_kernel(scale, core, strip, other, small, small_par, head, gain, loss):
    half = strip.shape[1]
    head[:, pl.ds(pl.multiple_of(core[0] * half, half), half)] = strip[...].astype(jnp.float32)
    head[:, pl.ds(pl.multiple_of((1 - core[0]) * half, half), half)] = other[...].astype(
        jnp.float32
    )
    both = small[...] + small_par[...]
    gain[...] = both[0:1, :]
    loss[...] = both[1:2, 0:1] * scale


SMEM = pl.BlockSpec(memory_space=pltpu.SMEM)
VMEM = pl.BlockSpec(memory_space=pltpu.VMEM)
ANY = pl.BlockSpec(memory_space=pl.ANY)


def shape(dims, dtype):
    return jax.ShapeDtypeStruct(dims, dtype)


def limit(mebibytes):
    return pltpu.CompilerParams(vmem_limit_bytes=mebibytes << 20)


def cost(flops, moved):
    return pl.CostEstimate(flops=flops, bytes_accessed=moved, transcendentals=0)


def on_device(
    thinker_rows,
    codec_ids,
    block_lengths,
    chosen_label,
    ref_logratio,
    pair_count,
    proj_weight,
    norm_gain,
    head_weight,
):
    slots = thinker_rows.shape[2]
    frames = thinker_rows.shape[4]
    tw = thinker_rows.shape[5]
    k_shard, width = proj_weight.shape
    d_shard, vocab = head_weight.shape
    half_v = vocab // 2
    half_d = width // 2
    count = slots * 2 * frames
    block = 2 * frames
    part = half_v // nx
    lines = d_shard // ny
    bf16, f32 = jnp.bfloat16, jnp.float32
    w = lax.axis_index("wide")
    z = lax.axis_index("narrow")
    c = w % 2
    x = (w // 2) % nx
    y = w // (2 * nx)
    a = jnp.where(c == 0, x, y)
    b = jnp.where(c == 0, y, x)
    core = jnp.stack([c, a, b]).astype(jnp.int32)
    back = x + y - jnp.arange(nx)
    origin = jnp.concatenate([(back + 2 * c) % nx, (back + 2 - 2 * c) % nx])
    table = jnp.array([near, far], jnp.int32).T
    places = ((z + jnp.take(table, origin, axis=0)) % nz).reshape(-1).astype(jnp.int32)

    p_piece = lax.dynamic_slice(proj_weight, (0, c * half_d), (k_shard, half_d))
    h_piece = jnp.concatenate(
        [
            lax.dynamic_slice(head_weight, (0, c * half_v), (d_shard, half_v)),
            jnp.pad(norm_gain.reshape(1, d_shard), ((0, small_rows - 1), (0, half_v - d_shard))),
        ],
        axis=0,
    )
    p_stacks = spread(fetch(p_piece))
    p_stacks = p_stacks + swap_all(p_stacks)
    h_stacks = spread(fetch(h_piece))

    rows = thinker_rows.reshape(count, tw)
    project = pl.pallas_call(
        functools.partial(project_kernel, block),
        out_shape=shape((count, width), bf16),
        in_specs=[SMEM, SMEM, VMEM] + [ANY] * (2 * nx),
        out_specs=VMEM,
        scratch_shapes=[
            pltpu.VMEM((tw, half_d), bf16),
            pltpu.VMEM((tw, half_d), bf16),
            pltpu.SemaphoreType.DMA((4 * nx,)),
        ],
        cost_estimate=cost(2 * count * tw * width, 12 << 20),
        compiler_params=limit(16),
        name="project",
    )
    projected = project(places, core, rows, *p_stacks)
    h_stacks = h_stacks + swap_all(h_stacks)

    near_half = pl.pallas_call(
        functools.partial(near_kernel, frames),
        out_shape=(
            shape((count, half_v), f32),
            shape((count, width), bf16),
            shape((width, count), bf16),
            shape((count, width), bf16),
        ),
        in_specs=[SMEM, VMEM] + [ANY] * nx,
        out_specs=(VMEM,) * 4,
        scratch_shapes=[
            pltpu.VMEM((width, half_v), bf16),
            pltpu.VMEM((nz, small_rows, d_shard), bf16),
            pltpu.SemaphoreType.DMA((2 * nx,)),
            pltpu.SemaphoreType.DMA((2 * nx,)),
        ],
        cost_estimate=cost(2 * count * width * half_v, 6 << 20),
        compiler_params=limit(20),
        name="near",
    )
    logits, normed, turned, kept = near_half(places, projected, *h_stacks[:nx])
    turned_par = lax.ppermute(turned, "wide", core_swap())
    far_half = pl.pallas_call(
        functools.partial(far_kernel, frames),
        out_shape=(
            shape((count, half_v), bf16),
            shape((count, half_v), bf16),
            shape((1, 1), f32),
        ),
        in_specs=[SMEM] * 6 + [VMEM] * 3 + [ANY] * nx,
        out_specs=(VMEM,) * 3,
        scratch_shapes=[
            pltpu.VMEM((width, half_v), bf16),
            pltpu.VMEM((block, half_v), f32),
            pltpu.VMEM((block, half_v), f32),
            pltpu.SemaphoreType.DMA((2 * nx,)),
        ],
        cost_estimate=cost(2 * count * width * half_v, 8 << 20),
        compiler_params=limit(24),
        name="far",
    )
    dl_own, dl_oth, loss = far_half(
        places,
        core,
        block_lengths.reshape(-1),
        chosen_label.reshape(-1),
        ref_logratio.reshape(-1),
        pair_count.reshape(-1),
        logits,
        normed,
        codec_ids.reshape(count, 1),
        *h_stacks[nx:],
    )
    dl_par = lax.ppermute(dl_oth, "wide", core_swap())
    mine = pl.pallas_call(
        own_kernel,
        out_shape=shape((nx, width, part), f32),
        grid=(nx,),
        in_specs=[SMEM, VMEM, VMEM],
        out_specs=pl.BlockSpec((None, width, part), lambda j: (j, 0, 0)),
        compiler_params=limit(20),
        cost_estimate=cost(2 * count * width * half_v, 8 << 20),
        name="own",
    )(core, turned, dl_own)

    def head_term(j):
        outs = ((width, part),) + ((1, part),) * (j > 0)
        return pl.pallas_call(
            functools.partial(head_kernel, j),
            out_shape=tuple(shape(dims, f32) for dims in outs),
            grid=(1,),
            in_specs=[SMEM, pl.BlockSpec((None, width, part), lambda i: (j, 0, 0)), VMEM, VMEM],
            out_specs=tuple(pl.BlockSpec(dims, lambda i: (0, 0)) for dims in outs),
            cost_estimate=cost(2 * count * width * part, 4 << 20),
            compiler_params=limit(16),
            name="head",
        )(core, mine, turned_par, dl_par)

    terms = {j: head_term(j) for j in (2, 1, 3, 0)}
    sent = {
        j: lax.ppermute(
            lax.optimization_barrier(terms[j][0].astype(jnp.float16)), "wide", plane_shift(j, True)
        ).astype(f32)
        for j in (2, 1, 3)
    }
    small = pl.pallas_call(
        functools.partial(gain_kernel, block),
        out_shape=shape((small_rows, part), f32),
        in_specs=[SMEM] + [VMEM] * 7 + [ANY] * (2 * nx),
        out_specs=VMEM,
        scratch_shapes=[
            pltpu.VMEM((width, half_v), bf16),
            pltpu.VMEM((width, half_v), bf16),
            pltpu.VMEM((1, width), f32),
            pltpu.SemaphoreType.DMA((4 * nx,)),
        ],
        cost_estimate=cost(2 * count * width * vocab, 8 << 20),
        compiler_params=limit(24),
        name="gain",
    )(places, dl_own, dl_oth, kept, loss, *(terms[j][1] for j in (1, 2, 3)), *h_stacks)
    s_sent = {j: lax.ppermute(small, "wide", plane_shift(j, True)) for j in (2, 1, 3)}
    coded = (nz, lines + small_rows, part)
    f16 = jnp.float16
    chunks = pl.pallas_call(
        sum_kernel,
        out_shape=tuple(shape(coded, f32) for _ in range(ny)),
        in_specs=[SMEM] + [VMEM] * 8,
        out_specs=(VMEM,) * ny,
        scratch_shapes=[pltpu.VMEM((width, part), f32)],
        cost_estimate=cost(0, 5 << 20),
        compiler_params=limit(24),
        name="fold",
    )(core, terms[0][0], sent[1], sent[2], sent[3], small, s_sent[1], s_sent[2], s_sent[3])
    rounded = [lax.optimization_barrier(chunk.astype(f16)) for chunk in chunks]
    got = [rounded[0]] + [
        lax.ppermute(rounded[j], "wide", plane_shift(j, False)) for j in range(1, ny)
    ]
    second = pl.pallas_call(
        second_kernel,
        out_shape=shape(coded, f32),
        in_specs=[VMEM] * ny,
        out_specs=VMEM,
        scratch_shapes=[pltpu.VMEM((nz, lines, part), f32)],
        cost_estimate=cost(0, 2 << 20),
        compiler_params=limit(8),
        name="second",
    )(*(g.astype(f32) for g in got))
    second = lax.optimization_barrier(second.astype(f16))
    third = lax.all_to_all(second, "narrow", 0, 0, tiled=True).astype(f32)
    piece, rest = pl.pallas_call(
        third_kernel,
        out_shape=(shape((lines, part), bf16), shape((small_rows, d_shard), f32)),
        in_specs=[VMEM],
        out_specs=(VMEM, VMEM),
        cost_estimate=cost(0, 1 << 20),
        compiler_params=limit(8),
        name="third",
    )(third)

    rest_par = lax.ppermute(rest, "wide", core_swap())
    strip_b = jnp.zeros((ny, lines, part), bf16)
    for j in range(ny):
        here = piece if j == 0 else lax.ppermute(piece, "wide", plane_shift(j, False))
        strip_b = lax.dynamic_update_index_in_dim(strip_b, here, (b - j) % ny, 0)
    strip_b = strip_b.reshape(d_shard, part)
    strip = jnp.zeros((d_shard, half_v), bf16)
    for j in range(nx):
        here = strip_b if j == 0 else lax.ppermute(strip_b, "wide", plane_shift(j, True))
        strip = lax.dynamic_update_slice(strip, here, (0, ((a - j) % nx) * part))
    other = lax.ppermute(strip, "wide", core_swap())
    pair_total = lax.axis_size("wide") * nz * ((slots + 1) // 2)
    grad_head, grad_gain, loss_sum = pl.pallas_call(
        functools.partial(last_kernel, 1.0 / pair_total),
        out_shape=(
            shape((d_shard, vocab), f32),
            shape((1, d_shard), f32),
            shape((1, 1), f32),
        ),
        in_specs=[SMEM] + [VMEM] * 4,
        out_specs=(VMEM,) * 3,
        cost_estimate=cost(0, 2 << 20),
        compiler_params=limit(8),
        name="last",
    )(core, strip, other, rest, rest_par)
    return (loss_sum.reshape(()), grad_head, grad_gain.reshape(d_shard))


def solution(mesh):
    in_specs = (
        P("wide", "narrow", None, None, None, None),
        P("wide", "narrow", None, None, None),
        P("wide", "narrow", None, None),
        P("wide", "narrow", None),
        P("wide", "narrow", None),
        P("wide", "narrow"),
        P("narrow", None),
        P("narrow"),
        P("narrow", None),
    )
    out_specs = (P(), P("narrow", None), P("narrow"))
    return jax.shard_map(
        on_device, mesh=mesh, in_specs=in_specs, out_specs=out_specs, check_vma=False
    )
```

```python
import functools

import jax
import jax.numpy as jnp
from jax import lax
from jax.experimental import pallas as pl
from jax.experimental.pallas import tpu as pltpu
from jax.sharding import PartitionSpec as P


norm_eps = 1e-06
margin_scale = 2.0
nx = 4
ny = 4
nz = 8
near = (1, 2, 3, 4)
far = (-1, -2, -3, 0)
small_rows = 8
half_top = 16384.0
log2_e = 1.4426950408889634


def wide_index(x, y, c):
    return ((y % ny) * nx + x % nx) * 2 + c % 2


def core_swap():
    return [
        (wide_index(x, y, c), wide_index(x, y, 1 - c))
        for y in range(ny)
        for x in range(nx)
        for c in range(2)
    ]


def plane_shift(step, first):
    pairs = []
    for y in range(ny):
        for x in range(nx):
            for c in range(2):
                if (c == 0) == first:
                    pairs.append((wide_index(x, y, c), wide_index(x + step, y, c)))
                else:
                    pairs.append((wide_index(x, y, c), wide_index(x, y + step, c)))
    return pairs


def fetch_pairs(distance):
    pairs = []
    for y in range(ny):
        for x in range(nx):
            for c in range(2):
                w = wide_index(x, y, c)
                d = distance[(x + y + 2 * c) % nx]
                pairs.extend((w * nz + (z + d) % nz, w * nz + z) for z in range(nz))
    return pairs


def fetch(piece):
    both = ("wide", "narrow")
    got = []
    for distance in (near, far):
        got.append(lax.ppermute(piece, both, fetch_pairs(distance)))
    return got


def spread(pieces):
    stack = jnp.stack(pieces)
    got = [stack]
    for j in range(1, nx):
        got.append(lax.ppermute(stack, "wide", plane_shift(j, True)))
    return got


def swap_all(stacks):
    got = []
    for stack in stacks:
        got.append(lax.ppermute(stack, "wide", core_swap()))
    return got


def load_pieces(places, stacks, targets, sems, skip=0):
    copies = []
    for i, stack in enumerate(stacks):
        target = targets[i // nx]
        rows = target.shape[0] // nz
        for s in range(2):
            k = 2 * i + s
            at = pl.multiple_of(places[k + 2 * skip] * rows, rows)
            copies.append(
                pltpu.make_async_copy(
                    stack.at[s, pl.ds(0, rows), :], target.at[pl.ds(at, rows), :], sems.at[k]
                )
            )
    for copy in copies:
        copy.start()
    return copies


def project_kernel(block, skip, places, rows, *refs):
    stacks, (projected, weight, sems) = refs[:nx], refs[nx:]
    copies = load_pieces(places, stacks, (weight,), sems, skip)
    for copy in copies:
        copy.wait()

    def step(i, carry):
        here = pl.ds(pl.multiple_of(i * block, block), block)
        projected[here, :] = jnp.dot(
            rows[here, :], weight[...], preferred_element_type=jnp.float32
        ).astype(jnp.bfloat16)
        return carry

    lax.fori_loop(0, rows.shape[0] // block, step, 0)


def near_kernel(frames, places, core, half_own, half_oth, *refs):
    stacks, (logits, normed, turned, kept), (h_own, gains, sems, g_sems) = (
        refs[:nx],
        refs[nx : nx + 4],
        refs[nx + 4 :],
    )
    copies = load_pieces(places, stacks, (h_own,), sems)
    shard = h_own.shape[0] // nz
    for i in range(nx):
        for s in range(2):
            k = 2 * i + s
            copies.append(
                pltpu.make_async_copy(
                    stacks[i].at[s, pl.ds(shard, small_rows), pl.ds(0, shard)],
                    gains.at[places[k]],
                    g_sems.at[k],
                )
            )
            copies[-1].start()
    for copy in copies:
        copy.wait()
    block = 2 * frames
    half = half_own.shape[1]
    at_own = pl.multiple_of(core[0] * half, half)
    at_oth = pl.multiple_of((1 - core[0]) * half, half)
    lines = shard // ny
    gain = jnp.concatenate([gains[z, 0:1, :].astype(jnp.float32) for z in range(nz)], axis=1)

    def pair(p, carry):
        at = pl.multiple_of(p * block, block)
        kept[pl.ds(at, block), pl.ds(at_own, half)] = half_own[pl.ds(at, block), :]
        kept[pl.ds(at, block), pl.ds(at_oth, half)] = half_oth[pl.ds(at, block), :]
        flat = kept[pl.ds(at, block), :].astype(jnp.float32)
        inverse = lax.rsqrt(jnp.mean(flat * flat, axis=1, keepdims=True) + norm_eps)
        value = flat * inverse * gain
        here = value.astype(jnp.bfloat16)
        normed[pl.ds(at, block), :] = here
        logits[pl.ds(at, block), :] = jnp.dot(
            here, h_own[...], preferred_element_type=jnp.float32
        )
        back = value.T.astype(jnp.bfloat16)
        for z in range(nz):
            for b in range(ny):
                turned[pl.ds((b * nz + z) * lines, lines), pl.ds(at, block)] = back[
                    (z * ny + b) * lines : (z * ny + b + 1) * lines, :
                ]
        return carry

    lax.fori_loop(0, half_own.shape[0] // block, pair, 0)


def far_kernel(frames, places, core, lengths, labels, ratios, live, logits, normed, codes, *refs):
    stacks, (dl_own, dl_oth, loss), (h_oth, e_own, e_oth, sems) = (
        refs[:nx],
        refs[nx : nx + 3],
        refs[nx + 3 :],
    )
    copies = load_pieces(places, stacks, (h_oth,), sems, nx)
    loss[...] = jnp.zeros_like(loss)
    for copy in copies:
        copy.wait()
    half = h_oth.shape[1]
    block = 2 * frames

    def pair(p, carry):
        at = pl.multiple_of(p * block, block)
        code = codes[pl.ds(at, block), :]
        l_own = logits[pl.ds(at, block), :]
        l_oth = jnp.dot(
            normed[pl.ds(at, block), :], h_oth[...], preferred_element_type=jnp.float32
        )
        highest = jnp.maximum(
            jnp.max(l_own, axis=1, keepdims=True), jnp.max(l_oth, axis=1, keepdims=True)
        )
        columns = lax.broadcasted_iota(jnp.int32, l_own.shape, 1)
        hit_own = columns == code - core[0] * half
        hit_oth = columns == code - (1 - core[0]) * half
        picked = jnp.sum(jnp.where(hit_own, l_own, 0.0), axis=1, keepdims=True) + jnp.sum(
            jnp.where(hit_oth, l_oth, 0.0), axis=1, keepdims=True
        )
        x_own = jnp.exp(l_own - highest)
        x_oth = jnp.exp(l_oth - highest)
        e_own[...] = x_own
        e_oth[...] = x_oth
        total = jnp.sum(x_own, axis=1, keepdims=True) + jnp.sum(x_oth, axis=1, keepdims=True)
        logp = picked - (highest + jnp.log(total))
        frame = lax.broadcasted_iota(jnp.int32, (block, 1), 0)
        second = frame >= frames
        one = (frame < lengths[2 * p]) & jnp.logical_not(second)
        two = second & (frame - frames < lengths[2 * p + 1])
        length_one = jnp.full((1, 1), lengths[2 * p], jnp.int32).astype(jnp.float32)
        length_two = jnp.full((1, 1), lengths[2 * p + 1], jnp.int32).astype(jnp.float32)
        alive = jnp.full((1, 1), (p < live[0]).astype(jnp.int32), jnp.int32).astype(jnp.float32)
        score_one = jnp.sum(jnp.where(one, logp, 0.0), axis=0, keepdims=True) / length_one
        score_two = jnp.sum(jnp.where(two, logp, 0.0), axis=0, keepdims=True) / length_two
        sign = jnp.full((1, 1), 1 - 2 * labels[p], jnp.int32).astype(jnp.float32)
        margin = margin_scale * (sign * (score_one - score_two) - ratios[p])
        turn = jnp.exp(-jnp.abs(margin))
        loss[...] += alive * (jnp.maximum(-margin, 0.0) + jnp.log1p(turn))
        slope = -alive * jnp.where(margin >= 0.0, turn, 1.0) / (1.0 + turn)
        weight_one = margin_scale * sign * slope / length_one
        weight_two = -(margin_scale * sign * slope) / length_two
        coeff = jnp.where(one, weight_one, jnp.where(two, weight_two, 0.0))
        scale = 1.0 / total
        dl_own[pl.ds(at, block), :] = (
            coeff * (hit_own.astype(jnp.float32) - e_own[...] * scale)
        ).astype(jnp.bfloat16)
        dl_oth[pl.ds(at, block), :] = (
            coeff * (hit_oth.astype(jnp.float32) - e_oth[...] * scale)
        ).astype(jnp.bfloat16)
        return carry

    lax.fori_loop(0, normed.shape[0] // block, pair, 0)


def gain_kernel(block, places, dl_own, dl_oth, projected, loss, u_one, u_two, u_three, *refs):
    stacks, (small,), (h_own, h_oth, total, sems) = (
        refs[: 2 * nx],
        refs[2 * nx : 2 * nx + 1],
        refs[2 * nx + 1 :],
    )
    copies = load_pieces(places, stacks, (h_own, h_oth), sems)
    total[...] = jnp.zeros_like(total)
    for copy in copies:
        copy.wait()
    contract = (((1,), (1,)), ((), ()))

    def step(i, carry):
        at = pl.multiple_of(i * block, block)
        dnormed = lax.dot_general(
            dl_own[pl.ds(at, block), :], h_own[...], contract, preferred_element_type=jnp.float32
        ) + lax.dot_general(
            dl_oth[pl.ds(at, block), :], h_oth[...], contract, preferred_element_type=jnp.float32
        )
        flat = projected[pl.ds(at, block), :].astype(jnp.float32)
        inverse = lax.rsqrt(jnp.mean(flat * flat, axis=1, keepdims=True) + norm_eps)
        total[...] += jnp.sum(dnormed * flat * inverse, axis=0, keepdims=True)
        return carry

    lax.fori_loop(0, dl_own.shape[0] // block, step, 0)
    part = small.shape[1]
    count = total.shape[1] // part
    for k in range(count):
        small[pl.ds(k, 1), :] = total[:, k * part : (k + 1) * part]
    small[pl.ds(count, 1), :] = jnp.broadcast_to(loss[...], (1, part))
    for j, unit in ((1, u_one), (2, u_two), (3, u_three)):
        small[pl.ds(small_rows - nx + j, 1), :] = unit[...]


def own_kernel(core, turned, dl_own, out):
    part = out.shape[1]
    at = pl.multiple_of(lax.rem(core[1] + pl.program_id(0), nx) * part, part)
    out[...] = jnp.dot(
        turned[...], dl_own[:, pl.ds(at, part)], preferred_element_type=jnp.float32
    )


def head_kernel(shift, core, term, turned, dl_par, out, *refs):
    part = out.shape[1]
    at = pl.multiple_of(lax.rem(core[1] + shift, nx) * part, part)
    value = term[...] + jnp.dot(
        turned[...], dl_par[:, pl.ds(at, part)], preferred_element_type=jnp.float32
    )
    out[...] = value
    if not refs:
        return
    largest = jnp.max(jnp.max(jnp.abs(value), axis=0, keepdims=True), axis=1, keepdims=True)
    largest = jnp.maximum(largest, 1e-30)
    refs[0][...] = jnp.broadcast_to(largest / half_top, refs[0].shape)
    out[...] = out[...] * (half_top / largest)


def exponent(largest):
    return jnp.ceil(jnp.log(jnp.maximum(largest, 1e-30)) * log2_e) - 14.0


def power(k):
    return jnp.exp(k * (1.0 / log2_e))


def top(value):
    return jnp.max(jnp.max(jnp.abs(value), axis=0, keepdims=True), axis=1, keepdims=True)


def split(value, width):
    head = value.astype(jnp.bfloat16).astype(jnp.float32)
    rest = (value - head) * 256.0
    wide = (1, width)
    return jnp.concatenate([jnp.broadcast_to(head, wide), jnp.broadcast_to(rest, wide)], axis=1)


def write_coded(out, blocks, scale, k, gains, loss):
    zs, lines, part = out.shape
    lines -= small_rows
    half = part // 2
    k_gain = exponent(functools.reduce(jnp.maximum, [top(g) for g in gains]))
    k_loss = exponent(loss)
    loss_row = split(loss * power(-k_loss), half)
    k_row = jnp.broadcast_to(k, (1, part))
    kk_row = jnp.concatenate(
        [jnp.broadcast_to(k_gain, (1, half)), jnp.broadcast_to(k_loss, (1, half))], axis=1
    )
    unit = power(-k_gain)
    for z in range(zs):
        out[z, pl.ds(0, lines), :] = blocks(z) * scale
        out[z, pl.ds(lines, 1), :] = split(gains[z] * unit, half)
        out[z, pl.ds(lines + 1, 1), :] = loss_row
        out[z, pl.ds(lines + 2, 1), :] = k_row
        out[z, pl.ds(lines + 3, 1), :] = kk_row
        out[z, pl.ds(lines + 4, small_rows - 4), :] = jnp.zeros((small_rows - 4, part), jnp.float32)


def read_coded(ref, z):
    lines = ref.shape[1] - small_rows
    half = ref.shape[2] // 2
    gain = ref[z, pl.ds(lines, 1), :]
    loss = ref[z, pl.ds(lines + 1, 1), :]
    k = ref[z, pl.ds(lines + 2, 1), :][:, :1]
    kk = ref[z, pl.ds(lines + 3, 1), :]
    return (
        power(k),
        (gain[:, :half] + gain[:, half:] * (1.0 / 256.0)) * power(kk[:, :1]),
        (loss[:, :1] + loss[:, half : half + 1] * (1.0 / 256.0)) * power(kk[:, half : half + 1]),
    )


def sum_kernel(core, *refs):
    (term, one, two, three), (s_term, s_one, s_two, s_three) = refs[:4], refs[4:8]
    outs, total = refs[8:-1], refs[-1]
    zs, lines, part = outs[0].shape
    lines -= small_rows
    rows = zs * lines
    half = part // 2
    small = (s_term[...] + s_two[...]) + (s_one[...] + s_three[...])
    first = small_rows - nx
    u_one, u_two, u_three = (
        ref[first + j : first + j + 1, :] for j, ref in ((1, s_one), (2, s_two), (3, s_three))
    )
    value = (term[...] + two[...] * u_two) + (one[...] * u_one + three[...] * u_three)
    total[...] = value
    k = exponent(top(value))
    scale = power(-k)
    gains = [small[z // 2 : z // 2 + 1, z % 2 * half : (z % 2 + 1) * half] for z in range(zs)]
    loss = small[zs // 2 : zs // 2 + 1, :1]
    for j, out in enumerate(outs):
        start = lax.rem(core[2] + j, ny) * rows
        write_coded(
            out,
            lambda z: total[pl.ds(pl.multiple_of(start + z * lines, lines), lines), :],
            scale,
            k,
            gains,
            loss,
        )


def second_kernel(term, one, two, three, out, total):
    zs, lines, _ = out.shape
    lines -= small_rows
    gains, loss, largest = [], None, None
    for z in range(zs):
        (u0, g0, l0), (u1, g1, l1), (u2, g2, l2), (u3, g3, l3) = (
            read_coded(ref, z) for ref in (term, one, two, three)
        )
        here = pl.ds(0, lines)
        value = (term[z, here, :] * u0 + two[z, here, :] * u2) + (
            one[z, here, :] * u1 + three[z, here, :] * u3
        )
        total[z] = value
        largest = top(value) if z == 0 else jnp.maximum(largest, top(value))
        gains.append((g0 + g2) + (g1 + g3))
        if z == 0:
            loss = (l0 + l2) + (l1 + l3)
    k = exponent(largest)
    write_coded(out, lambda z: total[z], power(-k), k, gains, loss)


def third_kernel(got, piece, small):
    zs, lines, part = got.shape
    lines -= small_rows
    half = part // 2
    value = gain = loss = None
    for z in range(zs):
        u, g, l = read_coded(got, z)
        here = got[z, pl.ds(0, lines), :] * u
        value, gain, loss = (here, g, l) if z == 0 else (value + here, gain + g, loss + l)
    piece[...] = value.astype(jnp.bfloat16)
    small[pl.ds(0, 1), :] = gain
    small[pl.ds(1, 1), :] = jnp.broadcast_to(loss, (1, half))
    small[pl.ds(2, small_rows - 2), :] = jnp.zeros((small_rows - 2, half), jnp.float32)


def last_kernel(scale, core, strip, other, small, small_par, head, gain, loss):
    half = strip.shape[1]
    head[:, pl.ds(pl.multiple_of(core[0] * half, half), half)] = strip[...].astype(jnp.float32)
    head[:, pl.ds(pl.multiple_of((1 - core[0]) * half, half), half)] = other[...].astype(
        jnp.float32
    )
    both = small[...] + small_par[...]
    gain[...] = both[0:1, :]
    loss[...] = both[1:2, 0:1] * scale


SMEM = pl.BlockSpec(memory_space=pltpu.SMEM)
VMEM = pl.BlockSpec(memory_space=pltpu.VMEM)
ANY = pl.BlockSpec(memory_space=pl.ANY)


def shape(dims, dtype):
    return jax.ShapeDtypeStruct(dims, dtype)


def limit(mebibytes):
    return pltpu.CompilerParams(vmem_limit_bytes=mebibytes << 20)


def cost(flops, moved):
    return pl.CostEstimate(flops=flops, bytes_accessed=moved, transcendentals=0)


def on_device(
    thinker_rows,
    codec_ids,
    block_lengths,
    chosen_label,
    ref_logratio,
    pair_count,
    proj_weight,
    norm_gain,
    head_weight,
):
    slots = thinker_rows.shape[2]
    frames = thinker_rows.shape[4]
    tw = thinker_rows.shape[5]
    k_shard, width = proj_weight.shape
    d_shard, vocab = head_weight.shape
    half_v = vocab // 2
    half_d = width // 2
    count = slots * 2 * frames
    block = 2 * frames
    part = half_v // nx
    lines = d_shard // ny
    bf16, f32 = jnp.bfloat16, jnp.float32
    w = lax.axis_index("wide")
    z = lax.axis_index("narrow")
    c = w % 2
    x = (w // 2) % nx
    y = w // (2 * nx)
    a = jnp.where(c == 0, x, y)
    b = jnp.where(c == 0, y, x)
    core = jnp.stack([c, a, b]).astype(jnp.int32)
    back = x + y - jnp.arange(nx)
    origin = jnp.concatenate([(back + 2 * c) % nx, (back + 2 - 2 * c) % nx])
    table = jnp.array([near, far], jnp.int32).T
    places = ((z + jnp.take(table, origin, axis=0)) % nz).reshape(-1).astype(jnp.int32)

    p_piece = lax.dynamic_slice(proj_weight, (0, c * half_d), (k_shard, half_d))
    h_piece = jnp.concatenate(
        [
            lax.dynamic_slice(head_weight, (0, c * half_v), (d_shard, half_v)),
            jnp.pad(norm_gain.reshape(1, d_shard), ((0, small_rows - 1), (0, half_v - d_shard))),
        ],
        axis=0,
    )
    p_stacks = spread(fetch(p_piece))
    p_stacks = p_stacks + swap_all(p_stacks)
    h_stacks = spread(fetch(h_piece))

    rows = thinker_rows.reshape(count, tw)

    def project(skip, stacks):
        return pl.pallas_call(
            functools.partial(project_kernel, block, skip),
            out_shape=shape((count, half_d), bf16),
            in_specs=[SMEM, VMEM] + [ANY] * nx,
            out_specs=VMEM,
            scratch_shapes=[pltpu.VMEM((tw, half_d), bf16), pltpu.SemaphoreType.DMA((2 * nx,))],
            cost_estimate=cost(2 * count * tw * half_d, 6 << 20),
            compiler_params=limit(12),
            name="project",
        )(places, rows, *stacks)

    half_own = project(0, p_stacks[:nx])
    half_oth = project(nx, p_stacks[nx:])
    h_stacks = h_stacks + swap_all(h_stacks)

    near_half = pl.pallas_call(
        functools.partial(near_kernel, frames),
        out_shape=(
            shape((count, half_v), f32),
            shape((count, width), bf16),
            shape((width, count), bf16),
            shape((count, width), bf16),
        ),
        in_specs=[SMEM, SMEM, VMEM, VMEM] + [ANY] * nx,
        out_specs=(VMEM,) * 4,
        scratch_shapes=[
            pltpu.VMEM((width, half_v), bf16),
            pltpu.VMEM((nz, small_rows, d_shard), bf16),
            pltpu.SemaphoreType.DMA((2 * nx,)),
            pltpu.SemaphoreType.DMA((2 * nx,)),
        ],
        cost_estimate=cost(2 * count * width * half_v, 6 << 20),
        compiler_params=limit(20),
        name="near",
    )
    logits, normed, turned, kept = near_half(places, core, half_own, half_oth, *h_stacks[:nx])
    turned_par = lax.ppermute(turned, "wide", core_swap())
    far_half = pl.pallas_call(
        functools.partial(far_kernel, frames),
        out_shape=(
            shape((count, half_v), bf16),
            shape((count, half_v), bf16),
            shape((1, 1), f32),
        ),
        in_specs=[SMEM] * 6 + [VMEM] * 3 + [ANY] * nx,
        out_specs=(VMEM,) * 3,
        scratch_shapes=[
            pltpu.VMEM((width, half_v), bf16),
            pltpu.VMEM((block, half_v), f32),
            pltpu.VMEM((block, half_v), f32),
            pltpu.SemaphoreType.DMA((2 * nx,)),
        ],
        cost_estimate=cost(2 * count * width * half_v, 8 << 20),
        compiler_params=limit(24),
        name="far",
    )
    dl_own, dl_oth, loss = far_half(
        places,
        core,
        block_lengths.reshape(-1),
        chosen_label.reshape(-1),
        ref_logratio.reshape(-1),
        pair_count.reshape(-1),
        logits,
        normed,
        codec_ids.reshape(count, 1),
        *h_stacks[nx:],
    )
    dl_par = lax.ppermute(dl_oth, "wide", core_swap())
    mine = pl.pallas_call(
        own_kernel,
        out_shape=shape((nx, width, part), f32),
        grid=(nx,),
        in_specs=[SMEM, VMEM, VMEM],
        out_specs=pl.BlockSpec((None, width, part), lambda j: (j, 0, 0)),
        compiler_params=limit(20),
        cost_estimate=cost(2 * count * width * half_v, 8 << 20),
        name="own",
    )(core, turned, dl_own)

    def head_term(j):
        outs = ((width, part),) + ((1, part),) * (j > 0)
        return pl.pallas_call(
            functools.partial(head_kernel, j),
            out_shape=tuple(shape(dims, f32) for dims in outs),
            grid=(1,),
            in_specs=[SMEM, pl.BlockSpec((None, width, part), lambda i: (j, 0, 0)), VMEM, VMEM],
            out_specs=tuple(pl.BlockSpec(dims, lambda i: (0, 0)) for dims in outs),
            cost_estimate=cost(2 * count * width * part, 4 << 20),
            compiler_params=limit(16),
            name="head",
        )(core, mine, turned_par, dl_par)

    terms = {j: head_term(j) for j in (2, 1, 3, 0)}
    sent = {
        j: lax.ppermute(
            lax.optimization_barrier(terms[j][0].astype(jnp.float16)), "wide", plane_shift(j, True)
        ).astype(f32)
        for j in (2, 1, 3)
    }
    small = pl.pallas_call(
        functools.partial(gain_kernel, block),
        out_shape=shape((small_rows, part), f32),
        in_specs=[SMEM] + [VMEM] * 7 + [ANY] * (2 * nx),
        out_specs=VMEM,
        scratch_shapes=[
            pltpu.VMEM((width, half_v), bf16),
            pltpu.VMEM((width, half_v), bf16),
            pltpu.VMEM((1, width), f32),
            pltpu.SemaphoreType.DMA((4 * nx,)),
        ],
        cost_estimate=cost(2 * count * width * vocab, 8 << 20),
        compiler_params=limit(24),
        name="gain",
    )(places, dl_own, dl_oth, kept, loss, *(terms[j][1] for j in (1, 2, 3)), *h_stacks)
    s_sent = {j: lax.ppermute(small, "wide", plane_shift(j, True)) for j in (2, 1, 3)}
    coded = (nz, lines + small_rows, part)
    f16 = jnp.float16
    chunks = pl.pallas_call(
        sum_kernel,
        out_shape=tuple(shape(coded, f32) for _ in range(ny)),
        in_specs=[SMEM] + [VMEM] * 8,
        out_specs=(VMEM,) * ny,
        scratch_shapes=[pltpu.VMEM((width, part), f32)],
        cost_estimate=cost(0, 5 << 20),
        compiler_params=limit(24),
        name="fold",
    )(core, terms[0][0], sent[1], sent[2], sent[3], small, s_sent[1], s_sent[2], s_sent[3])
    rounded = [lax.optimization_barrier(chunk.astype(f16)) for chunk in chunks]
    got = [rounded[0]] + [
        lax.ppermute(rounded[j], "wide", plane_shift(j, False)) for j in range(1, ny)
    ]
    second = pl.pallas_call(
        second_kernel,
        out_shape=shape(coded, f32),
        in_specs=[VMEM] * ny,
        out_specs=VMEM,
        scratch_shapes=[pltpu.VMEM((nz, lines, part), f32)],
        cost_estimate=cost(0, 2 << 20),
        compiler_params=limit(8),
        name="second",
    )(*(g.astype(f32) for g in got))
    second = lax.optimization_barrier(second.astype(f16))
    third = lax.all_to_all(second, "narrow", 0, 0, tiled=True).astype(f32)
    piece, rest = pl.pallas_call(
        third_kernel,
        out_shape=(shape((lines, part), bf16), shape((small_rows, d_shard), f32)),
        in_specs=[VMEM],
        out_specs=(VMEM, VMEM),
        cost_estimate=cost(0, 1 << 20),
        compiler_params=limit(8),
        name="third",
    )(third)

    rest_par = lax.ppermute(rest, "wide", core_swap())
    strip_b = jnp.zeros((ny, lines, part), bf16)
    for j in range(ny):
        here = piece if j == 0 else lax.ppermute(piece, "wide", plane_shift(j, False))
        strip_b = lax.dynamic_update_index_in_dim(strip_b, here, (b - j) % ny, 0)
    strip_b = strip_b.reshape(d_shard, part)
    strip = jnp.zeros((d_shard, half_v), bf16)
    for j in range(nx):
        here = strip_b if j == 0 else lax.ppermute(strip_b, "wide", plane_shift(j, True))
        strip = lax.dynamic_update_slice(strip, here, (0, ((a - j) % nx) * part))
    other = lax.ppermute(strip, "wide", core_swap())
    pair_total = lax.axis_size("wide") * nz * ((slots + 1) // 2)
    grad_head, grad_gain, loss_sum = pl.pallas_call(
        functools.partial(last_kernel, 1.0 / pair_total),
        out_shape=(
            shape((d_shard, vocab), f32),
            shape((1, d_shard), f32),
            shape((1, 1), f32),
        ),
        in_specs=[SMEM] + [VMEM] * 4,
        out_specs=(VMEM,) * 3,
        cost_estimate=cost(0, 2 << 20),
        compiler_params=limit(8),
        name="last",
    )(core, strip, other, rest, rest_par)
    return (loss_sum.reshape(()), grad_head, grad_gain.reshape(d_shard))


def solution(mesh):
    in_specs = (
        P("wide", "narrow", None, None, None, None),
        P("wide", "narrow", None, None, None),
        P("wide", "narrow", None, None),
        P("wide", "narrow", None),
        P("wide", "narrow", None),
        P("wide", "narrow"),
        P("narrow", None),
        P("narrow"),
        P("narrow", None),
    )
    out_specs = (P(), P("narrow", None), P("narrow"))
    return jax.shard_map(
        on_device, mesh=mesh, in_specs=in_specs, out_specs=out_specs, check_vma=False
    )
```

```python
import functools

import jax
import jax.numpy as jnp
from jax import lax
from jax.experimental import pallas as pl
from jax.experimental.pallas import tpu as pltpu
from jax.sharding import PartitionSpec as P


norm_eps = 1e-06
margin_scale = 2.0
nx = 4
ny = 4
nz = 8
near = (1, 2, 3, 4)
far = (-1, -2, -3, 0)
small_rows = 8
half_top = 16384.0
log2_e = 1.4426950408889634


def wide_index(x, y, c):
    return ((y % ny) * nx + x % nx) * 2 + c % 2


def core_swap():
    return [
        (wide_index(x, y, c), wide_index(x, y, 1 - c))
        for y in range(ny)
        for x in range(nx)
        for c in range(2)
    ]


def plane_shift(step, first):
    pairs = []
    for y in range(ny):
        for x in range(nx):
            for c in range(2):
                if (c == 0) == first:
                    pairs.append((wide_index(x, y, c), wide_index(x + step, y, c)))
                else:
                    pairs.append((wide_index(x, y, c), wide_index(x, y + step, c)))
    return pairs


def fetch_pairs(distance):
    pairs = []
    for y in range(ny):
        for x in range(nx):
            for c in range(2):
                w = wide_index(x, y, c)
                d = distance[(x + y + 2 * c) % nx]
                pairs.extend((w * nz + (z + d) % nz, w * nz + z) for z in range(nz))
    return pairs


def fetch(piece):
    both = ("wide", "narrow")
    got = []
    for distance in (near, far):
        got.append(lax.ppermute(piece, both, fetch_pairs(distance)))
    return got


def spread(pieces):
    stack = jnp.stack(pieces)
    got = [stack]
    for j in range(1, nx):
        got.append(lax.ppermute(stack, "wide", plane_shift(j, True)))
    return got


def swap_all(stacks):
    got = []
    for stack in stacks:
        got.append(lax.ppermute(stack, "wide", core_swap()))
    return got


def load_pieces(places, stacks, targets, sems, skip=0):
    copies = []
    for i, stack in enumerate(stacks):
        target = targets[i // nx]
        rows = target.shape[0] // nz
        for s in range(2):
            k = 2 * i + s
            at = pl.multiple_of(places[k + 2 * skip] * rows, rows)
            copies.append(
                pltpu.make_async_copy(
                    stack.at[s, pl.ds(0, rows), :], target.at[pl.ds(at, rows), :], sems.at[k]
                )
            )
    for copy in copies:
        copy.start()
    return copies


def project_kernel(block, skip, places, rows, *refs):
    stacks, (projected, weight, sems) = refs[:nx], refs[nx:]
    copies = load_pieces(places, stacks, (weight,), sems, skip)
    for copy in copies:
        copy.wait()

    def step(i, carry):
        here = pl.ds(pl.multiple_of(i * block, block), block)
        projected[here, :] = jnp.dot(
            rows[here, :], weight[...], preferred_element_type=jnp.float32
        ).astype(jnp.bfloat16)
        return carry

    lax.fori_loop(0, rows.shape[0] // block, step, 0)


def near_kernel(frames, places, core, half_own, half_oth, *refs):
    stacks, (logits, normed, turned, kept, h_own), (gains, sems, g_sems) = (
        refs[:nx],
        refs[nx : nx + 5],
        refs[nx + 5 :],
    )
    copies = load_pieces(places, stacks, (h_own,), sems)
    shard = h_own.shape[0] // nz
    for i in range(nx):
        for s in range(2):
            k = 2 * i + s
            copies.append(
                pltpu.make_async_copy(
                    stacks[i].at[s, pl.ds(shard, small_rows), pl.ds(0, shard)],
                    gains.at[places[k]],
                    g_sems.at[k],
                )
            )
            copies[-1].start()
    for copy in copies:
        copy.wait()
    block = 2 * frames
    half = half_own.shape[1]
    at_own = pl.multiple_of(core[0] * half, half)
    at_oth = pl.multiple_of((1 - core[0]) * half, half)
    lines = shard // ny
    gain = jnp.concatenate([gains[z, 0:1, :].astype(jnp.float32) for z in range(nz)], axis=1)

    def pair(p, carry):
        at = pl.multiple_of(p * block, block)
        kept[pl.ds(at, block), pl.ds(at_own, half)] = half_own[pl.ds(at, block), :]
        kept[pl.ds(at, block), pl.ds(at_oth, half)] = half_oth[pl.ds(at, block), :]
        flat = kept[pl.ds(at, block), :].astype(jnp.float32)
        inverse = lax.rsqrt(jnp.mean(flat * flat, axis=1, keepdims=True) + norm_eps)
        value = flat * inverse * gain
        here = value.astype(jnp.bfloat16)
        normed[pl.ds(at, block), :] = here
        logits[pl.ds(at, block), :] = jnp.dot(
            here, h_own[...], preferred_element_type=jnp.float32
        )
        back = value.T.astype(jnp.bfloat16)
        for z in range(nz):
            for b in range(ny):
                turned[pl.ds((b * nz + z) * lines, lines), pl.ds(at, block)] = back[
                    (z * ny + b) * lines : (z * ny + b + 1) * lines, :
                ]
        return carry

    lax.fori_loop(0, half_own.shape[0] // block, pair, 0)


def far_kernel(frames, places, core, lengths, labels, ratios, live, logits, normed, codes, *refs):
    stacks, (dl_own, dl_oth, h_oth, loss), (e_own, e_oth, sems) = (
        refs[:nx],
        refs[nx : nx + 4],
        refs[nx + 4 :],
    )
    copies = load_pieces(places, stacks, (h_oth,), sems, nx)
    loss[...] = jnp.zeros_like(loss)
    for copy in copies:
        copy.wait()
    half = h_oth.shape[1]
    block = 2 * frames

    def pair(p, carry):
        at = pl.multiple_of(p * block, block)
        code = codes[pl.ds(at, block), :]
        l_own = logits[pl.ds(at, block), :]
        l_oth = jnp.dot(
            normed[pl.ds(at, block), :], h_oth[...], preferred_element_type=jnp.float32
        )
        highest = jnp.maximum(
            jnp.max(l_own, axis=1, keepdims=True), jnp.max(l_oth, axis=1, keepdims=True)
        )
        columns = lax.broadcasted_iota(jnp.int32, l_own.shape, 1)
        hit_own = columns == code - core[0] * half
        hit_oth = columns == code - (1 - core[0]) * half
        picked = jnp.sum(jnp.where(hit_own, l_own, 0.0), axis=1, keepdims=True) + jnp.sum(
            jnp.where(hit_oth, l_oth, 0.0), axis=1, keepdims=True
        )
        x_own = jnp.exp(l_own - highest)
        x_oth = jnp.exp(l_oth - highest)
        e_own[...] = x_own
        e_oth[...] = x_oth
        total = jnp.sum(x_own, axis=1, keepdims=True) + jnp.sum(x_oth, axis=1, keepdims=True)
        logp = picked - (highest + jnp.log(total))
        frame = lax.broadcasted_iota(jnp.int32, (block, 1), 0)
        second = frame >= frames
        one = (frame < lengths[2 * p]) & jnp.logical_not(second)
        two = second & (frame - frames < lengths[2 * p + 1])
        length_one = jnp.full((1, 1), lengths[2 * p], jnp.int32).astype(jnp.float32)
        length_two = jnp.full((1, 1), lengths[2 * p + 1], jnp.int32).astype(jnp.float32)
        alive = jnp.full((1, 1), (p < live[0]).astype(jnp.int32), jnp.int32).astype(jnp.float32)
        score_one = jnp.sum(jnp.where(one, logp, 0.0), axis=0, keepdims=True) / length_one
        score_two = jnp.sum(jnp.where(two, logp, 0.0), axis=0, keepdims=True) / length_two
        sign = jnp.full((1, 1), 1 - 2 * labels[p], jnp.int32).astype(jnp.float32)
        margin = margin_scale * (sign * (score_one - score_two) - ratios[p])
        turn = jnp.exp(-jnp.abs(margin))
        loss[...] += alive * (jnp.maximum(-margin, 0.0) + jnp.log1p(turn))
        slope = -alive * jnp.where(margin >= 0.0, turn, 1.0) / (1.0 + turn)
        weight_one = margin_scale * sign * slope / length_one
        weight_two = -(margin_scale * sign * slope) / length_two
        coeff = jnp.where(one, weight_one, jnp.where(two, weight_two, 0.0))
        scale = 1.0 / total
        dl_own[pl.ds(at, block), :] = (
            coeff * (hit_own.astype(jnp.float32) - e_own[...] * scale)
        ).astype(jnp.bfloat16)
        dl_oth[pl.ds(at, block), :] = (
            coeff * (hit_oth.astype(jnp.float32) - e_oth[...] * scale)
        ).astype(jnp.bfloat16)
        return carry

    lax.fori_loop(0, normed.shape[0] // block, pair, 0)


def gain_kernel(
    block, dl_own, dl_oth, h_own, h_oth, projected, loss, u_one, u_two, u_three, small, total
):
    total[...] = jnp.zeros_like(total)
    contract = (((1,), (1,)), ((), ()))

    def step(i, carry):
        at = pl.multiple_of(i * block, block)
        dnormed = lax.dot_general(
            dl_own[pl.ds(at, block), :], h_own[...], contract, preferred_element_type=jnp.float32
        ) + lax.dot_general(
            dl_oth[pl.ds(at, block), :], h_oth[...], contract, preferred_element_type=jnp.float32
        )
        flat = projected[pl.ds(at, block), :].astype(jnp.float32)
        inverse = lax.rsqrt(jnp.mean(flat * flat, axis=1, keepdims=True) + norm_eps)
        total[...] += jnp.sum(dnormed * flat * inverse, axis=0, keepdims=True)
        return carry

    lax.fori_loop(0, dl_own.shape[0] // block, step, 0)
    part = small.shape[1]
    count = total.shape[1] // part
    for k in range(count):
        small[pl.ds(k, 1), :] = total[:, k * part : (k + 1) * part]
    small[pl.ds(count, 1), :] = jnp.broadcast_to(loss[...], (1, part))
    for j, unit in ((1, u_one), (2, u_two), (3, u_three)):
        small[pl.ds(small_rows - nx + j, 1), :] = unit[...]


def own_kernel(core, turned, dl_own, out):
    part = out.shape[1]
    at = pl.multiple_of(lax.rem(core[1] + pl.program_id(0), nx) * part, part)
    out[...] = jnp.dot(
        turned[...], dl_own[:, pl.ds(at, part)], preferred_element_type=jnp.float32
    )


def head_kernel(shift, core, term, turned, dl_par, out, *refs):
    part = out.shape[1]
    at = pl.multiple_of(lax.rem(core[1] + shift, nx) * part, part)
    value = term[...] + jnp.dot(
        turned[...], dl_par[:, pl.ds(at, part)], preferred_element_type=jnp.float32
    )
    out[...] = value
    if not refs:
        return
    largest = jnp.max(jnp.max(jnp.abs(value), axis=0, keepdims=True), axis=1, keepdims=True)
    largest = jnp.maximum(largest, 1e-30)
    refs[0][...] = jnp.broadcast_to(largest / half_top, refs[0].shape)
    out[...] = out[...] * (half_top / largest)


def exponent(largest):
    return jnp.ceil(jnp.log(jnp.maximum(largest, 1e-30)) * log2_e) - 14.0


def power(k):
    return jnp.exp(k * (1.0 / log2_e))


def top(value):
    return jnp.max(jnp.max(jnp.abs(value), axis=0, keepdims=True), axis=1, keepdims=True)


def split(value, width):
    head = value.astype(jnp.bfloat16).astype(jnp.float32)
    rest = (value - head) * 256.0
    wide = (1, width)
    return jnp.concatenate([jnp.broadcast_to(head, wide), jnp.broadcast_to(rest, wide)], axis=1)


def write_coded(out, blocks, scale, k, gains, loss):
    zs, lines, part = out.shape
    lines -= small_rows
    half = part // 2
    k_gain = exponent(functools.reduce(jnp.maximum, [top(g) for g in gains]))
    k_loss = exponent(loss)
    loss_row = split(loss * power(-k_loss), half)
    k_row = jnp.broadcast_to(k, (1, part))
    kk_row = jnp.concatenate(
        [jnp.broadcast_to(k_gain, (1, half)), jnp.broadcast_to(k_loss, (1, half))], axis=1
    )
    unit = power(-k_gain)
    for z in range(zs):
        out[z, pl.ds(0, lines), :] = blocks(z) * scale
        out[z, pl.ds(lines, 1), :] = split(gains[z] * unit, half)
        out[z, pl.ds(lines + 1, 1), :] = loss_row
        out[z, pl.ds(lines + 2, 1), :] = k_row
        out[z, pl.ds(lines + 3, 1), :] = kk_row
        out[z, pl.ds(lines + 4, small_rows - 4), :] = jnp.zeros((small_rows - 4, part), jnp.float32)


def read_coded(ref, z):
    lines = ref.shape[1] - small_rows
    half = ref.shape[2] // 2
    gain = ref[z, pl.ds(lines, 1), :]
    loss = ref[z, pl.ds(lines + 1, 1), :]
    k = ref[z, pl.ds(lines + 2, 1), :][:, :1]
    kk = ref[z, pl.ds(lines + 3, 1), :]
    return (
        power(k),
        (gain[:, :half] + gain[:, half:] * (1.0 / 256.0)) * power(kk[:, :1]),
        (loss[:, :1] + loss[:, half : half + 1] * (1.0 / 256.0)) * power(kk[:, half : half + 1]),
    )


def sum_kernel(core, *refs):
    (term, one, two, three), (s_term, s_one, s_two, s_three) = refs[:4], refs[4:8]
    outs, total = refs[8:-1], refs[-1]
    zs, lines, part = outs[0].shape
    lines -= small_rows
    rows = zs * lines
    half = part // 2
    small = (s_term[...] + s_two[...]) + (s_one[...] + s_three[...])
    first = small_rows - nx
    u_one, u_two, u_three = (
        ref[first + j : first + j + 1, :] for j, ref in ((1, s_one), (2, s_two), (3, s_three))
    )
    value = (term[...] + two[...] * u_two) + (one[...] * u_one + three[...] * u_three)
    total[...] = value
    k = exponent(top(value))
    scale = power(-k)
    gains = [small[z // 2 : z // 2 + 1, z % 2 * half : (z % 2 + 1) * half] for z in range(zs)]
    loss = small[zs // 2 : zs // 2 + 1, :1]
    for j, out in enumerate(outs):
        start = lax.rem(core[2] + j, ny) * rows
        write_coded(
            out,
            lambda z: total[pl.ds(pl.multiple_of(start + z * lines, lines), lines), :],
            scale,
            k,
            gains,
            loss,
        )


def second_kernel(term, one, two, three, out, total):
    zs, lines, _ = out.shape
    lines -= small_rows
    gains, loss, largest = [], None, None
    for z in range(zs):
        (u0, g0, l0), (u1, g1, l1), (u2, g2, l2), (u3, g3, l3) = (
            read_coded(ref, z) for ref in (term, one, two, three)
        )
        here = pl.ds(0, lines)
        value = (term[z, here, :] * u0 + two[z, here, :] * u2) + (
            one[z, here, :] * u1 + three[z, here, :] * u3
        )
        total[z] = value
        largest = top(value) if z == 0 else jnp.maximum(largest, top(value))
        gains.append((g0 + g2) + (g1 + g3))
        if z == 0:
            loss = (l0 + l2) + (l1 + l3)
    k = exponent(largest)
    write_coded(out, lambda z: total[z], power(-k), k, gains, loss)


def third_kernel(got, piece, small):
    zs, lines, part = got.shape
    lines -= small_rows
    half = part // 2
    value = gain = loss = None
    for z in range(zs):
        u, g, l = read_coded(got, z)
        here = got[z, pl.ds(0, lines), :] * u
        value, gain, loss = (here, g, l) if z == 0 else (value + here, gain + g, loss + l)
    piece[...] = value.astype(jnp.bfloat16)
    small[pl.ds(0, 1), :] = gain
    small[pl.ds(1, 1), :] = jnp.broadcast_to(loss, (1, half))
    small[pl.ds(2, small_rows - 2), :] = jnp.zeros((small_rows - 2, half), jnp.float32)


def last_kernel(scale, core, strip, other, small, small_par, head, gain, loss):
    half = strip.shape[1]
    head[:, pl.ds(pl.multiple_of(core[0] * half, half), half)] = strip[...].astype(jnp.float32)
    head[:, pl.ds(pl.multiple_of((1 - core[0]) * half, half), half)] = other[...].astype(
        jnp.float32
    )
    both = small[...] + small_par[...]
    gain[...] = both[0:1, :]
    loss[...] = both[1:2, 0:1] * scale


SMEM = pl.BlockSpec(memory_space=pltpu.SMEM)
VMEM = pl.BlockSpec(memory_space=pltpu.VMEM)
ANY = pl.BlockSpec(memory_space=pl.ANY)


def shape(dims, dtype):
    return jax.ShapeDtypeStruct(dims, dtype)


def limit(mebibytes):
    return pltpu.CompilerParams(vmem_limit_bytes=mebibytes << 20)


def cost(flops, moved):
    return pl.CostEstimate(flops=flops, bytes_accessed=moved, transcendentals=0)


def on_device(
    thinker_rows,
    codec_ids,
    block_lengths,
    chosen_label,
    ref_logratio,
    pair_count,
    proj_weight,
    norm_gain,
    head_weight,
):
    slots = thinker_rows.shape[2]
    frames = thinker_rows.shape[4]
    tw = thinker_rows.shape[5]
    k_shard, width = proj_weight.shape
    d_shard, vocab = head_weight.shape
    half_v = vocab // 2
    half_d = width // 2
    count = slots * 2 * frames
    block = 2 * frames
    part = half_v // nx
    lines = d_shard // ny
    bf16, f32 = jnp.bfloat16, jnp.float32
    w = lax.axis_index("wide")
    z = lax.axis_index("narrow")
    c = w % 2
    x = (w // 2) % nx
    y = w // (2 * nx)
    a = jnp.where(c == 0, x, y)
    b = jnp.where(c == 0, y, x)
    core = jnp.stack([c, a, b]).astype(jnp.int32)
    back = x + y - jnp.arange(nx)
    origin = jnp.concatenate([(back + 2 * c) % nx, (back + 2 - 2 * c) % nx])
    table = jnp.array([near, far], jnp.int32).T
    places = ((z + jnp.take(table, origin, axis=0)) % nz).reshape(-1).astype(jnp.int32)

    p_piece = lax.dynamic_slice(proj_weight, (0, c * half_d), (k_shard, half_d))
    h_piece = jnp.concatenate(
        [
            lax.dynamic_slice(head_weight, (0, c * half_v), (d_shard, half_v)),
            jnp.pad(norm_gain.reshape(1, d_shard), ((0, small_rows - 1), (0, half_v - d_shard))),
        ],
        axis=0,
    )
    p_stacks = spread(fetch(p_piece))
    p_stacks = p_stacks + swap_all(p_stacks)
    h_stacks = spread(fetch(h_piece))

    rows = thinker_rows.reshape(count, tw)

    def project(skip, stacks):
        return pl.pallas_call(
            functools.partial(project_kernel, block, skip),
            out_shape=shape((count, half_d), bf16),
            in_specs=[SMEM, VMEM] + [ANY] * nx,
            out_specs=VMEM,
            scratch_shapes=[pltpu.VMEM((tw, half_d), bf16), pltpu.SemaphoreType.DMA((2 * nx,))],
            cost_estimate=cost(2 * count * tw * half_d, 6 << 20),
            compiler_params=limit(8),
            name="project",
        )(places, rows, *stacks)

    half_own = project(0, p_stacks[:nx])
    half_oth = project(nx, p_stacks[nx:])
    h_stacks = h_stacks + swap_all(h_stacks)

    near_half = pl.pallas_call(
        functools.partial(near_kernel, frames),
        out_shape=(
            shape((count, half_v), f32),
            shape((count, width), bf16),
            shape((width, count), bf16),
            shape((count, width), bf16),
            shape((width, half_v), bf16),
        ),
        in_specs=[SMEM, SMEM, VMEM, VMEM] + [ANY] * nx,
        out_specs=(VMEM,) * 5,
        scratch_shapes=[
            pltpu.VMEM((nz, small_rows, d_shard), bf16),
            pltpu.SemaphoreType.DMA((2 * nx,)),
            pltpu.SemaphoreType.DMA((2 * nx,)),
        ],
        cost_estimate=cost(2 * count * width * half_v, 6 << 20),
        compiler_params=limit(12),
        name="near",
    )
    logits, normed, turned, kept, h_own = near_half(places, core, half_own, half_oth, *h_stacks[:nx])
    turned_par = lax.ppermute(turned, "wide", core_swap())
    far_half = pl.pallas_call(
        functools.partial(far_kernel, frames),
        out_shape=(
            shape((count, half_v), bf16),
            shape((count, half_v), bf16),
            shape((width, half_v), bf16),
            shape((1, 1), f32),
        ),
        in_specs=[SMEM] * 6 + [VMEM] * 3 + [ANY] * nx,
        out_specs=(VMEM,) * 4,
        scratch_shapes=[
            pltpu.VMEM((block, half_v), f32),
            pltpu.VMEM((block, half_v), f32),
            pltpu.SemaphoreType.DMA((2 * nx,)),
        ],
        cost_estimate=cost(2 * count * width * half_v, 8 << 20),
        compiler_params=limit(14),
        name="far",
    )
    dl_own, dl_oth, h_oth, loss = far_half(
        places,
        core,
        block_lengths.reshape(-1),
        chosen_label.reshape(-1),
        ref_logratio.reshape(-1),
        pair_count.reshape(-1),
        logits,
        normed,
        codec_ids.reshape(count, 1),
        *h_stacks[nx:],
    )
    dl_par = lax.ppermute(dl_oth, "wide", core_swap())
    mine = pl.pallas_call(
        own_kernel,
        out_shape=shape((nx, width, part), f32),
        grid=(nx,),
        in_specs=[SMEM, VMEM, VMEM],
        out_specs=pl.BlockSpec((None, width, part), lambda j: (j, 0, 0)),
        compiler_params=limit(12),
        cost_estimate=cost(2 * count * width * half_v, 8 << 20),
        name="own",
    )(core, turned, dl_own)

    def head_term(j):
        outs = ((width, part),) + ((1, part),) * (j > 0)
        return pl.pallas_call(
            functools.partial(head_kernel, j),
            out_shape=tuple(shape(dims, f32) for dims in outs),
            grid=(1,),
            in_specs=[SMEM, pl.BlockSpec((None, width, part), lambda i: (j, 0, 0)), VMEM, VMEM],
            out_specs=tuple(pl.BlockSpec(dims, lambda i: (0, 0)) for dims in outs),
            cost_estimate=cost(2 * count * width * part, 4 << 20),
            compiler_params=limit(8),
            name="head",
        )(core, mine, turned_par, dl_par)

    terms = {j: head_term(j) for j in (2, 1, 3, 0)}
    sent = {
        j: lax.ppermute(
            lax.optimization_barrier(terms[j][0].astype(jnp.float16)), "wide", plane_shift(j, True)
        ).astype(f32)
        for j in (2, 1, 3)
    }
    small = pl.pallas_call(
        functools.partial(gain_kernel, block),
        out_shape=shape((small_rows, part), f32),
        in_specs=[VMEM] * 9,
        out_specs=VMEM,
        scratch_shapes=[pltpu.VMEM((1, width), f32)],
        cost_estimate=cost(2 * count * width * vocab, 8 << 20),
        compiler_params=limit(14),
        name="gain",
    )(dl_own, dl_oth, h_own, h_oth, kept, loss, *(terms[j][1] for j in (1, 2, 3)))
    s_sent = {j: lax.ppermute(small, "wide", plane_shift(j, True)) for j in (2, 1, 3)}
    coded = (nz, lines + small_rows, part)
    f16 = jnp.float16
    chunks = pl.pallas_call(
        sum_kernel,
        out_shape=tuple(shape(coded, f32) for _ in range(ny)),
        in_specs=[SMEM] + [VMEM] * 8,
        out_specs=(VMEM,) * ny,
        scratch_shapes=[pltpu.VMEM((width, part), f32)],
        cost_estimate=cost(0, 5 << 20),
        compiler_params=limit(14),
        name="fold",
    )(core, terms[0][0], sent[1], sent[2], sent[3], small, s_sent[1], s_sent[2], s_sent[3])
    rounded = [lax.optimization_barrier(chunk.astype(f16)) for chunk in chunks]
    got = [rounded[0]] + [
        lax.ppermute(rounded[j], "wide", plane_shift(j, False)) for j in range(1, ny)
    ]
    second = pl.pallas_call(
        second_kernel,
        out_shape=shape(coded, f32),
        in_specs=[VMEM] * ny,
        out_specs=VMEM,
        scratch_shapes=[pltpu.VMEM((nz, lines, part), f32)],
        cost_estimate=cost(0, 2 << 20),
        compiler_params=limit(6),
        name="second",
    )(*(g.astype(f32) for g in got))
    second = lax.optimization_barrier(second.astype(f16))
    third = lax.all_to_all(second, "narrow", 0, 0, tiled=True).astype(f32)
    piece, rest = pl.pallas_call(
        third_kernel,
        out_shape=(shape((lines, part), bf16), shape((small_rows, d_shard), f32)),
        in_specs=[VMEM],
        out_specs=(VMEM, VMEM),
        cost_estimate=cost(0, 1 << 20),
        compiler_params=limit(4),
        name="third",
    )(third)

    rest_par = lax.ppermute(rest, "wide", core_swap())
    strip_b = jnp.zeros((ny, lines, part), bf16)
    for j in range(ny):
        here = piece if j == 0 else lax.ppermute(piece, "wide", plane_shift(j, False))
        strip_b = lax.dynamic_update_index_in_dim(strip_b, here, (b - j) % ny, 0)
    strip_b = strip_b.reshape(d_shard, part)
    strip = jnp.zeros((d_shard, half_v), bf16)
    for j in range(nx):
        here = strip_b if j == 0 else lax.ppermute(strip_b, "wide", plane_shift(j, True))
        strip = lax.dynamic_update_slice(strip, here, (0, ((a - j) % nx) * part))
    other = lax.ppermute(strip, "wide", core_swap())
    pair_total = lax.axis_size("wide") * nz * ((slots + 1) // 2)
    grad_head, grad_gain, loss_sum = pl.pallas_call(
        functools.partial(last_kernel, 1.0 / pair_total),
        out_shape=(
            shape((d_shard, vocab), f32),
            shape((1, d_shard), f32),
            shape((1, 1), f32),
        ),
        in_specs=[SMEM] + [VMEM] * 4,
        out_specs=(VMEM,) * 3,
        cost_estimate=cost(0, 2 << 20),
        compiler_params=limit(6),
        name="last",
    )(core, strip, other, rest, rest_par)
    return (loss_sum.reshape(()), grad_head, grad_gain.reshape(d_shard))


def solution(mesh):
    in_specs = (
        P("wide", "narrow", None, None, None, None),
        P("wide", "narrow", None, None, None),
        P("wide", "narrow", None, None),
        P("wide", "narrow", None),
        P("wide", "narrow", None),
        P("wide", "narrow"),
        P("narrow", None),
        P("narrow"),
        P("narrow", None),
    )
    out_specs = (P(), P("narrow", None), P("narrow"))
    return jax.shard_map(
        on_device, mesh=mesh, in_specs=in_specs, out_specs=out_specs, check_vma=False
    )
```

```python
import functools

import jax
import jax.numpy as jnp
from jax import lax
from jax.experimental import pallas as pl
from jax.experimental.pallas import tpu as pltpu
from jax.sharding import PartitionSpec as P


norm_eps = 1e-06
margin_scale = 2.0
nx = 4
ny = 4
nz = 8
near = (1, 2, 3, 4)
far = (-1, -2, -3, 0)
small_rows = 8
half_top = 16384.0
log2_e = 1.4426950408889634


def wide_index(x, y, c):
    return ((y % ny) * nx + x % nx) * 2 + c % 2


def core_swap():
    return [
        (wide_index(x, y, c), wide_index(x, y, 1 - c))
        for y in range(ny)
        for x in range(nx)
        for c in range(2)
    ]


def plane_shift(step, first):
    pairs = []
    for y in range(ny):
        for x in range(nx):
            for c in range(2):
                if (c == 0) == first:
                    pairs.append((wide_index(x, y, c), wide_index(x + step, y, c)))
                else:
                    pairs.append((wide_index(x, y, c), wide_index(x, y + step, c)))
    return pairs


def fetch_pairs(distance):
    pairs = []
    for y in range(ny):
        for x in range(nx):
            for c in range(2):
                w = wide_index(x, y, c)
                d = distance[(x + y + 2 * c) % nx]
                pairs.extend((w * nz + (z + d) % nz, w * nz + z) for z in range(nz))
    return pairs


def fetch(piece):
    both = ("wide", "narrow")
    got = []
    for distance in (near, far):
        got.append(lax.ppermute(piece, both, fetch_pairs(distance)))
    return got


def spread(pieces):
    stack = jnp.stack(pieces)
    got = [stack]
    for j in range(1, nx):
        got.append(lax.ppermute(stack, "wide", plane_shift(j, True)))
    return got


def swap_all(stacks):
    got = []
    for stack in stacks:
        got.append(lax.ppermute(stack, "wide", core_swap()))
    return got


def load_pieces(places, stacks, targets, sems, skip=0):
    copies = []
    for i, stack in enumerate(stacks):
        target = targets[i // nx]
        rows = target.shape[0] // nz
        for s in range(2):
            k = 2 * i + s
            at = pl.multiple_of(places[k + 2 * skip] * rows, rows)
            copies.append(
                pltpu.make_async_copy(
                    stack.at[s, pl.ds(0, rows), :], target.at[pl.ds(at, rows), :], sems.at[k]
                )
            )
    for copy in copies:
        copy.start()
    return copies


def project_kernel(block, skip, places, rows, *refs):
    stacks, (projected, weight, sems) = refs[:nx], refs[nx:]
    copies = load_pieces(places, stacks, (weight,), sems, skip)
    for copy in copies:
        copy.wait()

    def step(i, carry):
        here = pl.ds(pl.multiple_of(i * block, block), block)
        projected[here, :] = jnp.dot(
            rows[here, :], weight[...], preferred_element_type=jnp.float32
        ).astype(jnp.bfloat16)
        return carry

    lax.fori_loop(0, rows.shape[0] // block, step, 0)


def near_kernel(frames, places, core, half_own, half_oth, *refs):
    stacks, (logits, normed, turned, kept, h_own), (gains, sems, g_sems) = (
        refs[:nx],
        refs[nx : nx + 5],
        refs[nx + 5 :],
    )
    copies = load_pieces(places, stacks, (h_own,), sems)
    shard = h_own.shape[0] // nz
    for i in range(nx):
        for s in range(2):
            k = 2 * i + s
            copies.append(
                pltpu.make_async_copy(
                    stacks[i].at[s, pl.ds(shard, small_rows), pl.ds(0, shard)],
                    gains.at[places[k]],
                    g_sems.at[k],
                )
            )
            copies[-1].start()
    for copy in copies:
        copy.wait()
    block = 2 * frames
    half = half_own.shape[1]
    at_own = pl.multiple_of(core[0] * half, half)
    at_oth = pl.multiple_of((1 - core[0]) * half, half)
    lines = shard // ny
    gain = jnp.concatenate([gains[z, 0:1, :].astype(jnp.float32) for z in range(nz)], axis=1)

    def pair(p, carry):
        at = pl.multiple_of(p * block, block)
        kept[pl.ds(at, block), pl.ds(at_own, half)] = half_own[pl.ds(at, block), :]
        kept[pl.ds(at, block), pl.ds(at_oth, half)] = half_oth[pl.ds(at, block), :]
        flat = kept[pl.ds(at, block), :].astype(jnp.float32)
        inverse = lax.rsqrt(jnp.mean(flat * flat, axis=1, keepdims=True) + norm_eps)
        value = flat * inverse * gain
        here = value.astype(jnp.bfloat16)
        normed[pl.ds(at, block), :] = here
        logits[pl.ds(at, block), :] = jnp.dot(
            here, h_own[...], preferred_element_type=jnp.float32
        )
        back = value.T.astype(jnp.bfloat16)
        for z in range(nz):
            for b in range(ny):
                turned[pl.ds((b * nz + z) * lines, lines), pl.ds(at, block)] = back[
                    (z * ny + b) * lines : (z * ny + b + 1) * lines, :
                ]
        return carry

    lax.fori_loop(0, half_own.shape[0] // block, pair, 0)


def far_kernel(frames, places, core, lengths, labels, ratios, live, logits, normed, codes, *refs):
    stacks, (dl_own, dl_oth, h_oth, loss), (e_own, e_oth, near_top, near_pick, sems) = (
        refs[:nx],
        refs[nx : nx + 4],
        refs[nx + 4 :],
    )
    copies = load_pieces(places, stacks, (h_oth,), sems, nx)
    loss[...] = jnp.zeros_like(loss)
    half = h_oth.shape[1]
    block = 2 * frames

    def near(p, carry):
        here = pl.ds(pl.multiple_of(p * block, block), block)
        l_own = logits[here, :]
        near_top[here, :] = jnp.max(l_own, axis=1, keepdims=True)
        hit_own = (
            lax.broadcasted_iota(jnp.int32, l_own.shape, 1) == codes[here, :] - core[0] * half
        )
        near_pick[here, :] = jnp.sum(jnp.where(hit_own, l_own, 0.0), axis=1, keepdims=True)
        return carry

    lax.fori_loop(0, normed.shape[0] // block, near, 0)
    for copy in copies:
        copy.wait()

    def pair(p, carry):
        at = pl.multiple_of(p * block, block)
        code = codes[pl.ds(at, block), :]
        l_own = logits[pl.ds(at, block), :]
        l_oth = jnp.dot(
            normed[pl.ds(at, block), :], h_oth[...], preferred_element_type=jnp.float32
        )
        highest = jnp.maximum(near_top[pl.ds(at, block), :], jnp.max(l_oth, axis=1, keepdims=True))
        columns = lax.broadcasted_iota(jnp.int32, l_own.shape, 1)
        hit_own = columns == code - core[0] * half
        hit_oth = columns == code - (1 - core[0]) * half
        picked = near_pick[pl.ds(at, block), :] + jnp.sum(
            jnp.where(hit_oth, l_oth, 0.0), axis=1, keepdims=True
        )
        x_own = jnp.exp(l_own - highest)
        x_oth = jnp.exp(l_oth - highest)
        e_own[...] = x_own
        e_oth[...] = x_oth
        total = jnp.sum(x_own, axis=1, keepdims=True) + jnp.sum(x_oth, axis=1, keepdims=True)
        logp = picked - (highest + jnp.log(total))
        frame = lax.broadcasted_iota(jnp.int32, (block, 1), 0)
        second = frame >= frames
        one = (frame < lengths[2 * p]) & jnp.logical_not(second)
        two = second & (frame - frames < lengths[2 * p + 1])
        length_one = jnp.full((1, 1), lengths[2 * p], jnp.int32).astype(jnp.float32)
        length_two = jnp.full((1, 1), lengths[2 * p + 1], jnp.int32).astype(jnp.float32)
        alive = jnp.full((1, 1), (p < live[0]).astype(jnp.int32), jnp.int32).astype(jnp.float32)
        score_one = jnp.sum(jnp.where(one, logp, 0.0), axis=0, keepdims=True) / length_one
        score_two = jnp.sum(jnp.where(two, logp, 0.0), axis=0, keepdims=True) / length_two
        sign = jnp.full((1, 1), 1 - 2 * labels[p], jnp.int32).astype(jnp.float32)
        margin = margin_scale * (sign * (score_one - score_two) - ratios[p])
        turn = jnp.exp(-jnp.abs(margin))
        loss[...] += alive * (jnp.maximum(-margin, 0.0) + jnp.log1p(turn))
        slope = -alive * jnp.where(margin >= 0.0, turn, 1.0) / (1.0 + turn)
        weight_one = margin_scale * sign * slope / length_one
        weight_two = -(margin_scale * sign * slope) / length_two
        coeff = jnp.where(one, weight_one, jnp.where(two, weight_two, 0.0))
        scale = 1.0 / total
        dl_own[pl.ds(at, block), :] = (
            coeff * (hit_own.astype(jnp.float32) - e_own[...] * scale)
        ).astype(jnp.bfloat16)
        dl_oth[pl.ds(at, block), :] = (
            coeff * (hit_oth.astype(jnp.float32) - e_oth[...] * scale)
        ).astype(jnp.bfloat16)
        return carry

    lax.fori_loop(0, normed.shape[0] // block, pair, 0)


def gain_kernel(
    block, dl_own, dl_oth, h_own, h_oth, projected, loss, u_one, u_two, u_three, small, total
):
    total[...] = jnp.zeros_like(total)
    contract = (((1,), (1,)), ((), ()))

    def step(i, carry):
        at = pl.multiple_of(i * block, block)
        dnormed = lax.dot_general(
            dl_own[pl.ds(at, block), :], h_own[...], contract, preferred_element_type=jnp.float32
        ) + lax.dot_general(
            dl_oth[pl.ds(at, block), :], h_oth[...], contract, preferred_element_type=jnp.float32
        )
        flat = projected[pl.ds(at, block), :].astype(jnp.float32)
        inverse = lax.rsqrt(jnp.mean(flat * flat, axis=1, keepdims=True) + norm_eps)
        total[...] += jnp.sum(dnormed * flat * inverse, axis=0, keepdims=True)
        return carry

    lax.fori_loop(0, dl_own.shape[0] // block, step, 0)
    part = small.shape[1]
    count = total.shape[1] // part
    for k in range(count):
        small[pl.ds(k, 1), :] = total[:, k * part : (k + 1) * part]
    small[pl.ds(count, 1), :] = jnp.broadcast_to(loss[...], (1, part))
    for j, unit in ((1, u_one), (2, u_two), (3, u_three)):
        small[pl.ds(small_rows - nx + j, 1), :] = unit[...]


def own_kernel(core, turned, dl_own, out):
    part = out.shape[1]
    at = pl.multiple_of(lax.rem(core[1] + pl.program_id(0), nx) * part, part)
    out[...] = jnp.dot(
        turned[...], dl_own[:, pl.ds(at, part)], preferred_element_type=jnp.float32
    )


def head_kernel(shift, core, term, turned, dl_par, out, *refs):
    part = out.shape[1]
    at = pl.multiple_of(lax.rem(core[1] + shift, nx) * part, part)
    value = term[...] + jnp.dot(
        turned[...], dl_par[:, pl.ds(at, part)], preferred_element_type=jnp.float32
    )
    out[...] = value
    if not refs:
        return
    largest = jnp.max(jnp.max(jnp.abs(value), axis=0, keepdims=True), axis=1, keepdims=True)
    largest = jnp.maximum(largest, 1e-30)
    refs[0][...] = jnp.broadcast_to(largest / half_top, refs[0].shape)
    out[...] = out[...] * (half_top / largest)


def exponent(largest):
    return jnp.ceil(jnp.log(jnp.maximum(largest, 1e-30)) * log2_e) - 14.0


def power(k):
    return jnp.exp(k * (1.0 / log2_e))


def top(value):
    return jnp.max(jnp.max(jnp.abs(value), axis=0, keepdims=True), axis=1, keepdims=True)


def split(value, width):
    head = value.astype(jnp.bfloat16).astype(jnp.float32)
    rest = (value - head) * 256.0
    wide = (1, width)
    return jnp.concatenate([jnp.broadcast_to(head, wide), jnp.broadcast_to(rest, wide)], axis=1)


def write_coded(out, blocks, scale, k, gains, loss):
    zs, lines, part = out.shape
    lines -= small_rows
    half = part // 2
    k_gain = exponent(functools.reduce(jnp.maximum, [top(g) for g in gains]))
    k_loss = exponent(loss)
    loss_row = split(loss * power(-k_loss), half)
    k_row = jnp.broadcast_to(k, (1, part))
    kk_row = jnp.concatenate(
        [jnp.broadcast_to(k_gain, (1, half)), jnp.broadcast_to(k_loss, (1, half))], axis=1
    )
    unit = power(-k_gain)
    for z in range(zs):
        out[z, pl.ds(0, lines), :] = blocks(z) * scale
        out[z, pl.ds(lines, 1), :] = split(gains[z] * unit, half)
        out[z, pl.ds(lines + 1, 1), :] = loss_row
        out[z, pl.ds(lines + 2, 1), :] = k_row
        out[z, pl.ds(lines + 3, 1), :] = kk_row
        out[z, pl.ds(lines + 4, small_rows - 4), :] = jnp.zeros((small_rows - 4, part), jnp.float32)


def read_coded(ref, z):
    lines = ref.shape[1] - small_rows
    half = ref.shape[2] // 2
    gain = ref[z, pl.ds(lines, 1), :]
    loss = ref[z, pl.ds(lines + 1, 1), :]
    k = ref[z, pl.ds(lines + 2, 1), :][:, :1]
    kk = ref[z, pl.ds(lines + 3, 1), :]
    return (
        power(k),
        (gain[:, :half] + gain[:, half:] * (1.0 / 256.0)) * power(kk[:, :1]),
        (loss[:, :1] + loss[:, half : half + 1] * (1.0 / 256.0)) * power(kk[:, half : half + 1]),
    )


def sum_kernel(core, *refs):
    (term, one, two, three), (s_term, s_one, s_two, s_three) = refs[:4], refs[4:8]
    outs, total = refs[8:-1], refs[-1]
    zs, lines, part = outs[0].shape
    lines -= small_rows
    rows = zs * lines
    half = part // 2
    small = (s_term[...] + s_two[...]) + (s_one[...] + s_three[...])
    first = small_rows - nx
    u_one, u_two, u_three = (
        ref[first + j : first + j + 1, :] for j, ref in ((1, s_one), (2, s_two), (3, s_three))
    )
    value = (term[...] + two[...] * u_two) + (one[...] * u_one + three[...] * u_three)
    total[...] = value
    k = exponent(top(value))
    scale = power(-k)
    gains = [small[z // 2 : z // 2 + 1, z % 2 * half : (z % 2 + 1) * half] for z in range(zs)]
    loss = small[zs // 2 : zs // 2 + 1, :1]
    for j, out in enumerate(outs):
        start = lax.rem(core[2] + j, ny) * rows
        write_coded(
            out,
            lambda z: total[pl.ds(pl.multiple_of(start + z * lines, lines), lines), :],
            scale,
            k,
            gains,
            loss,
        )


def second_kernel(term, one, two, three, out, total):
    zs, lines, _ = out.shape
    lines -= small_rows
    gains, loss, largest = [], None, None
    for z in range(zs):
        (u0, g0, l0), (u1, g1, l1), (u2, g2, l2), (u3, g3, l3) = (
            read_coded(ref, z) for ref in (term, one, two, three)
        )
        here = pl.ds(0, lines)
        value = (term[z, here, :] * u0 + two[z, here, :] * u2) + (
            one[z, here, :] * u1 + three[z, here, :] * u3
        )
        total[z] = value
        largest = top(value) if z == 0 else jnp.maximum(largest, top(value))
        gains.append((g0 + g2) + (g1 + g3))
        if z == 0:
            loss = (l0 + l2) + (l1 + l3)
    k = exponent(largest)
    write_coded(out, lambda z: total[z], power(-k), k, gains, loss)


def third_kernel(got, piece, small):
    zs, lines, part = got.shape
    lines -= small_rows
    half = part // 2
    value = gain = loss = None
    for z in range(zs):
        u, g, l = read_coded(got, z)
        here = got[z, pl.ds(0, lines), :] * u
        value, gain, loss = (here, g, l) if z == 0 else (value + here, gain + g, loss + l)
    piece[...] = value.astype(jnp.bfloat16)
    small[pl.ds(0, 1), :] = gain
    small[pl.ds(1, 1), :] = jnp.broadcast_to(loss, (1, half))
    small[pl.ds(2, small_rows - 2), :] = jnp.zeros((small_rows - 2, half), jnp.float32)


def last_kernel(scale, core, strip, other, small, small_par, head, gain, loss):
    half = strip.shape[1]
    head[:, pl.ds(pl.multiple_of(core[0] * half, half), half)] = strip[...].astype(jnp.float32)
    head[:, pl.ds(pl.multiple_of((1 - core[0]) * half, half), half)] = other[...].astype(
        jnp.float32
    )
    both = small[...] + small_par[...]
    gain[...] = both[0:1, :]
    loss[...] = both[1:2, 0:1] * scale


SMEM = pl.BlockSpec(memory_space=pltpu.SMEM)
VMEM = pl.BlockSpec(memory_space=pltpu.VMEM)
ANY = pl.BlockSpec(memory_space=pl.ANY)


def shape(dims, dtype):
    return jax.ShapeDtypeStruct(dims, dtype)


def limit(mebibytes):
    return pltpu.CompilerParams(vmem_limit_bytes=mebibytes << 20)


def cost(flops, moved):
    return pl.CostEstimate(flops=flops, bytes_accessed=moved, transcendentals=0)


def on_device(
    thinker_rows,
    codec_ids,
    block_lengths,
    chosen_label,
    ref_logratio,
    pair_count,
    proj_weight,
    norm_gain,
    head_weight,
):
    slots = thinker_rows.shape[2]
    frames = thinker_rows.shape[4]
    tw = thinker_rows.shape[5]
    k_shard, width = proj_weight.shape
    d_shard, vocab = head_weight.shape
    half_v = vocab // 2
    half_d = width // 2
    count = slots * 2 * frames
    block = 2 * frames
    part = half_v // nx
    lines = d_shard // ny
    bf16, f32 = jnp.bfloat16, jnp.float32
    w = lax.axis_index("wide")
    z = lax.axis_index("narrow")
    c = w % 2
    x = (w // 2) % nx
    y = w // (2 * nx)
    a = jnp.where(c == 0, x, y)
    b = jnp.where(c == 0, y, x)
    core = jnp.stack([c, a, b]).astype(jnp.int32)
    back = x + y - jnp.arange(nx)
    origin = jnp.concatenate([(back + 2 * c) % nx, (back + 2 - 2 * c) % nx])
    table = jnp.array([near, far], jnp.int32).T
    places = ((z + jnp.take(table, origin, axis=0)) % nz).reshape(-1).astype(jnp.int32)

    p_piece = lax.dynamic_slice(proj_weight, (0, c * half_d), (k_shard, half_d))
    h_piece = jnp.concatenate(
        [
            lax.dynamic_slice(head_weight, (0, c * half_v), (d_shard, half_v)),
            jnp.pad(norm_gain.reshape(1, d_shard), ((0, small_rows - 1), (0, half_v - d_shard))),
        ],
        axis=0,
    )
    p_stacks = spread(fetch(p_piece))
    p_stacks = p_stacks + swap_all(p_stacks)
    h_stacks = spread(fetch(h_piece))

    rows = thinker_rows.reshape(count, tw)

    def project(skip, stacks):
        return pl.pallas_call(
            functools.partial(project_kernel, block, skip),
            out_shape=shape((count, half_d), bf16),
            in_specs=[SMEM, VMEM] + [ANY] * nx,
            out_specs=VMEM,
            scratch_shapes=[pltpu.VMEM((tw, half_d), bf16), pltpu.SemaphoreType.DMA((2 * nx,))],
            cost_estimate=cost(2 * count * tw * half_d, 6 << 20),
            compiler_params=limit(8),
            name="project",
        )(places, rows, *stacks)

    half_own = project(0, p_stacks[:nx])
    half_oth = project(nx, p_stacks[nx:])
    h_stacks = h_stacks + swap_all(h_stacks)

    near_half = pl.pallas_call(
        functools.partial(near_kernel, frames),
        out_shape=(
            shape((count, half_v), f32),
            shape((count, width), bf16),
            shape((width, count), bf16),
            shape((count, width), bf16),
            shape((width, half_v), bf16),
        ),
        in_specs=[SMEM, SMEM, VMEM, VMEM] + [ANY] * nx,
        out_specs=(VMEM,) * 5,
        scratch_shapes=[
            pltpu.VMEM((nz, small_rows, d_shard), bf16),
            pltpu.SemaphoreType.DMA((2 * nx,)),
            pltpu.SemaphoreType.DMA((2 * nx,)),
        ],
        cost_estimate=cost(2 * count * width * half_v, 6 << 20),
        compiler_params=limit(12),
        name="near",
    )
    logits, normed, turned, kept, h_own = near_half(places, core, half_own, half_oth, *h_stacks[:nx])
    turned_par = lax.ppermute(turned, "wide", core_swap())
    far_half = pl.pallas_call(
        functools.partial(far_kernel, frames),
        out_shape=(
            shape((count, half_v), bf16),
            shape((count, half_v), bf16),
            shape((width, half_v), bf16),
            shape((1, 1), f32),
        ),
        in_specs=[SMEM] * 6 + [VMEM] * 3 + [ANY] * nx,
        out_specs=(VMEM,) * 4,
        scratch_shapes=[
            pltpu.VMEM((block, half_v), f32),
            pltpu.VMEM((block, half_v), f32),
            pltpu.VMEM((count, 1), f32),
            pltpu.VMEM((count, 1), f32),
            pltpu.SemaphoreType.DMA((2 * nx,)),
        ],
        cost_estimate=cost(2 * count * width * half_v, 8 << 20),
        compiler_params=limit(14),
        name="far",
    )
    dl_own, dl_oth, h_oth, loss = far_half(
        places,
        core,
        block_lengths.reshape(-1),
        chosen_label.reshape(-1),
        ref_logratio.reshape(-1),
        pair_count.reshape(-1),
        logits,
        normed,
        codec_ids.reshape(count, 1),
        *h_stacks[nx:],
    )
    dl_par = lax.ppermute(dl_oth, "wide", core_swap())
    mine = pl.pallas_call(
        own_kernel,
        out_shape=shape((nx, width, part), f32),
        grid=(nx,),
        in_specs=[SMEM, VMEM, VMEM],
        out_specs=pl.BlockSpec((None, width, part), lambda j: (j, 0, 0)),
        compiler_params=limit(12),
        cost_estimate=cost(2 * count * width * half_v, 8 << 20),
        name="own",
    )(core, turned, dl_own)

    def head_term(j):
        outs = ((width, part),) + ((1, part),) * (j > 0)
        return pl.pallas_call(
            functools.partial(head_kernel, j),
            out_shape=tuple(shape(dims, f32) for dims in outs),
            grid=(1,),
            in_specs=[SMEM, pl.BlockSpec((None, width, part), lambda i: (j, 0, 0)), VMEM, VMEM],
            out_specs=tuple(pl.BlockSpec(dims, lambda i: (0, 0)) for dims in outs),
            cost_estimate=cost(2 * count * width * part, 4 << 20),
            compiler_params=limit(8),
            name="head",
        )(core, mine, turned_par, dl_par)

    terms = {j: head_term(j) for j in (2, 1, 3, 0)}
    sent = {
        j: lax.ppermute(
            lax.optimization_barrier(terms[j][0].astype(jnp.float16)), "wide", plane_shift(j, True)
        ).astype(f32)
        for j in (2, 1, 3)
    }
    small = pl.pallas_call(
        functools.partial(gain_kernel, block),
        out_shape=shape((small_rows, part), f32),
        in_specs=[VMEM] * 9,
        out_specs=VMEM,
        scratch_shapes=[pltpu.VMEM((1, width), f32)],
        cost_estimate=cost(2 * count * width * vocab, 8 << 20),
        compiler_params=limit(14),
        name="gain",
    )(dl_own, dl_oth, h_own, h_oth, kept, loss, *(terms[j][1] for j in (1, 2, 3)))
    s_sent = {j: lax.ppermute(small, "wide", plane_shift(j, True)) for j in (2, 1, 3)}
    coded = (nz, lines + small_rows, part)
    f16 = jnp.float16
    chunks = pl.pallas_call(
        sum_kernel,
        out_shape=tuple(shape(coded, f32) for _ in range(ny)),
        in_specs=[SMEM] + [VMEM] * 8,
        out_specs=(VMEM,) * ny,
        scratch_shapes=[pltpu.VMEM((width, part), f32)],
        cost_estimate=cost(0, 5 << 20),
        compiler_params=limit(14),
        name="fold",
    )(core, terms[0][0], sent[1], sent[2], sent[3], small, s_sent[1], s_sent[2], s_sent[3])
    rounded = [lax.optimization_barrier(chunk.astype(f16)) for chunk in chunks]
    got = [rounded[0]] + [
        lax.ppermute(rounded[j], "wide", plane_shift(j, False)) for j in range(1, ny)
    ]
    second = pl.pallas_call(
        second_kernel,
        out_shape=shape(coded, f32),
        in_specs=[VMEM] * ny,
        out_specs=VMEM,
        scratch_shapes=[pltpu.VMEM((nz, lines, part), f32)],
        cost_estimate=cost(0, 2 << 20),
        compiler_params=limit(6),
        name="second",
    )(*(g.astype(f32) for g in got))
    second = lax.optimization_barrier(second.astype(f16))
    third = lax.all_to_all(second, "narrow", 0, 0, tiled=True).astype(f32)
    piece, rest = pl.pallas_call(
        third_kernel,
        out_shape=(shape((lines, part), bf16), shape((small_rows, d_shard), f32)),
        in_specs=[VMEM],
        out_specs=(VMEM, VMEM),
        cost_estimate=cost(0, 1 << 20),
        compiler_params=limit(4),
        name="third",
    )(third)

    rest_par = lax.ppermute(rest, "wide", core_swap())
    strip_b = jnp.zeros((ny, lines, part), bf16)
    for j in range(ny):
        here = piece if j == 0 else lax.ppermute(piece, "wide", plane_shift(j, False))
        strip_b = lax.dynamic_update_index_in_dim(strip_b, here, (b - j) % ny, 0)
    strip_b = strip_b.reshape(d_shard, part)
    strip = jnp.zeros((d_shard, half_v), bf16)
    for j in range(nx):
        here = strip_b if j == 0 else lax.ppermute(strip_b, "wide", plane_shift(j, True))
        strip = lax.dynamic_update_slice(strip, here, (0, ((a - j) % nx) * part))
    other = lax.ppermute(strip, "wide", core_swap())
    pair_total = lax.axis_size("wide") * nz * ((slots + 1) // 2)
    grad_head, grad_gain, loss_sum = pl.pallas_call(
        functools.partial(last_kernel, 1.0 / pair_total),
        out_shape=(
            shape((d_shard, vocab), f32),
            shape((1, d_shard), f32),
            shape((1, 1), f32),
        ),
        in_specs=[SMEM] + [VMEM] * 4,
        out_specs=(VMEM,) * 3,
        cost_estimate=cost(0, 2 << 20),
        compiler_params=limit(6),
        name="last",
    )(core, strip, other, rest, rest_par)
    return (loss_sum.reshape(()), grad_head, grad_gain.reshape(d_shard))


def solution(mesh):
    in_specs = (
        P("wide", "narrow", None, None, None, None),
        P("wide", "narrow", None, None, None),
        P("wide", "narrow", None, None),
        P("wide", "narrow", None),
        P("wide", "narrow", None),
        P("wide", "narrow"),
        P("narrow", None),
        P("narrow"),
        P("narrow", None),
    )
    out_specs = (P(), P("narrow", None), P("narrow"))
    return jax.shard_map(
        on_device, mesh=mesh, in_specs=in_specs, out_specs=out_specs, check_vma=False
    )
```

```python
import functools

import jax
import jax.numpy as jnp
from jax import lax
from jax.experimental import pallas as pl
from jax.experimental.pallas import tpu as pltpu
from jax.sharding import PartitionSpec as P


norm_eps = 1e-06
margin_scale = 2.0
nx = 4
ny = 4
nz = 8
near = (1, 2, 3, 4)
far = (-1, -2, -3, 0)
small_rows = 8
half_top = 16384.0
log2_e = 1.4426950408889634


def wide_index(x, y, c):
    return ((y % ny) * nx + x % nx) * 2 + c % 2


def core_swap():
    return [
        (wide_index(x, y, c), wide_index(x, y, 1 - c))
        for y in range(ny)
        for x in range(nx)
        for c in range(2)
    ]


def plane_shift(step, first):
    pairs = []
    for y in range(ny):
        for x in range(nx):
            for c in range(2):
                if (c == 0) == first:
                    pairs.append((wide_index(x, y, c), wide_index(x + step, y, c)))
                else:
                    pairs.append((wide_index(x, y, c), wide_index(x, y + step, c)))
    return pairs


def fetch_pairs(distance):
    pairs = []
    for y in range(ny):
        for x in range(nx):
            for c in range(2):
                w = wide_index(x, y, c)
                d = distance[(x + y + 2 * c) % nx]
                pairs.extend((w * nz + (z + d) % nz, w * nz + z) for z in range(nz))
    return pairs


def fetch(piece):
    both = ("wide", "narrow")
    got = []
    for distance in (near, far):
        got.append(lax.ppermute(piece, both, fetch_pairs(distance)))
    return got


def spread(pieces):
    stack = jnp.stack(pieces)
    got = [stack]
    for j in range(1, nx):
        got.append(lax.ppermute(stack, "wide", plane_shift(j, True)))
    return got


def swap_all(stacks):
    got = []
    for stack in stacks:
        got.append(lax.ppermute(stack, "wide", core_swap()))
    return got


def load_pieces(places, stacks, targets, sems, skip=0):
    copies = []
    for i, stack in enumerate(stacks):
        target = targets[i // nx]
        rows = target.shape[0] // nz
        for s in range(2):
            k = 2 * i + s
            at = pl.multiple_of(places[k + 2 * skip] * rows, rows)
            copies.append(
                pltpu.make_async_copy(
                    stack.at[s, pl.ds(0, rows), :], target.at[pl.ds(at, rows), :], sems.at[k]
                )
            )
    for copy in copies:
        copy.start()
    return copies


def project_kernel(block, skip, places, rows, *refs):
    stacks, (projected, weight, sems) = refs[:nx], refs[nx:]
    copies = load_pieces(places, stacks, (weight,), sems, skip)
    for copy in copies:
        copy.wait()

    def step(i, carry):
        here = pl.ds(pl.multiple_of(i * block, block), block)
        projected[here, :] = jnp.dot(
            rows[here, :], weight[...], preferred_element_type=jnp.float32
        ).astype(jnp.bfloat16)
        return carry

    lax.fori_loop(0, rows.shape[0] // block, step, 0)


def near_kernel(frames, places, core, half_own, half_oth, *refs):
    stacks, (logits, normed, turned, kept, h_own), (gains, sems, g_sems) = (
        refs[:nx],
        refs[nx : nx + 5],
        refs[nx + 5 :],
    )
    copies = load_pieces(places, stacks, (h_own,), sems)
    shard = h_own.shape[0] // nz
    g_copies = []
    for i in range(nx):
        for s in range(2):
            k = 2 * i + s
            g_copies.append(
                pltpu.make_async_copy(
                    stacks[i].at[s, pl.ds(shard, small_rows), pl.ds(0, shard)],
                    gains.at[places[k]],
                    g_sems.at[k],
                )
            )
            g_copies[-1].start()
    for copy in g_copies:
        copy.wait()
    block = 2 * frames
    half = half_own.shape[1]
    at_own = pl.multiple_of(core[0] * half, half)
    at_oth = pl.multiple_of((1 - core[0]) * half, half)
    lines = shard // ny
    gain = jnp.concatenate([gains[z, 0:1, :].astype(jnp.float32) for z in range(nz)], axis=1)

    def pair(p, carry):
        at = pl.multiple_of(p * block, block)
        kept[pl.ds(at, block), pl.ds(at_own, half)] = half_own[pl.ds(at, block), :]
        kept[pl.ds(at, block), pl.ds(at_oth, half)] = half_oth[pl.ds(at, block), :]
        flat = kept[pl.ds(at, block), :].astype(jnp.float32)
        inverse = lax.rsqrt(jnp.mean(flat * flat, axis=1, keepdims=True) + norm_eps)
        value = flat * inverse * gain
        normed[pl.ds(at, block), :] = value.astype(jnp.bfloat16)
        back = value.T.astype(jnp.bfloat16)
        for z in range(nz):
            for b in range(ny):
                turned[pl.ds((b * nz + z) * lines, lines), pl.ds(at, block)] = back[
                    (z * ny + b) * lines : (z * ny + b + 1) * lines, :
                ]
        return carry

    lax.fori_loop(0, half_own.shape[0] // block, pair, 0)
    for copy in copies:
        copy.wait()

    def dot(p, carry):
        here = pl.ds(pl.multiple_of(p * block, block), block)
        logits[here, :] = jnp.dot(
            normed[here, :], h_own[...], preferred_element_type=jnp.float32
        )
        return carry

    lax.fori_loop(0, half_own.shape[0] // block, dot, 0)


def far_kernel(frames, places, core, lengths, labels, ratios, live, logits, normed, codes, *refs):
    stacks, (dl_own, dl_oth, h_oth, loss), (e_own, e_oth, near_top, near_pick, sems) = (
        refs[:nx],
        refs[nx : nx + 4],
        refs[nx + 4 :],
    )
    copies = load_pieces(places, stacks, (h_oth,), sems, nx)
    loss[...] = jnp.zeros_like(loss)
    half = h_oth.shape[1]
    block = 2 * frames

    def near(p, carry):
        here = pl.ds(pl.multiple_of(p * block, block), block)
        l_own = logits[here, :]
        near_top[here, :] = jnp.max(l_own, axis=1, keepdims=True)
        hit_own = (
            lax.broadcasted_iota(jnp.int32, l_own.shape, 1) == codes[here, :] - core[0] * half
        )
        near_pick[here, :] = jnp.sum(jnp.where(hit_own, l_own, 0.0), axis=1, keepdims=True)
        return carry

    lax.fori_loop(0, normed.shape[0] // block, near, 0)
    for copy in copies:
        copy.wait()

    def pair(p, carry):
        at = pl.multiple_of(p * block, block)
        code = codes[pl.ds(at, block), :]
        l_own = logits[pl.ds(at, block), :]
        l_oth = jnp.dot(
            normed[pl.ds(at, block), :], h_oth[...], preferred_element_type=jnp.float32
        )
        highest = jnp.maximum(near_top[pl.ds(at, block), :], jnp.max(l_oth, axis=1, keepdims=True))
        columns = lax.broadcasted_iota(jnp.int32, l_own.shape, 1)
        hit_own = columns == code - core[0] * half
        hit_oth = columns == code - (1 - core[0]) * half
        picked = near_pick[pl.ds(at, block), :] + jnp.sum(
            jnp.where(hit_oth, l_oth, 0.0), axis=1, keepdims=True
        )
        x_own = jnp.exp(l_own - highest)
        x_oth = jnp.exp(l_oth - highest)
        e_own[...] = x_own
        e_oth[...] = x_oth
        total = jnp.sum(x_own, axis=1, keepdims=True) + jnp.sum(x_oth, axis=1, keepdims=True)
        logp = picked - (highest + jnp.log(total))
        frame = lax.broadcasted_iota(jnp.int32, (block, 1), 0)
        second = frame >= frames
        one = (frame < lengths[2 * p]) & jnp.logical_not(second)
        two = second & (frame - frames < lengths[2 * p + 1])
        length_one = jnp.full((1, 1), lengths[2 * p], jnp.int32).astype(jnp.float32)
        length_two = jnp.full((1, 1), lengths[2 * p + 1], jnp.int32).astype(jnp.float32)
        alive = jnp.full((1, 1), (p < live[0]).astype(jnp.int32), jnp.int32).astype(jnp.float32)
        score_one = jnp.sum(jnp.where(one, logp, 0.0), axis=0, keepdims=True) / length_one
        score_two = jnp.sum(jnp.where(two, logp, 0.0), axis=0, keepdims=True) / length_two
        sign = jnp.full((1, 1), 1 - 2 * labels[p], jnp.int32).astype(jnp.float32)
        margin = margin_scale * (sign * (score_one - score_two) - ratios[p])
        turn = jnp.exp(-jnp.abs(margin))
        loss[...] += alive * (jnp.maximum(-margin, 0.0) + jnp.log1p(turn))
        slope = -alive * jnp.where(margin >= 0.0, turn, 1.0) / (1.0 + turn)
        weight_one = margin_scale * sign * slope / length_one
        weight_two = -(margin_scale * sign * slope) / length_two
        coeff = jnp.where(one, weight_one, jnp.where(two, weight_two, 0.0))
        scale = 1.0 / total
        dl_own[pl.ds(at, block), :] = (
            coeff * (hit_own.astype(jnp.float32) - e_own[...] * scale)
        ).astype(jnp.bfloat16)
        dl_oth[pl.ds(at, block), :] = (
            coeff * (hit_oth.astype(jnp.float32) - e_oth[...] * scale)
        ).astype(jnp.bfloat16)
        return carry

    lax.fori_loop(0, normed.shape[0] // block, pair, 0)


def gain_kernel(
    block, dl_own, dl_oth, h_own, h_oth, projected, loss, u_one, u_two, u_three, small, total
):
    total[...] = jnp.zeros_like(total)
    contract = (((1,), (1,)), ((), ()))

    def step(i, carry):
        at = pl.multiple_of(i * block, block)
        dnormed = lax.dot_general(
            dl_own[pl.ds(at, block), :], h_own[...], contract, preferred_element_type=jnp.float32
        ) + lax.dot_general(
            dl_oth[pl.ds(at, block), :], h_oth[...], contract, preferred_element_type=jnp.float32
        )
        flat = projected[pl.ds(at, block), :].astype(jnp.float32)
        inverse = lax.rsqrt(jnp.mean(flat * flat, axis=1, keepdims=True) + norm_eps)
        total[...] += jnp.sum(dnormed * flat * inverse, axis=0, keepdims=True)
        return carry

    lax.fori_loop(0, dl_own.shape[0] // block, step, 0)
    part = small.shape[1]
    count = total.shape[1] // part
    for k in range(count):
        small[pl.ds(k, 1), :] = total[:, k * part : (k + 1) * part]
    small[pl.ds(count, 1), :] = jnp.broadcast_to(loss[...], (1, part))
    for j, unit in ((1, u_one), (2, u_two), (3, u_three)):
        small[pl.ds(small_rows - nx + j, 1), :] = unit[...]


def own_kernel(core, turned, dl_own, out):
    part = out.shape[1]
    at = pl.multiple_of(lax.rem(core[1] + pl.program_id(0), nx) * part, part)
    out[...] = jnp.dot(
        turned[...], dl_own[:, pl.ds(at, part)], preferred_element_type=jnp.float32
    )


def head_kernel(shift, core, term, turned, dl_par, out, *refs):
    part = out.shape[1]
    at = pl.multiple_of(lax.rem(core[1] + shift, nx) * part, part)
    value = term[...] + jnp.dot(
        turned[...], dl_par[:, pl.ds(at, part)], preferred_element_type=jnp.float32
    )
    out[...] = value
    if not refs:
        return
    largest = jnp.max(jnp.max(jnp.abs(value), axis=0, keepdims=True), axis=1, keepdims=True)
    largest = jnp.maximum(largest, 1e-30)
    refs[0][...] = jnp.broadcast_to(largest / half_top, refs[0].shape)
    out[...] = out[...] * (half_top / largest)


def exponent(largest):
    return jnp.ceil(jnp.log(jnp.maximum(largest, 1e-30)) * log2_e) - 14.0


def power(k):
    return jnp.exp(k * (1.0 / log2_e))


def top(value):
    return jnp.max(jnp.max(jnp.abs(value), axis=0, keepdims=True), axis=1, keepdims=True)


def split(value, width):
    head = value.astype(jnp.bfloat16).astype(jnp.float32)
    rest = (value - head) * 256.0
    wide = (1, width)
    return jnp.concatenate([jnp.broadcast_to(head, wide), jnp.broadcast_to(rest, wide)], axis=1)


def write_coded(out, blocks, scale, k, gains, loss):
    zs, lines, part = out.shape
    lines -= small_rows
    half = part // 2
    k_gain = exponent(functools.reduce(jnp.maximum, [top(g) for g in gains]))
    k_loss = exponent(loss)
    loss_row = split(loss * power(-k_loss), half)
    k_row = jnp.broadcast_to(k, (1, part))
    kk_row = jnp.concatenate(
        [jnp.broadcast_to(k_gain, (1, half)), jnp.broadcast_to(k_loss, (1, half))], axis=1
    )
    unit = power(-k_gain)
    for z in range(zs):
        out[z, pl.ds(0, lines), :] = blocks(z) * scale
        out[z, pl.ds(lines, 1), :] = split(gains[z] * unit, half)
        out[z, pl.ds(lines + 1, 1), :] = loss_row
        out[z, pl.ds(lines + 2, 1), :] = k_row
        out[z, pl.ds(lines + 3, 1), :] = kk_row
        out[z, pl.ds(lines + 4, small_rows - 4), :] = jnp.zeros((small_rows - 4, part), jnp.float32)


def read_coded(ref, z):
    lines = ref.shape[1] - small_rows
    half = ref.shape[2] // 2
    gain = ref[z, pl.ds(lines, 1), :]
    loss = ref[z, pl.ds(lines + 1, 1), :]
    k = ref[z, pl.ds(lines + 2, 1), :][:, :1]
    kk = ref[z, pl.ds(lines + 3, 1), :]
    return (
        power(k),
        (gain[:, :half] + gain[:, half:] * (1.0 / 256.0)) * power(kk[:, :1]),
        (loss[:, :1] + loss[:, half : half + 1] * (1.0 / 256.0)) * power(kk[:, half : half + 1]),
    )


def sum_kernel(core, *refs):
    (term, one, two, three), (s_term, s_one, s_two, s_three) = refs[:4], refs[4:8]
    outs, total = refs[8:-1], refs[-1]
    zs, lines, part = outs[0].shape
    lines -= small_rows
    rows = zs * lines
    half = part // 2
    small = (s_term[...] + s_two[...]) + (s_one[...] + s_three[...])
    first = small_rows - nx
    u_one, u_two, u_three = (
        ref[first + j : first + j + 1, :] for j, ref in ((1, s_one), (2, s_two), (3, s_three))
    )
    value = (term[...] + two[...] * u_two) + (one[...] * u_one + three[...] * u_three)
    total[...] = value
    k = exponent(top(value))
    scale = power(-k)
    gains = [small[z // 2 : z // 2 + 1, z % 2 * half : (z % 2 + 1) * half] for z in range(zs)]
    loss = small[zs // 2 : zs // 2 + 1, :1]
    for j, out in enumerate(outs):
        start = lax.rem(core[2] + j, ny) * rows
        write_coded(
            out,
            lambda z: total[pl.ds(pl.multiple_of(start + z * lines, lines), lines), :],
            scale,
            k,
            gains,
            loss,
        )


def second_kernel(term, one, two, three, out, total):
    zs, lines, _ = out.shape
    lines -= small_rows
    gains, loss, largest = [], None, None
    for z in range(zs):
        (u0, g0, l0), (u1, g1, l1), (u2, g2, l2), (u3, g3, l3) = (
            read_coded(ref, z) for ref in (term, one, two, three)
        )
        here = pl.ds(0, lines)
        value = (term[z, here, :] * u0 + two[z, here, :] * u2) + (
            one[z, here, :] * u1 + three[z, here, :] * u3
        )
        total[z] = value
        largest = top(value) if z == 0 else jnp.maximum(largest, top(value))
        gains.append((g0 + g2) + (g1 + g3))
        if z == 0:
            loss = (l0 + l2) + (l1 + l3)
    k = exponent(largest)
    write_coded(out, lambda z: total[z], power(-k), k, gains, loss)


def third_kernel(got, piece, small):
    zs, lines, part = got.shape
    lines -= small_rows
    half = part // 2
    value = gain = loss = None
    for z in range(zs):
        u, g, l = read_coded(got, z)
        here = got[z, pl.ds(0, lines), :] * u
        value, gain, loss = (here, g, l) if z == 0 else (value + here, gain + g, loss + l)
    piece[...] = value.astype(jnp.bfloat16)
    small[pl.ds(0, 1), :] = gain
    small[pl.ds(1, 1), :] = jnp.broadcast_to(loss, (1, half))
    small[pl.ds(2, small_rows - 2), :] = jnp.zeros((small_rows - 2, half), jnp.float32)


def last_kernel(scale, core, strip, other, small, small_par, head, gain, loss):
    half = strip.shape[1]
    head[:, pl.ds(pl.multiple_of(core[0] * half, half), half)] = strip[...].astype(jnp.float32)
    head[:, pl.ds(pl.multiple_of((1 - core[0]) * half, half), half)] = other[...].astype(
        jnp.float32
    )
    both = small[...] + small_par[...]
    gain[...] = both[0:1, :]
    loss[...] = both[1:2, 0:1] * scale


SMEM = pl.BlockSpec(memory_space=pltpu.SMEM)
VMEM = pl.BlockSpec(memory_space=pltpu.VMEM)
ANY = pl.BlockSpec(memory_space=pl.ANY)


def shape(dims, dtype):
    return jax.ShapeDtypeStruct(dims, dtype)


def limit(mebibytes):
    return pltpu.CompilerParams(vmem_limit_bytes=mebibytes << 20)


def cost(flops, moved):
    return pl.CostEstimate(flops=flops, bytes_accessed=moved, transcendentals=0)


def on_device(
    thinker_rows,
    codec_ids,
    block_lengths,
    chosen_label,
    ref_logratio,
    pair_count,
    proj_weight,
    norm_gain,
    head_weight,
):
    slots = thinker_rows.shape[2]
    frames = thinker_rows.shape[4]
    tw = thinker_rows.shape[5]
    k_shard, width = proj_weight.shape
    d_shard, vocab = head_weight.shape
    half_v = vocab // 2
    half_d = width // 2
    count = slots * 2 * frames
    block = 2 * frames
    part = half_v // nx
    lines = d_shard // ny
    bf16, f32 = jnp.bfloat16, jnp.float32
    w = lax.axis_index("wide")
    z = lax.axis_index("narrow")
    c = w % 2
    x = (w // 2) % nx
    y = w // (2 * nx)
    a = jnp.where(c == 0, x, y)
    b = jnp.where(c == 0, y, x)
    core = jnp.stack([c, a, b]).astype(jnp.int32)
    back = x + y - jnp.arange(nx)
    origin = jnp.concatenate([(back + 2 * c) % nx, (back + 2 - 2 * c) % nx])
    table = jnp.array([near, far], jnp.int32).T
    places = ((z + jnp.take(table, origin, axis=0)) % nz).reshape(-1).astype(jnp.int32)

    p_piece = lax.dynamic_slice(proj_weight, (0, c * half_d), (k_shard, half_d))
    h_piece = jnp.concatenate(
        [
            lax.dynamic_slice(head_weight, (0, c * half_v), (d_shard, half_v)),
            jnp.pad(norm_gain.reshape(1, d_shard), ((0, small_rows - 1), (0, half_v - d_shard))),
        ],
        axis=0,
    )
    p_stacks = spread(fetch(p_piece))
    p_stacks = p_stacks + swap_all(p_stacks)
    h_stacks = spread(fetch(h_piece))

    rows = thinker_rows.reshape(count, tw)

    def project(skip, stacks):
        return pl.pallas_call(
            functools.partial(project_kernel, block, skip),
            out_shape=shape((count, half_d), bf16),
            in_specs=[SMEM, VMEM] + [ANY] * nx,
            out_specs=VMEM,
            scratch_shapes=[pltpu.VMEM((tw, half_d), bf16), pltpu.SemaphoreType.DMA((2 * nx,))],
            cost_estimate=cost(2 * count * tw * half_d, 6 << 20),
            compiler_params=limit(8),
            name="project",
        )(places, rows, *stacks)

    half_own = project(0, p_stacks[:nx])
    half_oth = project(nx, p_stacks[nx:])
    h_stacks = h_stacks + swap_all(h_stacks)

    near_half = pl.pallas_call(
        functools.partial(near_kernel, frames),
        out_shape=(
            shape((count, half_v), f32),
            shape((count, width), bf16),
            shape((width, count), bf16),
            shape((count, width), bf16),
            shape((width, half_v), bf16),
        ),
        in_specs=[SMEM, SMEM, VMEM, VMEM] + [ANY] * nx,
        out_specs=(VMEM,) * 5,
        scratch_shapes=[
            pltpu.VMEM((nz, small_rows, d_shard), bf16),
            pltpu.SemaphoreType.DMA((2 * nx,)),
            pltpu.SemaphoreType.DMA((2 * nx,)),
        ],
        cost_estimate=cost(2 * count * width * half_v, 6 << 20),
        compiler_params=limit(12),
        name="near",
    )
    logits, normed, turned, kept, h_own = near_half(places, core, half_own, half_oth, *h_stacks[:nx])
    turned_par = lax.ppermute(turned, "wide", core_swap())
    far_half = pl.pallas_call(
        functools.partial(far_kernel, frames),
        out_shape=(
            shape((count, half_v), bf16),
            shape((count, half_v), bf16),
            shape((width, half_v), bf16),
            shape((1, 1), f32),
        ),
        in_specs=[SMEM] * 6 + [VMEM] * 3 + [ANY] * nx,
        out_specs=(VMEM,) * 4,
        scratch_shapes=[
            pltpu.VMEM((block, half_v), f32),
            pltpu.VMEM((block, half_v), f32),
            pltpu.VMEM((count, 1), f32),
            pltpu.VMEM((count, 1), f32),
            pltpu.SemaphoreType.DMA((2 * nx,)),
        ],
        cost_estimate=cost(2 * count * width * half_v, 8 << 20),
        compiler_params=limit(14),
        name="far",
    )
    dl_own, dl_oth, h_oth, loss = far_half(
        places,
        core,
        block_lengths.reshape(-1),
        chosen_label.reshape(-1),
        ref_logratio.reshape(-1),
        pair_count.reshape(-1),
        logits,
        normed,
        codec_ids.reshape(count, 1),
        *h_stacks[nx:],
    )
    dl_par = lax.ppermute(dl_oth, "wide", core_swap())
    mine = pl.pallas_call(
        own_kernel,
        out_shape=shape((nx, width, part), f32),
        grid=(nx,),
        in_specs=[SMEM, VMEM, VMEM],
        out_specs=pl.BlockSpec((None, width, part), lambda j: (j, 0, 0)),
        compiler_params=limit(12),
        cost_estimate=cost(2 * count * width * half_v, 8 << 20),
        name="own",
    )(core, turned, dl_own)

    def head_term(j):
        outs = ((width, part),) + ((1, part),) * (j > 0)
        return pl.pallas_call(
            functools.partial(head_kernel, j),
            out_shape=tuple(shape(dims, f32) for dims in outs),
            grid=(1,),
            in_specs=[SMEM, pl.BlockSpec((None, width, part), lambda i: (j, 0, 0)), VMEM, VMEM],
            out_specs=tuple(pl.BlockSpec(dims, lambda i: (0, 0)) for dims in outs),
            cost_estimate=cost(2 * count * width * part, 4 << 20),
            compiler_params=limit(8),
            name="head",
        )(core, mine, turned_par, dl_par)

    terms = {j: head_term(j) for j in (2, 1, 3, 0)}
    sent = {
        j: lax.ppermute(
            lax.optimization_barrier(terms[j][0].astype(jnp.float16)), "wide", plane_shift(j, True)
        ).astype(f32)
        for j in (2, 1, 3)
    }
    small = pl.pallas_call(
        functools.partial(gain_kernel, block),
        out_shape=shape((small_rows, part), f32),
        in_specs=[VMEM] * 9,
        out_specs=VMEM,
        scratch_shapes=[pltpu.VMEM((1, width), f32)],
        cost_estimate=cost(2 * count * width * vocab, 8 << 20),
        compiler_params=limit(14),
        name="gain",
    )(dl_own, dl_oth, h_own, h_oth, kept, loss, *(terms[j][1] for j in (1, 2, 3)))
    s_sent = {j: lax.ppermute(small, "wide", plane_shift(j, True)) for j in (2, 1, 3)}
    coded = (nz, lines + small_rows, part)
    f16 = jnp.float16
    chunks = pl.pallas_call(
        sum_kernel,
        out_shape=tuple(shape(coded, f32) for _ in range(ny)),
        in_specs=[SMEM] + [VMEM] * 8,
        out_specs=(VMEM,) * ny,
        scratch_shapes=[pltpu.VMEM((width, part), f32)],
        cost_estimate=cost(0, 5 << 20),
        compiler_params=limit(14),
        name="fold",
    )(core, terms[0][0], sent[1], sent[2], sent[3], small, s_sent[1], s_sent[2], s_sent[3])
    rounded = [lax.optimization_barrier(chunk.astype(f16)) for chunk in chunks]
    got = [rounded[0]] + [
        lax.ppermute(rounded[j], "wide", plane_shift(j, False)) for j in range(1, ny)
    ]
    second = pl.pallas_call(
        second_kernel,
        out_shape=shape(coded, f32),
        in_specs=[VMEM] * ny,
        out_specs=VMEM,
        scratch_shapes=[pltpu.VMEM((nz, lines, part), f32)],
        cost_estimate=cost(0, 2 << 20),
        compiler_params=limit(6),
        name="second",
    )(*(g.astype(f32) for g in got))
    second = lax.optimization_barrier(second.astype(f16))
    third = lax.all_to_all(second, "narrow", 0, 0, tiled=True).astype(f32)
    piece, rest = pl.pallas_call(
        third_kernel,
        out_shape=(shape((lines, part), bf16), shape((small_rows, d_shard), f32)),
        in_specs=[VMEM],
        out_specs=(VMEM, VMEM),
        cost_estimate=cost(0, 1 << 20),
        compiler_params=limit(4),
        name="third",
    )(third)

    rest_par = lax.ppermute(rest, "wide", core_swap())
    strip_b = jnp.zeros((ny, lines, part), bf16)
    for j in range(ny):
        here = piece if j == 0 else lax.ppermute(piece, "wide", plane_shift(j, False))
        strip_b = lax.dynamic_update_index_in_dim(strip_b, here, (b - j) % ny, 0)
    strip_b = strip_b.reshape(d_shard, part)
    strip = jnp.zeros((d_shard, half_v), bf16)
    for j in range(nx):
        here = strip_b if j == 0 else lax.ppermute(strip_b, "wide", plane_shift(j, True))
        strip = lax.dynamic_update_slice(strip, here, (0, ((a - j) % nx) * part))
    other = lax.ppermute(strip, "wide", core_swap())
    pair_total = lax.axis_size("wide") * nz * ((slots + 1) // 2)
    grad_head, grad_gain, loss_sum = pl.pallas_call(
        functools.partial(last_kernel, 1.0 / pair_total),
        out_shape=(
            shape((d_shard, vocab), f32),
            shape((1, d_shard), f32),
            shape((1, 1), f32),
        ),
        in_specs=[SMEM] + [VMEM] * 4,
        out_specs=(VMEM,) * 3,
        cost_estimate=cost(0, 2 << 20),
        compiler_params=limit(6),
        name="last",
    )(core, strip, other, rest, rest_par)
    return (loss_sum.reshape(()), grad_head, grad_gain.reshape(d_shard))


def solution(mesh):
    in_specs = (
        P("wide", "narrow", None, None, None, None),
        P("wide", "narrow", None, None, None),
        P("wide", "narrow", None, None),
        P("wide", "narrow", None),
        P("wide", "narrow", None),
        P("wide", "narrow"),
        P("narrow", None),
        P("narrow"),
        P("narrow", None),
    )
    out_specs = (P(), P("narrow", None), P("narrow"))
    return jax.shard_map(
        on_device, mesh=mesh, in_specs=in_specs, out_specs=out_specs, check_vma=False
    )
```
